32 devices in a mesh: exp: 4 (over x, core), fsdp: 8 (over z, y).
Axes of the slice: x: 2, y: 2, z: 4, core: 2. Of those that a mesh axis runs over, the one named last changes fastest.
Arguments:
- patches: bfloat16 [32768, 768], P(('exp', 'fsdp')), may hold values from -6 to 6
- cond_embed: bfloat16 [128, 768], P(('exp', 'fsdp')), may hold values from -4 to 4, as said below
- image_kind: int32 [32], P(('exp', 'fsdp')), may hold values from 0 to 1, as said below
- expert_ids: int32 [32768, 2], P(('exp', 'fsdp')), may hold values from 0 to 7, all different within a row; in each aligned block of 1024 rows (0 to 1023, 1024 to 2047, ...) at most 288 rows name the same one
- out_grad: bfloat16 [32768, 768], P(('exp', 'fsdp')), may hold values from -6 to 6
- modulate_weight: bfloat16 [768, 4608], P('fsdp', 'exp'), may hold values from -0.21875 to 0.21875
- attend_weight: bfloat16 [768, 2304], P('fsdp', 'exp'), may hold values from -0.21875 to 0.21875
- output_weight: bfloat16 [768, 768], P('fsdp', 'exp'), may hold values from -2 to 2
- router_weight: bfloat16 [768, 8], P('fsdp', 'exp'), may hold values from -0.15625 to 0.15625
- shared_in: bfloat16 [768, 3072], P('fsdp', 'exp'), may hold values from -0.21875 to 0.21875
- shared_out: bfloat16 [3072, 768], P('fsdp', 'exp'), may hold values from -0.109375 to 0.109375
- expert_in: bfloat16 [8, 768, 3072], P('exp', None, 'fsdp'), may hold values from -0.21875 to 0.21875
- expert_out: bfloat16 [8, 3072, 768], P('exp', 'fsdp'), may hold values from -0.109375 to 0.109375
Outputs:
- block_out: bfloat16 [32768, 768], P(('exp', 'fsdp'))
- patches_grad: float32 [32768, 768], P(('exp', 'fsdp'))
- cond_grad: float32 [128, 768], P(('exp', 'fsdp'))
- modulate_grad: float32 [768, 4608], P('fsdp', 'exp')
- attend_grad: float32 [768, 2304], P('fsdp', 'exp')
- output_grad: float32 [768, 768], P('fsdp', 'exp')
- router_grad: float32 [768, 8], P('fsdp', 'exp')
- shared_in_grad: float32 [768, 3072], P('fsdp', 'exp')
- shared_out_grad: float32 [3072, 768], P('fsdp', 'exp')
- expert_in_grad: float32 [8, 768, 3072], P('exp', None, 'fsdp')
- expert_out_grad: float32 [8, 3072, 768], P('exp', 'fsdp')
The draws below stay inside these ranges and needn't reach their ends.
Inputs may be any that keep to these rules, and one draw needn't show every extreme that they name: `image_kind`: each group of 1024 patches holds one image (1) or four images of 256 patches (0). `cond_embed`: the rows of the blocks of a group whose image_kind is 1 are equal. `expert_ids`: the two experts of a row differ; among the rows of one device no expert is named more than 288 times, and that bound is reached.
All inputs are finite; a program needn't handle non-finite values.
Results may differ from the reference program's by a relative error of at most 0.02.
Values may be sent and summed in bfloat16 or wider, within the bound.
No kernel may reach another device: no remote copies, remote signals or barrier semaphores. Data moves between devices by JAX's collectives and lax.ppermute only.
A program may use at most 256 MiB of HBM per device.

```python
import math
import jax
import jax.numpy as jnp
import numpy as np
from jax import lax

D = 768
H = 12
HD = 64
FF = 3072
E = 8
TOPK = 2
SHORT = 256
GROUP = 1024
TOK_DEV = 1024
CAP = 288
TOKENS = 32768
GROUPS = 32
N_EXP = 4
N_FSDP = 8


def kind_table(key):
    return jax.random.randint(jax.random.fold_in(key, 17), (GROUPS,), 0, 2, dtype=jnp.int32)


def draw_image_kind(key, part):
    return kind_table(key)


def draw_cond_embed(key, part):
    long_flags = kind_table(key)
    inner_key = jax.random.fold_in(key, 23)
    base = jnp.clip(jax.random.normal(inner_key, (GROUPS, 4, D), jnp.float32), -4.0, 4.0)
    joined = jnp.where(long_flags[:, None, None] == 1, base[:, :1, :], base)
    return joined.reshape(GROUPS * 4, D).astype(jnp.bfloat16)


def block_scale(key, shape, cuts, low, high):
    loudness = 1.0
    for position, parts in cuts:
        draws = jax.random.uniform(jax.random.fold_in(jax.random.fold_in(key, 6), position), (parts,), jnp.float32, low / len(cuts), high / len(cuts))
        loudness = loudness * jnp.repeat(jnp.exp(draws), shape[position] // parts).reshape((-1,) + (1,) * (len(shape) - 1 - position))
    return loudness


def assign_block(stream_key, own, number, rows, number_of, top, bound, skew):
    ranking = jax.random.permutation(stream_key, number_of)
    crowded, common = shares(number_of, rows * top, bound, skew, True), shares(number_of, rows * top, bound, skew, False)
    places = jnp.arange(number_of)

    def named(sizes, turn):
        used = int((sizes > 0).sum())
        fixed = max(1, used // 4)
        shifted = fixed + (places - fixed + turn * (used - fixed)) % max(1, number_of - fixed)
        return jnp.zeros((number_of,), jnp.int32).at[ranking[jnp.where(places < fixed, places, shifted)]].set(jnp.asarray(sizes, jnp.int32))

    sizes = jnp.where(number % 4 == 0, named(crowded, number // 4), named(common, number - number // 4 - 1))
    mixed = jax.random.permutation(jax.random.fold_in(own, 3), number_of)
    giver, receiver = mixed[0:number_of // 2 * 2:2], mixed[1:number_of // 2 * 2:2]
    margin = jnp.minimum(sizes[giver] - 1, bound - sizes[receiver]) // 2
    margin = jnp.where((giver == ranking[0]) | (receiver == ranking[0]) | (sizes[receiver] == 0), 0, jnp.maximum(margin, 0))
    shifted = jax.random.randint(jax.random.fold_in(own, 4), (number_of // 2,), 0, 1 << 20) % (margin + 1)
    sizes = sizes.at[giver].add(-shifted).at[receiver].add(shifted)
    labels = jnp.searchsorted(jnp.cumsum(sizes), jnp.arange(rows * top), side="right").astype(jnp.int32)
    table = labels.reshape(top, rows).T
    table = table[jax.random.permutation(jax.random.fold_in(own, 1), rows)]
    turn = jax.random.randint(jax.random.fold_in(own, 2), (rows, 1), 0, top)
    return jnp.take_along_axis(table, (jnp.arange(top)[None, :] + turn) % top, axis=1)


def shares(number_of, total, most, lean, full):
    weights = [(1 << 20) // math.isqrt(grade ** lean) + 1 for grade in range(1, number_of + 1)]
    largest = most if full else min(most, max(-(-total // number_of), total * weights[0] // sum(weights)))
    least = 1 if total - largest >= number_of - 1 else 0
    counts, spare = [largest] + [least] * (number_of - 1), total - largest - least * (number_of - 1)
    while spare > 0:
        candidates = [i for i in range(1, number_of) if counts[i] < largest] or [i for i in range(1, number_of) if counts[i] < most]
        whole, left = sum([weights[i] for i in candidates]), spare
        for i in candidates:
            extra = min(most - counts[i], max(1, left * weights[i] // whole), spare)
            counts[i] = counts[i] + extra
            spare = spare - extra
    return np.array(counts)


def gaussian(own_key, dims, width, most, cuts=(), kind=jnp.bfloat16):
    values = width * jax.random.normal(own_key, dims, jnp.float32)
    if cuts:
        values = values * block_scale(own_key, dims, cuts, -0.22, 0.18)
    return jnp.clip(values, -most, most).astype(kind)


def setup_inputs(seed: int = 0) -> dict:
    seeds = jax.random.split(jax.random.key(seed), 14)
    patches = gaussian(seeds[0], (TOKENS, D), 1.0, 6.0, ((0, 32),))
    cond_embed = draw_cond_embed(jax.random.fold_in(seeds[13], 71), 0)
    image_kind = draw_image_kind(jax.random.fold_in(seeds[13], 71), 0)
    expert_ids_keys = jax.random.split(jax.random.fold_in(seeds[3], 1), TOKENS // TOK_DEV)
    expert_ids_turns = jax.random.permutation(jax.random.fold_in(seeds[3], 3), TOKENS // TOK_DEV)
    expert_ids = jax.vmap(lambda own, number: assign_block(jax.random.fold_in(seeds[3], 2), own, number, TOK_DEV, E, TOPK, CAP, 1))(expert_ids_keys, expert_ids_turns).reshape((TOKENS, TOPK))
    out_grad = gaussian(seeds[4], (TOKENS, D), 1.0, 6.0, ((0, 32),))
    modulate_weight = gaussian(seeds[5], (D, 6 * D), D ** -0.5, 0.21875, ((0, 8), (1, 4)))
    attend_weight = gaussian(seeds[6], (D, 3 * D), D ** -0.5, 0.21875, ((0, 8), (1, 4)))
    output_weight = gaussian(seeds[7], (D, D), (max(D // 96, 1)) ** -0.5, 2.0, ((0, 8), (1, 4)))
    router_weight = gaussian(seeds[8], (D, E), (2 * D) ** -0.5, 0.15625, ((0, 8), (1, 4)))
    shared_in = gaussian(seeds[9], (D, FF), D ** -0.5, 0.21875, ((0, 8), (1, 4)))
    shared_out = gaussian(seeds[10], (FF, D), FF ** -0.5, 0.109375, ((0, 8), (1, 4)))
    expert_in = gaussian(seeds[11], (E, D, FF), D ** -0.5, 0.21875, ((0, 4), (2, 8)))
    expert_out = gaussian(seeds[12], (E, FF, D), FF ** -0.5, 0.109375, ((0, 4), (1, 8)))
    return {"patches": patches, "cond_embed": cond_embed, "image_kind": image_kind, "expert_ids": expert_ids, "out_grad": out_grad, "modulate_weight": modulate_weight, "attend_weight": attend_weight, "output_weight": output_weight, "router_weight": router_weight, "shared_in": shared_in, "shared_out": shared_out, "expert_in": expert_in, "expert_out": expert_out}


@jax.custom_vjp
def low(v):
    return lax.optimization_barrier(v.astype(jnp.bfloat16)).astype(jnp.float32)

@jax.custom_vjp
def low_back(v):
    return v

def low_keep(v):
    return (low(v), None)

def low_pass(kept, grad):
    return (grad,)

def back_keep(v):
    return (v, None)

def back_low(kept, grad):
    return (low(grad),)
low.defvjp(low_keep, low_pass)
low_back.defvjp(back_keep, back_low)
eps_norm = 1e-06

def product(left, right):
    return jnp.dot(left, right, precision=lax.Precision.HIGHEST, preferred_element_type=jnp.float32)

def layer_norm(values):
    centered = values - lax.optimization_barrier(jnp.mean(values, axis=-1, keepdims=True))
    return centered * lax.rsqrt(lax.optimization_barrier(jnp.mean(centered * centered, axis=-1, keepdims=True)) + eps_norm)

def gelu_tanh(values):
    return jax.nn.gelu(values, approximate=True)

def slot_table(expert_ids):
    flat = expert_ids.reshape(-1)
    onehot = (flat[:, None] == jnp.arange(E, dtype=jnp.int32)[None, :]).astype(jnp.int32)
    before = jnp.cumsum(onehot, axis=0) - onehot
    return lax.optimization_barrier(jnp.sum(before * onehot, axis=1)).astype(jnp.int32).reshape(expert_ids.shape)

def attend(inputs):
    triple_group, long_flag = inputs
    query = triple_group[:, 0]
    keys = triple_group[:, 1]
    values = triple_group[:, 2]
    scores = low_back(jnp.einsum('qhd,khd->hqk', query, keys, precision=lax.Precision.HIGHEST) * HD ** (-0.5))
    block = jnp.arange(GROUP, dtype=jnp.int32) // SHORT
    allowed = (block[:, None] == block[None, :]) | (long_flag == 1)
    attention = jax.nn.softmax(jnp.where(allowed[None], scores, -1e+30), axis=-1)
    mixed = jnp.einsum('hqk,khd->qhd', low(attention), values, precision=lax.Precision.HIGHEST)
    return low(low_back(mixed)).reshape(GROUP, D)

def run_span(weights, span):
    modulate_full, attend_full, output_full, router_full, upward_full, downward_full, expert_up, expert_down = weights
    patches, cond_embed, image_kind, expert_ids = span
    blocks = TOK_DEV // SHORT
    cond_act = low(jax.nn.silu(cond_embed))
    modulation = low_back(product(cond_act, modulate_full)).reshape(blocks, 1, 6, D)
    inputs = patches.reshape(blocks, SHORT, D)
    normed_first = layer_norm(inputs)
    attend_in = low(normed_first * (1.0 + modulation[:, :, 1]) + modulation[:, :, 0]).reshape(TOK_DEV, D)
    triple = low(low_back(product(attend_in, attend_full))).reshape(TOK_DEV // GROUP, GROUP, 3, H, HD)
    attended = lax.map(jax.checkpoint(attend), (triple, image_kind)).reshape(TOK_DEV, D)
    projected = low_back(product(attended, output_full)).reshape(blocks, SHORT, D)
    residual = inputs + modulation[:, :, 2] * projected
    normed_second = layer_norm(residual)
    branch_in = low(normed_second * (1.0 + modulation[:, :, 4]) + modulation[:, :, 3]).reshape(TOK_DEV, D)
    logits = low_back(product(branch_in, router_full))
    gates = jax.nn.softmax(jnp.take_along_axis(logits, expert_ids, axis=1), axis=-1)
    shared_act = low(gelu_tanh(low_back(product(branch_in, upward_full))))
    shared_res = product(shared_act, downward_full)
    slots = slot_table(expert_ids)
    buffer = jnp.zeros((E, CAP, D), jnp.float32).at[expert_ids, slots].set(jnp.broadcast_to(branch_in[:, None, :], (TOK_DEV, TOPK, D)))
    buffer = low_back(buffer)
    expert_pre = low_back(jnp.einsum('erd,edf->erf', buffer, expert_up, precision=lax.Precision.HIGHEST))
    expert_act = low(gelu_tanh(expert_pre))
    expert_res = low(low_back(jnp.einsum('erf,efd->erd', expert_act, expert_down, precision=lax.Precision.HIGHEST)))
    picked = expert_res[expert_ids, slots]
    mixture = lax.optimization_barrier(jnp.sum(gates[:, :, None] * picked, axis=1))
    branch_out = low_back(shared_res + mixture).reshape(blocks, SHORT, D)
    return (residual + modulation[:, :, 5] * branch_out).reshape(TOK_DEV, D)

def reference(patches, cond_embed, image_kind, expert_ids, out_grad, modulate_weight, attend_weight, output_weight, router_weight, shared_in, shared_out, expert_in, expert_out):
    count = N_EXP * N_FSDP
    kinds_split = image_kind.reshape(count, TOK_DEV // GROUP)
    ids_split = expert_ids.reshape(count, TOK_DEV, TOPK)

    def forward(inputs, embeds, *weights):

        def step(carry, span):
            return (carry, run_span(weights, span))
        spans = (inputs.reshape(count, TOK_DEV, D), embeds.reshape(count, TOK_DEV // SHORT, D), kinds_split, ids_split)
        carry, outputs = lax.scan(jax.checkpoint(step), jnp.zeros((), jnp.float32), spans)
        return outputs.reshape(count * TOK_DEV, D)
    floats = (patches, cond_embed, modulate_weight, attend_weight, output_weight, router_weight, shared_in, shared_out, expert_in, expert_out)
    floats = tuple((item.astype(jnp.float32) for item in floats))
    result, pull = jax.vjp(forward, *floats)
    grads = pull(out_grad.astype(jnp.float32))
    return (result.astype(jnp.bfloat16), grads[0], grads[1], grads[2], grads[3], grads[4], grads[5], grads[6], grads[7], grads[8], grads[9])
```

```python
import jax
import jax.numpy as jnp
from jax import lax
from jax.experimental import pallas as pl
from jax.experimental.pallas import tpu as pltpu
from jax.sharding import Mesh
from jax.sharding import PartitionSpec as P

H = 12
HD = 64
E = 8
TOPK = 2
SHORT = 256
GROUP = 1024
CAP = 288
RING_MOST = 8

F32 = jnp.float32
BF16 = jnp.bfloat16

eps_norm = 1e-06
tanh_gain = 0.7978845608028654
ALL = ("exp", "zi", "yi")


def layer_norm(values):
    centered = values - jnp.mean(values, axis=-1, keepdims=True)
    inverse = lax.rsqrt(jnp.mean(centered * centered, axis=-1, keepdims=True) + eps_norm)
    return (centered * inverse, inverse)


def norm_back(grad, normed, inverse):
    return inverse * (
        grad
        - jnp.mean(grad, axis=-1, keepdims=True)
        - normed * jnp.mean(grad * normed, axis=-1, keepdims=True)
    )


def gelu_tanh(values):
    return jax.nn.gelu(values, approximate=True)


def gelu_slope(values):
    hyper = jnp.tanh(tanh_gain * (values + 0.044715 * values * values * values))
    return 0.5 * (1.0 + hyper) + 0.5 * values * (1.0 - hyper * hyper) * tanh_gain * (
        1.0 + 3.0 * 0.044715 * values * values
    )


def silu_slope(values):
    sigma = jax.nn.sigmoid(values)
    return sigma * (1.0 + values * (1.0 - sigma))


def dot(left, right, dims):
    return lax.dot_general(left, right, (dims, ((), ())), preferred_element_type=F32)


def mm(left, right):
    return dot(left, right, ((1,), (0,)))


def mm_rt(left, right):
    return dot(left, right, ((1,), (1,)))


def mm_lt(left, right):
    return dot(left, right, ((0,), (0,)))


def slot_table(expert_ids):
    flat = expert_ids.reshape(-1)
    onehot = (flat[:, None] == jnp.arange(E, dtype=jnp.int32)[None, :]).astype(jnp.int32)
    before = jnp.cumsum(onehot, axis=0) - onehot
    return jnp.sum(before * onehot, axis=1).reshape(expert_ids.shape)


LOG2E = 1.4426950408889634
SCORE = HD ** (-0.5)


def attend_kernel(kind_ref, query_ref, key_ref, value_ref, mixed_ref, logsum_ref):
    left = lax.broadcasted_iota(jnp.int32, (GROUP, 2 * HD), 1) < HD
    keys = key_ref[...]
    zero = jnp.zeros_like(keys)
    split_keys = (jnp.where(left, keys, zero), jnp.where(left, zero, keys))

    def rows_of(part, first, count):
        rows = pl.ds(part * SHORT, SHORT)
        query = query_ref[rows, :]
        value = value_ref[pl.ds(first, count), :]
        halves = []
        for half in range(2):
            scores = mm_rt(query, split_keys[half][first : first + count])
            peak = jnp.max(scores, axis=1, keepdims=True)
            weights = jnp.exp2((scores - peak) * (SCORE * LOG2E))
            total = jnp.sum(weights, axis=1, keepdims=True)
            halves.append(mm(weights.astype(BF16), value) / total)
            logsum = peak * (SCORE * LOG2E) + jnp.log2(total)
            logsum_ref[0, 0, half, rows] = jnp.transpose(
                jnp.broadcast_to(logsum, (SHORT, 2 * HD))
            )[0]
        mixed_ref[rows, :] = jnp.where(left[:SHORT], halves[0], halves[1]).astype(BF16)

    is_long = kind_ref[pl.program_id(0)] == 1

    @pl.when(is_long)
    def _():
        for part in range(GROUP // SHORT):
            rows_of(part, 0, GROUP)

    @pl.when(jnp.logical_not(is_long))
    def _():
        for part in range(GROUP // SHORT):
            rows_of(part, part * SHORT, SHORT)


def attend(triple, image_kind):
    groups = triple.shape[0] // GROUP
    pairs = H // 2

    def part(offset):
        return pl.BlockSpec((GROUP, 2 * HD), lambda g, i, kind: (g, offset + i))

    return pl.pallas_call(
        attend_kernel,
        out_shape=(
            jax.ShapeDtypeStruct((triple.shape[0], H * HD), BF16),
            jax.ShapeDtypeStruct((groups, pairs, 8, GROUP), F32),
        ),
        grid_spec=pltpu.PrefetchScalarGridSpec(
            num_scalar_prefetch=1,
            grid=(groups, pairs),
            in_specs=[part(0), part(pairs), part(2 * pairs)],
            out_specs=(
                part(0),
                pl.BlockSpec((1, 1, 8, GROUP), lambda g, i, kind: (g, i, 0, 0)),
            ),
        ),
        compiler_params=pltpu.CompilerParams(vmem_limit_bytes=32 << 20),
        name="attend",
    )(image_kind, triple, triple, triple)


def attend_back_kernel(
    kind_ref,
    query_ref,
    key_ref,
    value_ref,
    mixed_ref,
    grad_ref,
    logsum_ref,
    grads_ref,
    key_sum,
    value_sum,
):
    left = lax.broadcasted_iota(jnp.int32, (GROUP, 2 * HD), 1) < HD

    def split(values):
        zero = jnp.zeros_like(values)
        return (jnp.where(left, values, zero), jnp.where(left, zero, values))

    split_query = split(query_ref[...])
    split_keys = split(key_ref[...])
    split_values = split(value_ref[...])
    split_grad = split(grad_ref[...])
    outer = jnp.transpose(mixed_ref[...].astype(F32) * grad_ref[...].astype(F32))
    inner = (
        jnp.sum(outer[:HD], axis=0, keepdims=True),
        jnp.sum(outer[HD:], axis=0, keepdims=True),
    )

    def rows_of(part, first, count, fresh):
        low, high = part * SHORT, (part + 1) * SHORT
        keys_at = pl.ds(first, count)
        query = query_ref[pl.ds(low, SHORT), :]
        grad = grad_ref[pl.ds(low, SHORT), :]
        key_part = value_part = query_part = None
        for half in range(2):
            keys = split_keys[half][first : first + count]
            scores = mm_rt(keys, query)
            logsum = logsum_ref[0, 0, half : half + 1, low:high]
            attention = jnp.exp2(scores * (SCORE * LOG2E) - logsum)
            moved = mm_rt(split_values[half][first : first + count], grad)
            grad_scores = (attention * (moved - inner[half][:, low:high])).astype(BF16)
            value_add = mm(attention.astype(BF16), split_grad[half][low:high])
            key_add = mm(grad_scores, split_query[half][low:high])
            query_add = mm_lt(grad_scores, keys)
            if half == 0:
                key_part, value_part, query_part = key_add, value_add, query_add
            else:
                key_part, value_part = key_part + key_add, value_part + value_add
                query_part = query_part + query_add
        grads_ref[0, pl.ds(low, SHORT), :] = (query_part * SCORE).astype(BF16)
        if fresh:
            key_sum[keys_at, :] = key_part
            value_sum[keys_at, :] = value_part
        else:
            key_sum[keys_at, :] += key_part
            value_sum[keys_at, :] += value_part

    is_long = kind_ref[pl.program_id(0)] == 1

    @pl.when(is_long)
    def _():
        for part in range(GROUP // SHORT):
            rows_of(part, 0, GROUP, part == 0)

    @pl.when(jnp.logical_not(is_long))
    def _():
        for part in range(GROUP // SHORT):
            rows_of(part, part * SHORT, SHORT, True)

    grads_ref[1, :, :] = (key_sum[...] * SCORE).astype(BF16)
    grads_ref[2, :, :] = value_sum[...].astype(BF16)


def attend_back(triple, attended, logsum, grad_attended, image_kind):
    groups = triple.shape[0] // GROUP
    pairs = H // 2

    def part(offset):
        return pl.BlockSpec((GROUP, 2 * HD), lambda g, i, kind: (g, offset + i))

    return pl.pallas_call(
        attend_back_kernel,
        out_shape=jax.ShapeDtypeStruct((3, triple.shape[0], H * HD), BF16),
        grid_spec=pltpu.PrefetchScalarGridSpec(
            num_scalar_prefetch=1,
            grid=(groups, pairs),
            in_specs=[
                part(0),
                part(pairs),
                part(2 * pairs),
                part(0),
                part(0),
                pl.BlockSpec((1, 1, 8, GROUP), lambda g, i, kind: (g, i, 0, 0)),
            ],
            out_specs=pl.BlockSpec((3, GROUP, 2 * HD), lambda g, i, kind: (0, g, i)),
            scratch_shapes=[pltpu.VMEM((GROUP, 2 * HD), F32)] * 2,
        ),
        compiler_params=pltpu.CompilerParams(vmem_limit_bytes=32 << 20),
        name="attend_back",
    )(image_kind, triple, triple, triple, attended, grad_attended, logsum)


class Ring:
    def __init__(self, mesh):
        self.n_exp = mesh.shape["exp"]
        self.n_ring = mesh.shape["zi"]
        self.n_pair = mesh.shape["yi"]
        self.bits = []
        bit = self.n_exp // 2
        while bit:
            self.bits.append(bit)
            bit //= 2
        self.direct = self.n_ring <= RING_MOST

    def step(self, value):
        n = self.n_ring
        return lax.ppermute(value, "zi", [(i, (i + 1) % n) for i in range(n)])

    def swap(self, value):
        return lax.ppermute(value, "yi", [(0, 1), (1, 0)])

    def cross(self, value, bit):
        return lax.ppermute(value, "exp", [(i, i ^ bit) for i in range(self.n_exp)])

    def place(self):
        return (lax.axis_index("exp"), lax.axis_index("zi"), lax.axis_index("yi"))

    def gather(self, block):
        e, z, y = self.place()
        rows, cols = block.shape
        if not self.direct:
            whole = lax.all_gather(block, ("zi", "yi"), axis=0, tiled=False)
            return lax.all_gather(whole, "exp", axis=0, tiled=False)
        n = self.n_ring
        held, pieces = block, [block]
        for _ in range(n - 1):
            held = self.step(held)
            pieces.append(held)
        stacked = jnp.stack(pieces, axis=0)
        order = (z - jnp.arange(n, dtype=jnp.int32)) % n
        held = jnp.take(stacked, order, axis=0)
        if self.n_pair == 2:
            other = self.swap(held)
            held = jnp.stack(
                (jnp.where(y == 0, held, other), jnp.where(y == 0, other, held)), axis=1
            )
        held = held.reshape(1, n * self.n_pair, rows, cols)
        for bit in self.bits:
            other = self.cross(held, bit)
            low = (e & bit) == 0
            held = jnp.stack((jnp.where(low, held, other), jnp.where(low, other, held)), axis=1)
            held = held.reshape(held.shape[0] * 2, n * self.n_pair, rows, cols)
        return held

    def scatter(self, blocks):
        e, z, y = self.place()
        rows, cols = blocks.shape[2:]
        if not self.direct:
            part = lax.psum_scatter(blocks, "exp", scatter_dimension=0, tiled=True)
            part = part.reshape(-1, rows, cols)
            part = lax.psum_scatter(part, ("zi", "yi"), scatter_dimension=0, tiled=True)
            return part.reshape(rows, cols).astype(F32)
        held = blocks
        for bit in reversed(self.bits):
            half = held.reshape(held.shape[0] // 2, 2, *held.shape[1:])
            mine = ((e & bit) != 0).astype(jnp.int32)
            keep = lax.dynamic_index_in_dim(half, mine, 1, keepdims=False)
            give = lax.dynamic_index_in_dim(half, 1 - mine, 1, keepdims=False)
            held = (keep.astype(F32) + self.cross(give, bit).astype(F32)).astype(BF16)
        held = held.reshape(self.n_ring, self.n_pair, rows, cols)
        if self.n_pair == 2:
            keep = lax.dynamic_index_in_dim(held, y, 1, keepdims=False)
            give = lax.dynamic_index_in_dim(held, 1 - y, 1, keepdims=False)
            held = (keep.astype(F32) + self.swap(give).astype(F32)).astype(BF16)
        else:
            held = held[:, 0]
        n = self.n_ring
        own = [
            lax.dynamic_index_in_dim(held, (z - 1 - k) % n, 0, keepdims=False) for k in range(n)
        ]
        moving = own[0].astype(F32)
        for k in range(1, n):
            moving = own[k].astype(F32) + self.step(moving.astype(BF16)).astype(F32)
        return moving


def local(
    ring,
    patches,
    cond_embed,
    image_kind,
    expert_ids,
    out_grad,
    modulate_weight,
    attend_weight,
    output_weight,
    router_weight,
    shared_in,
    shared_out,
    expert_in,
    expert_out,
):
    tok_count, width = patches.shape
    blocks = tok_count // SHORT
    n_exp, n_ring, n_pair = ring.n_exp, ring.n_ring, ring.n_pair
    n_fsdp = n_ring * n_pair
    n_all = n_exp * n_fsdp
    e, z, y = ring.place()
    kept = expert_in.shape[0] // n_pair
    mod_rows, mod_cols = modulate_weight.shape

    cond_float = cond_embed.astype(F32)
    cond_act = jax.nn.silu(cond_float).astype(BF16)
    cond_send = cond_act.reshape(blocks, n_fsdp, mod_rows).transpose(1, 0, 2)
    cond_send = jnp.broadcast_to(cond_send[None], (n_exp, n_fsdp, blocks, mod_rows))
    cond_all = lax.all_to_all(
        cond_send.reshape(n_all, blocks, mod_rows), ALL, 0, 0, tiled=True
    ).reshape(n_all * blocks, mod_rows)
    mod_part = mm(cond_all, modulate_weight).reshape(n_all, blocks, mod_cols)
    mod_part = lax.all_to_all(mod_part, ALL, 0, 0, tiled=True)
    modulation = jnp.sum(mod_part.reshape(n_exp, n_fsdp, blocks, mod_cols), axis=1)
    modulation = modulation.transpose(1, 0, 2).reshape(blocks, 1, 6, width)

    attend_blocks = ring.gather(attend_weight)
    attend_full = attend_blocks.reshape(n_exp, width, -1).transpose(1, 0, 2).reshape(width, -1)
    output_blocks = ring.gather(output_weight)
    output_full = output_blocks.reshape(n_exp, width, -1).transpose(1, 0, 2).reshape(width, -1)
    router_blocks = lax.all_to_all(
        jnp.broadcast_to(router_weight[None], (n_all,) + router_weight.shape),
        ALL,
        0,
        0,
        tiled=True,
    )
    router_full = (
        router_blocks.reshape(n_exp, width, -1).transpose(1, 0, 2).reshape(width, E)
    )
    upward_blocks = ring.gather(shared_in)
    upward_full = upward_blocks.reshape(n_exp, width, -1).transpose(1, 0, 2).reshape(width, -1)
    downward_blocks = ring.gather(shared_out)
    hidden = shared_out.shape[0] * n_fsdp
    downward_full = (
        downward_blocks.reshape(n_exp, hidden, -1).transpose(1, 0, 2).reshape(hidden, width)
    )

    if n_pair == 2:
        own_in = jnp.where(y == 0, expert_in[0], expert_in[1])
        give_in = jnp.where(y == 0, expert_in[1], expert_in[0])
        own_out = jnp.where(y == 0, expert_out[0], expert_out[1])
        give_out = jnp.where(y == 0, expert_out[1], expert_out[0])
        up_block = jnp.concatenate((own_in, ring.swap(give_in)), axis=1)
        down_block = jnp.concatenate((own_out, ring.swap(give_out)), axis=0)
    else:
        up_block, down_block = expert_in[0], expert_out[0]
    if ring.direct:
        ups, downs = [up_block], [down_block]
        for _ in range(n_ring - 1):
            ups.append(ring.step(ups[-1]))
            downs.append(ring.step(downs[-1]))
        ups, downs = ups[1:] + ups[:1], downs[1:] + downs[:1]
    else:
        ups = [lax.all_gather(up_block, "zi", axis=1, tiled=True)]
        downs = [lax.all_gather(down_block, "zi", axis=0, tiled=True)]

    shift_first = modulation[:, :, 0]
    scale_first = modulation[:, :, 1]
    gate_first = modulation[:, :, 2]
    shift_second = modulation[:, :, 3]
    scale_second = modulation[:, :, 4]
    gate_second = modulation[:, :, 5]
    inputs = patches.astype(F32).reshape(blocks, SHORT, width)
    normed_first, inverse_first = layer_norm(inputs)
    attend_in = (
        (normed_first * (1.0 + scale_first) + shift_first).astype(BF16).reshape(tok_count, width)
    )
    triple = mm(attend_in, attend_full).astype(BF16)
    attended, logsum = attend(triple, image_kind)
    projected = mm(attended, output_full).reshape(blocks, SHORT, width)
    residual = inputs + gate_first * projected
    normed_second, inverse_second = layer_norm(residual)
    branch_in = (
        (normed_second * (1.0 + scale_second) + shift_second)
        .astype(BF16)
        .reshape(tok_count, width)
    )
    logits = mm(branch_in, router_full)
    choose = expert_ids[:, :, None] == jnp.arange(E, dtype=jnp.int32)[None, None, :]
    choose = choose.astype(F32)
    gates = jax.nn.softmax(jnp.sum(choose * logits[:, None, :], axis=-1), axis=-1)

    grad_out = out_grad.astype(F32).reshape(blocks, SHORT, width)
    grad_branch = (gate_second * grad_out).astype(BF16).reshape(tok_count, width)
    grad_branch_wide = grad_branch.astype(F32)

    slots = slot_table(expert_ids)
    target = expert_ids * CAP + slots
    row_of = jnp.arange(E * CAP, dtype=jnp.int32)[:, None]
    pick0 = (row_of == target[None, :, 0]).astype(BF16)
    pick1 = (row_of == target[None, :, 1]).astype(BF16)
    send_rows = mm(pick0 + pick1, branch_in).astype(BF16).reshape(E, CAP, width)
    received = lax.all_to_all(send_rows, ("exp", "yi"), 0, 0, tiled=True)
    received = received.reshape(-1, width)
    grad_picked = (gates[:, :, None] * grad_branch_wide[:, None, :]).astype(BF16)
    grad_send = (
        (mm(pick0, grad_picked[:, 0]) + mm(pick1, grad_picked[:, 1]))
        .astype(BF16)
        .reshape(E, CAP, width)
    )
    grad_received = lax.all_to_all(grad_send, ("exp", "yi"), 0, 0, tiled=True)
    grad_received = grad_received.reshape(-1, width)

    shared_pre = mm(branch_in, upward_full)
    shared_act = gelu_tanh(shared_pre).astype(BF16)
    shared_res = mm(shared_act, downward_full)
    shared_out_grad = mm_lt(shared_act, grad_branch).astype(BF16)
    grad_shared_pre = (mm_rt(grad_branch, downward_full) * gelu_slope(shared_pre)).astype(BF16)
    shared_in_grad = mm_lt(branch_in, grad_shared_pre).astype(BF16)
    grad_branch_in = mm_rt(grad_shared_pre, upward_full)

    expert_res = 0.0
    pres, acts = [], []
    for up, down in zip(ups, downs):
        pre = mm(received, up)
        act = gelu_tanh(pre).astype(BF16)
        expert_res = expert_res + mm(act, down)
        pres.append(pre)
        acts.append(act)
    expert_res = expert_res.astype(BF16).reshape(E, CAP, width)
    returned = lax.all_to_all(expert_res, ("exp", "yi"), 0, 0, tiled=True).reshape(-1, width)
    grad_rows = 0.0
    grad_ups, grad_downs = [], []
    for up, down, pre, act in zip(ups, downs, pres, acts):
        grad_pre = (mm_rt(grad_received, down) * gelu_slope(pre)).astype(BF16)
        grad_rows = grad_rows + mm_rt(grad_pre, up)
        grad_downs.append(mm_lt(act, grad_received))
        grad_ups.append(mm_lt(received, grad_pre))
    grad_rows = grad_rows.astype(BF16).reshape(E, CAP, width)
    grad_returned = lax.all_to_all(grad_rows, ("exp", "yi"), 0, 0, tiled=True)
    grad_returned = grad_returned.reshape(-1, width)

    if ring.direct:
        up_sum, down_sum = grad_ups[0], grad_downs[0]
        for k in range(1, n_ring):
            up_sum = grad_ups[k] + ring.step(up_sum.astype(BF16)).astype(F32)
            down_sum = grad_downs[k] + ring.step(down_sum.astype(BF16)).astype(F32)
    else:
        up_sum = lax.psum_scatter(
            grad_ups[0].astype(BF16), "zi", scatter_dimension=1, tiled=True
        ).astype(F32)
        down_sum = lax.psum_scatter(
            grad_downs[0].astype(BF16), "zi", scatter_dimension=0, tiled=True
        ).astype(F32)
    if n_pair == 2:
        slice_cols = up_sum.shape[1] // 2
        own_up, give_up = up_sum[:, :slice_cols], up_sum[:, slice_cols:]
        own_down, give_down = down_sum[:slice_cols], down_sum[slice_cols:]
        got_up = ring.swap(give_up.astype(BF16)).astype(F32)
        got_down = ring.swap(give_down.astype(BF16)).astype(F32)
        expert_in_grad = jnp.stack(
            (jnp.where(y == 0, own_up, got_up), jnp.where(y == 0, got_up, own_up))
        )
        expert_out_grad = jnp.stack(
            (jnp.where(y == 0, own_down, got_down), jnp.where(y == 0, got_down, own_down))
        )
    else:
        expert_in_grad, expert_out_grad = up_sum[None], down_sum[None]

    picked0 = mm_lt(pick0, returned)
    picked1 = mm_lt(pick1, returned)
    mixture = gates[:, 0:1] * picked0 + gates[:, 1:2] * picked1
    branch_out = (shared_res + mixture).reshape(blocks, SHORT, width)
    block_out = (residual + gate_second * branch_out).reshape(tok_count, width).astype(BF16)
    grad_gate_second = jnp.sum(grad_out * branch_out, axis=1)
    grad_gates = jnp.stack(
        (
            jnp.sum(grad_branch_wide * picked0, axis=-1),
            jnp.sum(grad_branch_wide * picked1, axis=-1),
        ),
        axis=1,
    )
    grad_chosen = gates * (grad_gates - jnp.sum(gates * grad_gates, axis=-1, keepdims=True))
    grad_logits = jnp.sum(choose * grad_chosen[:, :, None], axis=1).astype(BF16)
    router_grad = mm_lt(branch_in, grad_logits)
    grad_branch_in = (
        grad_branch_in + mm_lt(pick0 + pick1, grad_returned) + mm_rt(grad_logits, router_full)
    )
    grad_norm_in = grad_branch_in.reshape(blocks, SHORT, width)
    grad_shift_second = jnp.sum(grad_norm_in, axis=1)
    grad_scale_second = jnp.sum(grad_norm_in * normed_second, axis=1)
    grad_residual = grad_out + norm_back(
        grad_norm_in * (1.0 + scale_second), normed_second, inverse_second
    )
    grad_gate_first = jnp.sum(grad_residual * projected, axis=1)
    grad_projected = (gate_first * grad_residual).astype(BF16).reshape(tok_count, width)
    output_grad = mm_lt(attended, grad_projected).astype(BF16)
    grad_attended = mm_rt(grad_projected, output_full).astype(BF16)
    grad_triple = attend_back(triple, attended, logsum, grad_attended, image_kind)
    grad_triple = grad_triple.transpose(1, 0, 2).reshape(tok_count, 3 * width)
    attend_grad = mm_lt(attend_in, grad_triple).astype(BF16)
    grad_attend_in = mm_rt(grad_triple, attend_full).reshape(blocks, SHORT, width)
    grad_shift_first = jnp.sum(grad_attend_in, axis=1)
    grad_scale_first = jnp.sum(grad_attend_in * normed_first, axis=1)
    patches_grad = grad_residual + norm_back(
        grad_attend_in * (1.0 + scale_first), normed_first, inverse_first
    )
    patches_grad = patches_grad.reshape(tok_count, width)

    grad_modulation = jnp.stack(
        (
            grad_shift_first,
            grad_scale_first,
            grad_gate_first,
            grad_shift_second,
            grad_scale_second,
            grad_gate_second,
        ),
        axis=1,
    )
    grad_modulation = grad_modulation.reshape(blocks, n_exp, mod_cols).astype(BF16)
    mod_send = jnp.broadcast_to(
        grad_modulation.transpose(1, 0, 2)[:, None], (n_exp, n_fsdp, blocks, mod_cols)
    )
    mod_all = lax.all_to_all(
        mod_send.reshape(n_all, blocks, mod_cols), ALL, 0, 0, tiled=True
    ).reshape(n_all * blocks, mod_cols)
    modulate_grad = mm_lt(cond_all, mod_all)
    cond_part = mm_rt(mod_all, modulate_weight).reshape(n_all, blocks, mod_rows)
    cond_part = lax.all_to_all(cond_part, ALL, 0, 0, tiled=True)
    cond_grad = jnp.sum(cond_part.reshape(n_exp, n_fsdp, blocks, mod_rows), axis=0)
    cond_grad = cond_grad.transpose(1, 0, 2).reshape(blocks, width) * silu_slope(cond_float)

    def dense(grad, shard):
        rows, cols = shard.shape
        return ring.scatter(
            grad.reshape(n_fsdp, rows, n_exp, cols).transpose(2, 0, 1, 3).astype(BF16)
        )

    shared_out_grad = dense(shared_out_grad, shared_out)
    shared_in_grad = dense(shared_in_grad, shared_in)
    output_grad = dense(output_grad, output_weight)
    attend_grad = dense(attend_grad, attend_weight)
    router_parts = router_grad.reshape(n_fsdp, mod_rows, n_exp, -1).transpose(2, 0, 1, 3)
    router_parts = router_parts.reshape(n_all, mod_rows, -1)
    router_grad = jnp.sum(lax.all_to_all(router_parts, ALL, 0, 0, tiled=True), axis=0)
    return (
        block_out,
        patches_grad,
        cond_grad,
        modulate_grad,
        attend_grad,
        output_grad,
        router_grad,
        shared_in_grad,
        shared_out_grad,
        expert_in_grad,
        expert_out_grad,
    )


def solution(mesh):
    n_exp, n_fsdp = mesh.shape["exp"], mesh.shape["fsdp"]
    n_pair = E // n_exp
    if n_pair not in (1, 2) or n_fsdp % n_pair:
        raise ValueError("unsupported mesh")
    fine = Mesh(mesh.devices.reshape(n_exp, n_fsdp // n_pair, n_pair), ALL)
    ring = Ring(fine)
    fsdp = ("zi", "yi")
    in_specs = (
        P(ALL, None),
        P(ALL, None),
        P(ALL),
        P(ALL, None),
        P(ALL, None),
        P(fsdp, "exp"),
        P(fsdp, "exp"),
        P(fsdp, "exp"),
        P(fsdp, "exp"),
        P(fsdp, "exp"),
        P(fsdp, "exp"),
        P("exp", None, fsdp),
        P("exp", fsdp, None),
    )
    out_specs = (
        P(ALL, None),
        P(ALL, None),
        P(ALL, None),
        P(fsdp, "exp"),
        P(fsdp, "exp"),
        P(fsdp, "exp"),
        P(fsdp, "exp"),
        P(fsdp, "exp"),
        P(fsdp, "exp"),
        P("exp", None, fsdp),
        P("exp", fsdp, None),
    )

    def step(*args):
        return local(ring, *args)

    return jax.shard_map(step, mesh=fine, in_specs=in_specs, out_specs=out_specs, check_vma=False)
```

```python
import functools

import jax
import jax.numpy as jnp
from jax import lax
from jax.experimental import pallas as pl
from jax.experimental.pallas import tpu as pltpu
from jax.sharding import Mesh
from jax.sharding import PartitionSpec as P

H = 12
HD = 64
E = 8
TOPK = 2
SHORT = 256
GROUP = 1024
CAP = 288

F32 = jnp.float32
BF16 = jnp.bfloat16

eps_norm = 1e-06
tanh_gain = 0.7978845608028654
ALL = ("exp", "zi", "yi")
FSDP = ("zi", "yi")

PIECES = 4
STRIPS = 8
LANES = 128
OUT_LANES = 2 * LANES


def layer_norm(values):
    centered = values - jnp.mean(values, axis=-1, keepdims=True)
    inverse = lax.rsqrt(jnp.mean(centered * centered, axis=-1, keepdims=True) + eps_norm)
    return (centered * inverse, inverse)


def norm_back(grad, normed, inverse):
    return inverse * (
        grad
        - jnp.mean(grad, axis=-1, keepdims=True)
        - normed * jnp.mean(grad * normed, axis=-1, keepdims=True)
    )


def silu_slope(values):
    sigma = jax.nn.sigmoid(values)
    return sigma * (1.0 + values * (1.0 - sigma))


def dot(left, right, dims):
    return lax.dot_general(left, right, (dims, ((), ())), preferred_element_type=F32)


def mm(left, right):
    return dot(left, right, ((1,), (0,)))


def mm_rt(left, right):
    return dot(left, right, ((1,), (1,)))


def mm_lt(left, right):
    return dot(left, right, ((0,), (0,)))


def slot_table(expert_ids):
    flat = expert_ids.reshape(-1)
    onehot = (flat[:, None] == jnp.arange(E, dtype=jnp.int32)[None, :]).astype(jnp.int32)
    before = jnp.cumsum(onehot, axis=0) - onehot
    return jnp.sum(before * onehot, axis=1).reshape(expert_ids.shape)


def cost(flops, moved):
    return pl.CostEstimate(flops=flops, transcendentals=0, bytes_accessed=moved)


def fixed(shape):
    return pl.BlockSpec(shape, lambda *_: (0,) * len(shape), pipeline_mode=pl.Buffered(1))


LOG2E = 1.4426950408889634
SCORE = HD ** (-0.5)


def attend_kernel(kind_ref, query_ref, key_ref, value_ref, mixed_ref, logsum_ref):
    left = lax.broadcasted_iota(jnp.int32, (GROUP, 2 * HD), 1) < HD
    keys = key_ref[...]
    zero = jnp.zeros_like(keys)
    split_keys = (jnp.where(left, keys, zero), jnp.where(left, zero, keys))

    def rows_of(part, first, count):
        rows = pl.ds(part * SHORT, SHORT)
        query = query_ref[rows, :]
        value = value_ref[pl.ds(first, count), :]
        halves = []
        for half in range(2):
            scores = mm_rt(query, split_keys[half][first : first + count])
            peak = jnp.max(scores, axis=1, keepdims=True)
            weights = jnp.exp2((scores - peak) * (SCORE * LOG2E))
            total = jnp.sum(weights, axis=1, keepdims=True)
            halves.append(mm(weights.astype(BF16), value) / total)
            logsum = peak * (SCORE * LOG2E) + jnp.log2(total)
            logsum_ref[0, 0, half, rows] = jnp.transpose(
                jnp.broadcast_to(logsum, (SHORT, 2 * HD))
            )[0]
        mixed_ref[rows, :] = jnp.where(left[:SHORT], halves[0], halves[1]).astype(BF16)

    is_long = kind_ref[pl.program_id(0)] == 1

    @pl.when(is_long)
    def _():
        for part in range(GROUP // SHORT):
            rows_of(part, 0, GROUP)

    @pl.when(jnp.logical_not(is_long))
    def _():
        for part in range(GROUP // SHORT):
            rows_of(part, part * SHORT, SHORT)


def attend(triple, image_kind):
    groups = triple.shape[0] // GROUP
    pairs = H // 2

    def part(offset):
        return pl.BlockSpec((GROUP, 2 * HD), lambda g, i, kind: (g, offset + i))

    return pl.pallas_call(
        attend_kernel,
        out_shape=(
            jax.ShapeDtypeStruct((triple.shape[0], H * HD), BF16),
            jax.ShapeDtypeStruct((groups, pairs, 8, GROUP), F32),
        ),
        grid_spec=pltpu.PrefetchScalarGridSpec(
            num_scalar_prefetch=1,
            grid=(groups, pairs),
            in_specs=[part(0), part(pairs), part(2 * pairs)],
            out_specs=(
                part(0),
                pl.BlockSpec((1, 1, 8, GROUP), lambda g, i, kind: (g, i, 0, 0)),
            ),
        ),
        compiler_params=pltpu.CompilerParams(vmem_limit_bytes=32 << 20),
        cost_estimate=cost(16 * triple.shape[0] * GROUP * H * HD, 8 * triple.size),
        name="attend",
    )(image_kind, triple, triple, triple)


def attend_back_kernel(
    kind_ref,
    query_ref,
    key_ref,
    value_ref,
    mixed_ref,
    grad_ref,
    logsum_ref,
    grads_ref,
    key_sum,
    value_sum,
):
    left = lax.broadcasted_iota(jnp.int32, (GROUP, 2 * HD), 1) < HD

    def split(values):
        zero = jnp.zeros_like(values)
        return (jnp.where(left, values, zero), jnp.where(left, zero, values))

    split_query = split(query_ref[...])
    split_keys = split(key_ref[...])
    split_values = split(value_ref[...])
    split_grad = split(grad_ref[...])
    outer = jnp.transpose(mixed_ref[...].astype(F32) * grad_ref[...].astype(F32))
    inner = (
        jnp.sum(outer[:HD], axis=0, keepdims=True),
        jnp.sum(outer[HD:], axis=0, keepdims=True),
    )

    def rows_of(part, first, count, fresh):
        low, high = part * SHORT, (part + 1) * SHORT
        keys_at = pl.ds(first, count)
        query = query_ref[pl.ds(low, SHORT), :]
        grad = grad_ref[pl.ds(low, SHORT), :]
        key_part = value_part = query_part = None
        for half in range(2):
            keys = split_keys[half][first : first + count]
            scores = mm_rt(keys, query)
            logsum = logsum_ref[0, 0, half : half + 1, low:high]
            attention = jnp.exp2(scores * (SCORE * LOG2E) - logsum)
            moved = mm_rt(split_values[half][first : first + count], grad)
            grad_scores = (attention * (moved - inner[half][:, low:high])).astype(BF16)
            value_add = mm(attention.astype(BF16), split_grad[half][low:high])
            key_add = mm(grad_scores, split_query[half][low:high])
            query_add = mm_lt(grad_scores, keys)
            if half == 0:
                key_part, value_part, query_part = key_add, value_add, query_add
            else:
                key_part, value_part = key_part + key_add, value_part + value_add
                query_part = query_part + query_add
        grads_ref[0, pl.ds(low, SHORT), :] = (query_part * SCORE).astype(BF16)
        if fresh:
            key_sum[keys_at, :] = key_part
            value_sum[keys_at, :] = value_part
        else:
            key_sum[keys_at, :] += key_part
            value_sum[keys_at, :] += value_part

    is_long = kind_ref[pl.program_id(0)] == 1

    @pl.when(is_long)
    def _():
        for part in range(GROUP // SHORT):
            rows_of(part, 0, GROUP, part == 0)

    @pl.when(jnp.logical_not(is_long))
    def _():
        for part in range(GROUP // SHORT):
            rows_of(part, part * SHORT, SHORT, True)

    grads_ref[1, :, :] = (key_sum[...] * SCORE).astype(BF16)
    grads_ref[2, :, :] = value_sum[...].astype(BF16)


def attend_back(triple, attended, logsum, grad_attended, image_kind):
    groups = triple.shape[0] // GROUP
    pairs = H // 2

    def part(offset):
        return pl.BlockSpec((GROUP, 2 * HD), lambda g, i, kind: (g, offset + i))

    return pl.pallas_call(
        attend_back_kernel,
        out_shape=jax.ShapeDtypeStruct((3, triple.shape[0], H * HD), BF16),
        grid_spec=pltpu.PrefetchScalarGridSpec(
            num_scalar_prefetch=1,
            grid=(groups, pairs),
            in_specs=[
                part(0),
                part(pairs),
                part(2 * pairs),
                part(0),
                part(0),
                pl.BlockSpec((1, 1, 8, GROUP), lambda g, i, kind: (g, i, 0, 0)),
            ],
            out_specs=pl.BlockSpec((3, GROUP, 2 * HD), lambda g, i, kind: (0, g, i)),
            scratch_shapes=[pltpu.VMEM((GROUP, 2 * HD), F32)] * 2,
        ),
        compiler_params=pltpu.CompilerParams(vmem_limit_bytes=32 << 20),
        cost_estimate=cost(40 * triple.shape[0] * GROUP * H * HD, 12 * triple.size),
        name="attend_back",
    )(image_kind, triple, triple, triple, attended, grad_attended, logsum)


def gelu_both(values):
    square = values * values
    side = tanh_gain * 0.044715 * square
    half = 0.5 + 0.5 * jnp.tanh(values * (tanh_gain + side))
    slope = half + 2.0 * values * (tanh_gain + 3.0 * side) * (half * (1.0 - half))
    return values * half, slope


def way(me, piece, strip):
    sx, other = (piece >> 1) ^ me[1], (piece & 1) ^ me[0]
    sy, k = (strip & 1) ^ me[2], (me[3] - (strip >> 1)) & 3
    return other, sx, sy, k


def on_side(other, own_ref, other_ref, action):
    @pl.when(other == 0)
    def _():
        action(own_ref)

    @pl.when(other == 1)
    def _():
        action(other_ref)


def normalize(values):
    mean = jnp.mean(values, axis=1, keepdims=True)
    centered = values - mean
    return centered * lax.rsqrt(jnp.mean(centered * centered, axis=1, keepdims=True) + eps_norm)


def triple_kernel(me, x_ref, shift_ref, scale_ref, q1a, q1b, q2a, q2b, in_ref, out_ref, weight_ref):
    rows, cols = q1a.shape[3], q1a.shape[4] - OUT_LANES

    @pl.when(pl.program_id(0) == 0)
    def _():
        for piece in range(PIECES):
            for strip in range(STRIPS):
                other, sx, sy, k = way(me, piece, strip)
                low, at = strip * 2 * rows, slice(piece * cols, (piece + 1) * cols)

                def first(ref):
                    weight_ref[low : low + rows, at] = ref[sx, sy, k, :, OUT_LANES:]

                def second(ref):
                    weight_ref[low + rows : low + 2 * rows, at] = ref[sy, sx, k, :, OUT_LANES:]

                on_side(other, q1a, q1b, first)
                on_side(other, q2a, q2b, second)

    normed = normalize(x_ref[...].astype(F32))
    attend_in = (normed * (1.0 + scale_ref[0]) + shift_ref[0]).astype(BF16)
    in_ref[...] = attend_in
    out_ref[...] = mm(attend_in, weight_ref[...]).astype(BF16)


def make_triple(me, patches, shift, scale, weights):
    tok_count, width = patches.shape
    hidden = PIECES * (weights[0].shape[4] - OUT_LANES)
    rows = pl.BlockSpec((SHORT, width), lambda i, me: (i, 0))
    each = pl.BlockSpec((1, 1, width), lambda i, me: (i, 0, 0))
    return pl.pallas_call(
        triple_kernel,
        out_shape=(
            jax.ShapeDtypeStruct((tok_count, width), BF16),
            jax.ShapeDtypeStruct((tok_count, hidden), BF16),
            jax.ShapeDtypeStruct((width, hidden), BF16),
        ),
        grid_spec=pltpu.PrefetchScalarGridSpec(
            num_scalar_prefetch=1,
            grid=(tok_count // SHORT,),
            in_specs=[rows, each, each] + [fixed(w.shape) for w in weights],
            out_specs=(
                rows,
                pl.BlockSpec((SHORT, hidden), lambda i, me: (i, 0)),
                fixed((width, hidden)),
            ),
        ),
        compiler_params=pltpu.CompilerParams(vmem_limit_bytes=40 << 20),
        cost_estimate=cost(2 * tok_count * width * hidden, 8 * tok_count * width),
        name="triple",
    )(me, patches, shift, scale, *weights)


def project_kernel(
    me,
    attended_ref,
    x_ref,
    gate_ref,
    shift_ref,
    scale_ref,
    q1a,
    q1b,
    q2a,
    q2b,
    projected_ref,
    residual_ref,
    branch_ref,
    logits_ref,
    weight_ref,
    router_ref,
):
    width = x_ref.shape[1]
    rows, cols, experts = q1a.shape[3], width // PIECES, E // PIECES

    @pl.when(pl.program_id(0) == 0)
    def _():
        router_ref[...] = jnp.zeros_like(router_ref)
        for piece in range(PIECES):
            for strip in range(STRIPS):
                other, sx, sy, k = way(me, piece, strip)

                def place(block, low):
                    weight_ref[low : low + rows, piece * cols : (piece + 1) * cols] = block[
                        :, :cols
                    ]
                    router_ref[
                        low : low + rows, piece * experts : (piece + 1) * experts
                    ] = block[:, cols : cols + experts]

                def first(ref):
                    place(ref[sx, sy, k], strip * 2 * rows)

                def second(ref):
                    place(ref[sy, sx, k], strip * 2 * rows + rows)

                on_side(other, q1a, q1b, first)
                on_side(other, q2a, q2b, second)

    projected = mm(attended_ref[...], weight_ref[...])
    projected_ref[...] = projected
    residual = x_ref[...].astype(F32) + gate_ref[0] * projected
    residual_ref[...] = residual
    branch = (normalize(residual) * (1.0 + scale_ref[0]) + shift_ref[0]).astype(BF16)
    branch_ref[...] = branch
    logits_ref[...] = mm(branch, router_ref[...])


def make_branch(me, attended, patches, gate, shift, scale, weights):
    tok_count, width = patches.shape
    rows = pl.BlockSpec((SHORT, width), lambda i, me: (i, 0))
    each = pl.BlockSpec((1, 1, width), lambda i, me: (i, 0, 0))
    outs = fixed(weights[0].shape[:4] + (OUT_LANES,))
    return pl.pallas_call(
        project_kernel,
        out_shape=(
            jax.ShapeDtypeStruct((tok_count, width), F32),
            jax.ShapeDtypeStruct((tok_count, width), F32),
            jax.ShapeDtypeStruct((tok_count, width), BF16),
            jax.ShapeDtypeStruct((tok_count, LANES), F32),
            jax.ShapeDtypeStruct((width, width), BF16),
            jax.ShapeDtypeStruct((width, LANES), BF16),
        ),
        grid_spec=pltpu.PrefetchScalarGridSpec(
            num_scalar_prefetch=1,
            grid=(tok_count // SHORT,),
            in_specs=[rows, rows, each, each, each, outs, outs, outs, outs],
            out_specs=(
                rows,
                rows,
                rows,
                pl.BlockSpec((SHORT, LANES), lambda i, me: (i, 0)),
                fixed((width, width)),
                fixed((width, LANES)),
            ),
        ),
        compiler_params=pltpu.CompilerParams(vmem_limit_bytes=32 << 20),
        cost_estimate=cost(2 * tok_count * width * width, 16 * tok_count * width),
        name="project",
    )(me, attended, patches, gate, shift, scale, *weights)


def shared_kernel(
    x_ref,
    grad_ref,
    in_ref,
    out_ref,
    res_ref,
    x_grad_ref,
    weight_grad_ref,
    weight_out,
    x_turned,
    grad_turned,
):
    step = pl.program_id(0)
    width = x_ref.shape[1]
    rows, half = width // STRIPS, width // 2

    @pl.when(step == 0)
    def _():
        x_turned[...] = jnp.transpose(x_ref[...])
        grad_turned[...] = jnp.transpose(grad_ref[...])

    halves = [slice(0, half), slice(half, width)]
    for piece in range(PIECES):
        for strip in range(2):
            for part in range(2):
                low = (2 * piece + part) * rows
                weight_out[low : low + rows, halves[strip]] = out_ref[piece, strip, :, halves[part]]
    weight_in = in_ref[...].reshape(width, width)
    act, slope = gelu_both(mm(x_ref[...], weight_in))
    act = act.astype(BF16)
    grad_pre = (mm(grad_ref[...], weight_out[...]) * slope).astype(BF16)
    res = mm_rt(act, weight_out[...])
    x_grad = mm_rt(grad_pre, weight_in)

    @pl.when(step == 0)
    def _():
        res_ref[...] = res
        x_grad_ref[...] = x_grad

    @pl.when(step != 0)
    def _():
        res_ref[...] += res
        x_grad_ref[...] += x_grad

    in_grad = mm(x_turned[...], grad_pre).astype(BF16)
    out_grad = mm(grad_turned[...], act).astype(BF16)
    weight_grad_ref[step, :, :rows, :] = in_grad.reshape(STRIPS, rows, width)
    for piece in range(PIECES):
        for strip in range(2):
            for part in range(2):
                low = (2 * piece + part) * rows
                weight_grad_ref[piece, 2 * step + strip, rows:, halves[part]] = out_grad[
                    low : low + rows, halves[strip]
                ]


def shared_expert(x, grad, weights):
    tok_count, width = x.shape
    rows = width // STRIPS
    whole = fixed((tok_count, width))
    return pl.pallas_call(
        shared_kernel,
        out_shape=(
            jax.ShapeDtypeStruct((tok_count, width), F32),
            jax.ShapeDtypeStruct((tok_count, width), F32),
            jax.ShapeDtypeStruct(weights.shape, BF16),
        ),
        grid=(PIECES,),
        in_specs=[
            whole,
            whole,
            pl.BlockSpec((1, STRIPS, rows, width), lambda j: (j, 0, 0, 0)),
            pl.BlockSpec((PIECES, 2, rows, width), lambda j: (0, j, 1, 0)),
        ],
        out_specs=(whole, whole, fixed(weights.shape)),
        scratch_shapes=[pltpu.VMEM((width, width), BF16)]
        + [pltpu.VMEM((width, tok_count), BF16)] * 2,
        compiler_params=pltpu.CompilerParams(vmem_limit_bytes=56 << 20),
        cost_estimate=cost(12 * tok_count * width * 4 * width, 16 * tok_count * width),
        name="shared_expert",
    )(x, grad, weights, weights)


def project_back_kernel(
    attended_ref, grad_ref, branch_ref, logits_ref, weight_ref, back_ref, out_grad_ref, router_ref
):
    back_ref[...] = mm_rt(grad_ref[...], weight_ref[...]).astype(BF16)
    out_grad_ref[...] = mm_lt(attended_ref[...], grad_ref[...]).astype(BF16)
    router_ref[...] = mm_lt(branch_ref[...], logits_ref[...]).astype(BF16)


def project_back(attended, grad, branch, grad_logits, weight):
    tok_count, width = attended.shape
    whole = fixed((tok_count, width))
    return pl.pallas_call(
        project_back_kernel,
        out_shape=(
            jax.ShapeDtypeStruct((tok_count, width), BF16),
            jax.ShapeDtypeStruct((width, width), BF16),
            jax.ShapeDtypeStruct((width, LANES), BF16),
        ),
        grid=(1,),
        in_specs=[whole, whole, whole, fixed((tok_count, LANES)), fixed((width, width))],
        out_specs=(whole, fixed((width, width)), fixed((width, LANES))),
        compiler_params=pltpu.CompilerParams(vmem_limit_bytes=32 << 20),
        cost_estimate=cost(4 * tok_count * width * width, 8 * tok_count * width),
        name="project_back",
    )(attended, grad, branch, grad_logits, weight)


def triple_back_kernel(
    me,
    grad_ref,
    in_ref,
    weight_ref,
    out_grad_ref,
    router_ref,
    back_ref,
    q1a,
    q1b,
    q2a,
    q2b,
    in_turned,
    weight_grad,
):
    step = pl.program_id(0)
    rows, cols = q1a.shape[3], q1a.shape[4] - OUT_LANES
    width = in_ref.shape[1]
    outs, experts = width // PIECES, E // PIECES

    @pl.when(step == 0)
    def _():
        in_turned[...] = jnp.transpose(in_ref[...])

    grad = grad_ref[0]
    at = pl.ds(pl.multiple_of(step * width, LANES), width)
    weight_grad[:, at] = mm(in_turned[...], grad).astype(BF16)
    back = mm_rt(grad, weight_ref[...])

    @pl.when(step == 0)
    def _():
        back_ref[...] = back

    @pl.when(step != 0)
    def _():
        back_ref[...] += back

    @pl.when(step == 2)
    def _():
        for piece in range(PIECES):
            for strip in range(STRIPS):
                other, sx, sy, k = way(me, piece, strip)

                def place(ref, where, low):
                    at = slice(low, low + rows)
                    ref[where + (slice(None), slice(0, outs))] = out_grad_ref[
                        at, piece * outs : (piece + 1) * outs
                    ]
                    ref[where + (slice(None), slice(outs, outs + experts))] = router_ref[
                        at, piece * experts : (piece + 1) * experts
                    ]
                    ref[where + (slice(None), slice(outs + experts, OUT_LANES))] = jnp.zeros(
                        (rows, OUT_LANES - outs - experts), BF16
                    )
                    ref[where + (slice(None), slice(OUT_LANES, None))] = weight_grad[
                        at, piece * cols : (piece + 1) * cols
                    ]

                def first(ref):
                    place(ref, (sx, sy, k), strip * 2 * rows)

                def second(ref):
                    place(ref, (sy, sx, k), strip * 2 * rows + rows)

                on_side(other, q1a, q1b, first)
                on_side(other, q2a, q2b, second)


def triple_back(me, grads, attend_in, weight, out_grad, router_grad):
    tok_count, width = attend_in.shape
    hidden = weight.shape[1]
    block = (2, 2, 4, width // STRIPS // 2, OUT_LANES + hidden // PIECES)
    block = jax.ShapeDtypeStruct(block, BF16)
    return pl.pallas_call(
        triple_back_kernel,
        out_shape=(jax.ShapeDtypeStruct((tok_count, width), F32),) + (block,) * 4,
        grid_spec=pltpu.PrefetchScalarGridSpec(
            num_scalar_prefetch=1,
            grid=(3,),
            in_specs=[
                pl.BlockSpec((1, tok_count, width), lambda p, me: (p, 0, 0)),
                fixed((tok_count, width)),
                pl.BlockSpec((width, width), lambda p, me: (0, p)),
                fixed((width, width)),
                fixed((width, LANES)),
            ],
            out_specs=(fixed((tok_count, width)),) + (fixed(block.shape),) * 4,
            scratch_shapes=[
                pltpu.VMEM((width, tok_count), BF16),
                pltpu.VMEM((width, hidden), BF16),
            ],
        ),
        compiler_params=pltpu.CompilerParams(vmem_limit_bytes=40 << 20),
        cost_estimate=cost(4 * tok_count * width * hidden, 12 * tok_count * width),
        name="triple_back",
    )(me, grads, attend_in, weight, out_grad, router_grad)


ROW_TILE = 576


def expert_kernel(parts, x_ref, *refs):
    weights, (res_ref, act_ref, slope_ref) = refs[:parts], refs[parts:]
    x = x_ref[...]
    total = None
    for part in range(parts):
        width = weights[part].shape[1]
        at = pl.ds(part * width, width)
        act, slope = gelu_both(mm(x, weights[part][:width, :]))
        act = act.astype(BF16)
        act_ref[:, at] = act
        slope_ref[:, at] = slope.astype(BF16)
        res = mm(act, weights[part][width:, :])
        total = res if total is None else total + res
    res_ref[...] = total.astype(BF16)


def expert_back_kernel(parts, grad_ref, slope_ref, *refs):
    weights, (rows_ref, pre_ref) = refs[:parts], refs[parts:]
    grad = grad_ref[...]
    total = None
    for part in range(parts):
        width = weights[part].shape[1]
        at = pl.ds(part * width, width)
        grad_pre = mm_rt(grad, weights[part][width:, :]) * slope_ref[:, at].astype(F32)
        grad_pre = grad_pre.astype(BF16)
        pre_ref[:, at] = grad_pre
        rows = mm_rt(grad_pre, weights[part][:width, :])
        total = rows if total is None else total + rows
    rows_ref[...] = total.astype(BF16)


def expert_call(kernel, name, rows_in, wide_in, weights, n_wide):
    rows, width = rows_in.shape
    hidden = len(weights) * width
    narrow = pl.BlockSpec((ROW_TILE, width), lambda i: (i, 0))
    wide = pl.BlockSpec((ROW_TILE, hidden), lambda i: (i, 0))
    fixed = pl.BlockSpec((2 * width, width), lambda i: (0, 0), pipeline_mode=pl.Buffered(1))
    return pl.pallas_call(
        functools.partial(kernel, len(weights)),
        out_shape=(jax.ShapeDtypeStruct((rows, width), BF16),)
        + (jax.ShapeDtypeStruct((rows, hidden), BF16),) * n_wide,
        grid=(rows // ROW_TILE,),
        in_specs=[narrow] + [wide] * len(wide_in) + [fixed] * len(weights),
        out_specs=(narrow,) + (wide,) * n_wide,
        compiler_params=pltpu.CompilerParams(vmem_limit_bytes=48 << 20),
        cost_estimate=cost(8 * rows * hidden * width, 2 * rows * hidden * (1 + n_wide)),
        name=name,
    )(rows_in, *wide_in, *weights)


def by_way(blocks, y_outer):
    rows, cols = blocks.shape[2:]
    blocks = blocks.reshape(2, 2, 4, 2, rows, cols)[:, :, jnp.array([0, 3, 2, 1])]
    blocks = blocks.transpose((1, 3, 0, 2, 4, 5) if y_outer else (1, 0, 3, 2, 4, 5))
    return blocks[0], blocks[1]


def by_place(own, other, y_outer):
    blocks = jnp.stack((own, other))
    blocks = blocks.transpose((2, 0, 3, 1, 4, 5) if y_outer else (1, 0, 3, 2, 4, 5))
    rows, cols = blocks.shape[4:]
    return blocks[:, :, jnp.array([0, 3, 2, 1])].reshape(PIECES, STRIPS, rows, cols)


def to_blocks(whole):
    rows, cols = whole.shape
    return whole.reshape(STRIPS, rows // STRIPS, PIECES, cols // PIECES).transpose(2, 0, 1, 3)


def to_whole(blocks):
    rows, cols = blocks.shape[2:]
    return blocks.transpose(1, 2, 0, 3).reshape(STRIPS * rows, PIECES * cols)


def turn(block):
    block = block.T
    half = block.shape[0] // 2
    return jnp.concatenate((block[:half], block[half:]), axis=1)


def turn_back(block):
    half = block.shape[1] // 2
    return jnp.concatenate((block[:, :half], block[:, half:]), axis=0).T


def shared_bundle(up, down):
    down = to_blocks(down).swapaxes(2, 3)
    half = down.shape[2] // 2
    return jnp.concatenate(
        (to_blocks(up), jnp.concatenate((down[:, :, :half], down[:, :, half:]), axis=3)), axis=2
    )


def shared_unbundle(grads):
    rows, half = grads.shape[2] // 2, grads.shape[3] // 2
    down = grads[:, :, rows:]
    down = jnp.concatenate((down[..., :half], down[..., half:]), axis=2).swapaxes(2, 3)
    return to_whole(grads[:, :, :rows]), to_whole(down)


class Ring:
    def __init__(self, mesh):
        self.n_exp = mesh.shape["exp"]
        self.n_ring = mesh.shape["zi"]
        self.n_pair = mesh.shape["yi"]
        self.direct = (self.n_exp, self.n_ring, self.n_pair) == (PIECES, 4, 2)

    def step(self, value, by=1):
        n = self.n_ring
        return lax.ppermute(value, "zi", [(i, (i + by) % n) for i in range(n)])

    def over_y(self, value):
        return lax.ppermute(value, "yi", [(0, 1), (1, 0)])

    def over_x(self, value):
        return lax.ppermute(value, "exp", [(i, i ^ 2) for i in range(4)])

    def over_core(self, value):
        return lax.ppermute(value, "exp", [(i, i ^ 1) for i in range(4)])

    def near(self, block):
        return jnp.stack([block] + [self.step(block, k) for k in range(1, 4)])

    def second(self, held, y_outer):
        return jnp.stack((held, (self.over_x if y_outer else self.over_y)(held)))

    def third(self, held, y_outer):
        return jnp.stack((held, (self.over_y if y_outer else self.over_x)(held)))

    def outer(self, value, y_outer):
        return (self.over_y if y_outer else self.over_x)(value)

    def inner(self, value, y_outer):
        return (self.over_x if y_outer else self.over_y)(value)

    def line(self, held):
        return tuple(self.step(held[k], -k) for k in range(1, 4))


def add_both(keep, got):
    return add(keep[0], got[0]), add(keep[1], got[1])


def add_line(held, got):
    total = held.astype(F32)
    for part in got:
        total = total + part.astype(F32)
    return total


def add(left, right):
    return (left.astype(F32) + right.astype(F32)).astype(BF16)


def tie(*values):
    return lax.optimization_barrier(values)


def after(value, *others):
    return lax.optimization_barrier((value,) + others)[0]


def picked_experts(ring, y, expert_in, expert_out):
    own_in = jnp.where(y == 0, expert_in[0], expert_in[1])
    give_in = jnp.where(y == 0, expert_in[1], expert_in[0])
    own_out = jnp.where(y == 0, expert_out[0], expert_out[1])
    give_out = jnp.where(y == 0, expert_out[1], expert_out[0])
    ups = jnp.concatenate((own_in, ring.over_y(give_in)), axis=1)
    downs = jnp.concatenate((own_out, ring.over_y(give_out)), axis=0)
    return jnp.concatenate((ups, downs), axis=0)


def local(
    ring,
    patches,
    cond_embed,
    image_kind,
    expert_ids,
    out_grad,
    modulate_weight,
    attend_weight,
    output_weight,
    router_weight,
    shared_in,
    shared_out,
    expert_in,
    expert_out,
):
    tok_count, width = patches.shape
    blocks = tok_count // SHORT
    n_exp, n_ring, n_pair = ring.n_exp, ring.n_ring, ring.n_pair
    n_fsdp = n_ring * n_pair
    n_all = n_exp * n_fsdp
    e, z, y = (lax.axis_index(name) for name in ("exp", "zi", "yi"))
    mod_rows, mod_cols = modulate_weight.shape
    half = width // STRIPS // 2
    if ring.direct:
        me = jnp.stack((e & 1, e >> 1, y, z)).astype(jnp.int32)
    else:
        me = jnp.zeros((4,), jnp.int32)

    cond_float = cond_embed.astype(F32)
    cond_act = jax.nn.silu(cond_float).astype(BF16)
    cond_send = cond_act.reshape(blocks, n_fsdp, mod_rows).transpose(1, 0, 2)
    cond_send = jnp.broadcast_to(cond_send[None], (n_exp, n_fsdp, blocks, mod_rows))
    cond_all = lax.all_to_all(
        cond_send.reshape(n_all, blocks, mod_rows), ALL, 0, 0, tiled=True
    ).reshape(n_all * blocks, mod_rows)
    mod_part = mm(cond_all, modulate_weight).reshape(n_all, blocks, mod_cols)
    mod_early = mod_part
    mod_part = lax.all_to_all(mod_part, ALL, 0, 0, tiled=True)
    modulation = jnp.sum(mod_part.reshape(n_exp, n_fsdp, blocks, mod_cols), axis=1)
    modulation = modulation.transpose(1, 0, 2).reshape(blocks, 1, 6, width)

    if ring.direct:
        spare = OUT_LANES - output_weight.shape[1] - router_weight.shape[1]
        block = jnp.concatenate(
            (
                output_weight,
                router_weight,
                jnp.zeros((router_weight.shape[0], spare), BF16),
                attend_weight,
            ),
            axis=1,
        )
        bundle = jnp.concatenate((shared_in, turn(shared_out)), axis=0)
        shared_weights = lax.all_gather(bundle, ALL, axis=0, tiled=False)
        shared_weights = shared_weights.reshape((PIECES, STRIPS) + bundle.shape)
        expert_block = picked_experts(ring, y, expert_in, expert_out)
        held = after(ring.near(block), mod_early)
        held_1 = ring.second(held[:, :half], False)
        held_2 = ring.second(held[:, half:], True)
        held_1 = ring.third(after(held_1, expert_block), False)
        held_2 = ring.third(after(held_2, expert_block), True)
        dense_weights = (held_1, ring.over_core(held_1), held_2, ring.over_core(held_2))
        expert_block = after(expert_block, modulation)
        expert_weights = [expert_block, ring.step(expert_block)]
    else:
        wholes = [
            lax.all_gather(
                lax.all_gather(w, FSDP, axis=0, tiled=True), "exp", axis=1, tiled=True
            )
            for w in (attend_weight, output_weight, router_weight, shared_in, shared_out)
        ]
        attend_all, output_all, router_all = map(to_blocks, wholes[:3])
        up_all, down_all = wholes[3:]
        spare = jnp.zeros((PIECES, STRIPS, 2 * half, OUT_LANES - (width + E) // PIECES), BF16)
        dense_all = jnp.concatenate((output_all, router_all, spare, attend_all), axis=3)
        dense_weights = by_way(dense_all[:, :, :half], False)
        dense_weights += by_way(dense_all[:, :, half:], True)
        shared_weights = shared_bundle(up_all, down_all)
        up_all = lax.all_gather(expert_in[0], FSDP, axis=1, tiled=True)
        down_all = lax.all_gather(expert_out[0], FSDP, axis=0, tiled=True)
        expert_weights = [
            jnp.concatenate((up_all[:, at : at + width], down_all[at : at + width]), axis=0)
            for at in range(0, up_all.shape[1], width)
        ]

    shift_first = modulation[:, :, 0]
    scale_first = modulation[:, :, 1]
    gate_first = modulation[:, :, 2]
    shift_second = modulation[:, :, 3]
    scale_second = modulation[:, :, 4]
    gate_second = modulation[:, :, 5]
    attend_in, triple, triple_weight = make_triple(
        me, patches, shift_first, scale_first, dense_weights
    )
    attended, logsum = attend(triple, image_kind)
    projected, residual, branch_in, logits, output_weight_all, router_all = make_branch(
        me, attended, patches, gate_first, shift_second, scale_second, dense_weights
    )
    if ring.direct:
        branch_in = after(branch_in, expert_weights[1])
        expert_weights.append(ring.step(expert_weights[1]))
    choose = expert_ids[:, :, None] == jnp.arange(E, dtype=jnp.int32)[None, None, :]
    choose = choose.astype(F32)
    gates = jax.nn.softmax(jnp.sum(choose * logits[:, None, :E], axis=-1), axis=-1)

    grad_out = out_grad.astype(F32).reshape(blocks, SHORT, width)
    grad_branch = (gate_second * grad_out).astype(BF16).reshape(tok_count, width)
    grad_branch_wide = grad_branch.astype(F32)

    slots = slot_table(expert_ids)
    target = expert_ids * CAP + slots
    row_of = jnp.arange(E * CAP, dtype=jnp.int32)[:, None]
    pick0 = (row_of == target[None, :, 0]).astype(BF16)
    pick1 = (row_of == target[None, :, 1]).astype(BF16)
    send_rows = mm(pick0 + pick1, branch_in).astype(BF16).reshape(E, CAP, width)
    grad_picked = (gates[:, :, None] * grad_branch_wide[:, None, :]).astype(BF16)
    grad_send = mm(pick0, grad_picked[:, 0]) + mm(pick1, grad_picked[:, 1])
    grad_send = grad_send.astype(BF16).reshape(E, CAP, width)
    shared_x = after(branch_in, send_rows, grad_send)

    def exchange(rows):
        return lax.all_to_all(rows, ("exp", "yi"), 0, 0, tiled=True)

    received = exchange(send_rows)

    shared_res, grad_branch_in, shared_grads = shared_expert(shared_x, grad_branch, shared_weights)

    received = after(received, shared_res)
    if ring.direct:
        expert_weights[2] = after(expert_weights[2], shared_res)
        expert_weights.append(ring.step(expert_weights[2]))
        expert_weights = expert_weights[1:] + expert_weights[:1]
    received = received.reshape(-1, width)
    grad_received = exchange(after(grad_send, received))
    expert_res, expert_act, expert_slope = expert_call(
        expert_kernel, "experts", received, (), expert_weights, 2
    )
    grad_received = grad_received.reshape(-1, width)
    expert_res = after(expert_res, grad_received)
    returned = exchange(expert_res.reshape(E, CAP, width))
    grad_rows, grad_pre = expert_call(
        expert_back_kernel, "experts_back", grad_received, (expert_slope,), expert_weights, 1
    )
    returned = returned.reshape(-1, width)
    grad_rows = after(grad_rows, returned)
    grad_returned = exchange(grad_rows.reshape(E, CAP, width)).reshape(-1, width)

    def expert_grads(part):
        at = slice(part * width, (part + 1) * width)
        return jnp.concatenate(
            (
                mm_lt(received, grad_pre[:, at]).astype(BF16),
                mm_lt(expert_act[:, at], grad_received).astype(BF16),
            ),
            axis=0,
        )

    grad_blocks = [expert_grads(part) for part in range(len(expert_weights))]
    returned = after(returned, *grad_blocks)
    if ring.direct:
        moved = ring.step(grad_blocks[0])

    picked0 = mm_lt(pick0, returned)
    picked1 = mm_lt(pick1, returned)
    mixture = gates[:, 0:1] * picked0 + gates[:, 1:2] * picked1
    branch_out = (shared_res + mixture).reshape(blocks, SHORT, width)
    projected = projected.reshape(blocks, SHORT, width)
    residual = residual.reshape(blocks, SHORT, width)
    normed_second, inverse_second = layer_norm(residual)
    block_out = (residual + gate_second * branch_out).reshape(tok_count, width).astype(BF16)
    grad_gate_second = jnp.sum(grad_out * branch_out, axis=1)
    grad_gates = jnp.stack(
        (
            jnp.sum(grad_branch_wide * picked0, axis=-1),
            jnp.sum(grad_branch_wide * picked1, axis=-1),
        ),
        axis=1,
    )
    grad_chosen = gates * (grad_gates - jnp.sum(gates * grad_gates, axis=-1, keepdims=True))
    grad_logits = jnp.sum(choose * grad_chosen[:, :, None], axis=1).astype(BF16)
    grad_logits = jnp.concatenate((grad_logits, jnp.zeros((tok_count, LANES - E), BF16)), axis=1)
    grad_branch_in = (
        grad_branch_in
        + mm_lt(pick0 + pick1, grad_returned)
        + mm_rt(grad_logits, router_all)
    )
    grad_norm_in = grad_branch_in.reshape(blocks, SHORT, width)
    grad_shift_second = jnp.sum(grad_norm_in, axis=1)
    grad_scale_second = jnp.sum(grad_norm_in * normed_second, axis=1)
    grad_residual = grad_out + norm_back(
        grad_norm_in * (1.0 + scale_second), normed_second, inverse_second
    )
    grad_gate_first = jnp.sum(grad_residual * projected, axis=1)
    grad_projected = (gate_first * grad_residual).astype(BF16).reshape(tok_count, width)
    grad_attended, out_grad_all, router_grad_all = project_back(
        attended, grad_projected, branch_in, grad_logits, output_weight_all
    )
    if ring.direct:
        grad_attended, moved = tie(grad_attended, moved)
        moved = ring.step(add(moved, grad_blocks[1]))
    grad_triple = attend_back(triple, attended, logsum, grad_attended, image_kind)
    if ring.direct:
        grad_triple, moved = tie(grad_triple, moved)
        moved = ring.step(add(moved, grad_blocks[2]))
    grad_attend_in, *dense_grads = triple_back(
        me, grad_triple, attend_in, triple_weight, out_grad_all, router_grad_all
    )
    if ring.direct:
        own_1, give_1, own_2, give_2 = dense_grads
        sum_1, give_1 = add_both(own_1, ring.over_core(give_1))
        sum_2, give_2 = add_both(own_2, ring.over_core(give_2))
        got_1, got_2 = ring.outer(give_1, False), ring.outer(give_2, True)
    inputs = patches.astype(F32).reshape(blocks, SHORT, width)
    normed_first, inverse_first = layer_norm(inputs)
    grad_attend_in = grad_attend_in.reshape(blocks, SHORT, width)
    grad_shift_first = jnp.sum(grad_attend_in, axis=1)
    grad_scale_first = jnp.sum(grad_attend_in * normed_first, axis=1)
    patches_grad = grad_residual + norm_back(
        grad_attend_in * (1.0 + scale_first), normed_first, inverse_first
    )
    patches_grad = patches_grad.reshape(tok_count, width)

    grad_modulation = jnp.stack(
        (
            grad_shift_first,
            grad_scale_first,
            grad_gate_first,
            grad_shift_second,
            grad_scale_second,
            grad_gate_second,
        ),
        axis=1,
    )
    grad_modulation = grad_modulation.reshape(blocks, n_exp, mod_cols).astype(BF16)
    mod_send = jnp.broadcast_to(
        grad_modulation.transpose(1, 0, 2)[:, None], (n_exp, n_fsdp, blocks, mod_cols)
    )
    mod_all = lax.all_to_all(
        mod_send.reshape(n_all, blocks, mod_cols), ALL, 0, 0, tiled=True
    ).reshape(n_all * blocks, mod_cols)
    modulate_grad = mm_lt(cond_all, mod_all)
    cond_part = mm_rt(mod_all, modulate_weight).reshape(n_all, blocks, mod_rows)
    if ring.direct:
        mod_all = after(mod_all, got_1, got_2)
        sum_1, give_1 = add_both(sum_1, got_1)
        sum_2, give_2 = add_both(sum_2, got_2)
        sum_1 = add(sum_1, ring.inner(give_1, False))
        sum_2 = add(sum_2, ring.inner(give_2, True))
        cond_part = after(cond_part, sum_1, sum_2)
    cond_part = lax.all_to_all(cond_part, ALL, 0, 0, tiled=True)
    cond_grad = jnp.sum(cond_part.reshape(n_exp, n_fsdp, blocks, mod_rows), axis=0)
    cond_grad = cond_grad.transpose(1, 0, 2).reshape(blocks, width) * silu_slope(cond_float)

    if ring.direct:
        cols, experts = width // PIECES, E // PIECES
        summed = jnp.concatenate(
            (add_line(sum_1[0], ring.line(sum_1)), add_line(sum_2[0], ring.line(sum_2))), axis=0
        )
        output_grad, router_grad = summed[:, :cols], summed[:, cols : cols + experts]
        attend_grad = summed[:, OUT_LANES:]
        summed = lax.psum_scatter(
            shared_grads.reshape((n_all,) + bundle.shape), ALL, scatter_dimension=0
        ).astype(F32)
        shared_in_grad = summed[: 2 * half]
        shared_out_grad = turn_back(summed[2 * half :])
        moved = moved.astype(F32) + grad_blocks[3].astype(F32)
        up_sum, down_sum = moved[:width], moved[width:]
        split = width // 2
        got_up = ring.over_y(up_sum[:, split:].astype(BF16)).astype(F32)
        got_down = ring.over_y(down_sum[split:].astype(BF16)).astype(F32)
        own_up, own_down = up_sum[:, :split], down_sum[:split]
        expert_in_grad = jnp.stack(
            (jnp.where(y == 0, own_up, got_up), jnp.where(y == 0, got_up, own_up))
        )
        expert_out_grad = jnp.stack(
            (jnp.where(y == 0, own_down, got_down), jnp.where(y == 0, got_down, own_down))
        )
    else:

        def spread(grad):
            part = lax.psum_scatter(grad, "exp", scatter_dimension=1, tiled=True)
            return lax.psum_scatter(part, FSDP, scatter_dimension=0, tiled=True).astype(F32)

        dense_all = jnp.concatenate(
            (by_place(*dense_grads[:2], False), by_place(*dense_grads[2:], True)), axis=2
        )
        cols, experts = width // PIECES, E // PIECES
        attend_grad = spread(to_whole(dense_all[..., OUT_LANES:]))
        output_grad = spread(to_whole(dense_all[..., :cols]))
        router_grad = spread(to_whole(dense_all[..., cols : cols + experts]))
        shared_in_grad, shared_out_grad = map(spread, shared_unbundle(shared_grads))
        up_sum = jnp.concatenate([b[:width] for b in grad_blocks], axis=1)
        down_sum = jnp.concatenate([b[width:] for b in grad_blocks], axis=0)
        expert_in_grad = lax.psum_scatter(up_sum, FSDP, scatter_dimension=1, tiled=True)
        expert_out_grad = lax.psum_scatter(down_sum, FSDP, scatter_dimension=0, tiled=True)
        expert_in_grad = expert_in_grad.astype(F32)[None]
        expert_out_grad = expert_out_grad.astype(F32)[None]
    return (
        block_out,
        patches_grad,
        cond_grad,
        modulate_grad,
        attend_grad,
        output_grad,
        router_grad,
        shared_in_grad,
        shared_out_grad,
        expert_in_grad,
        expert_out_grad,
    )


def solution(mesh):
    n_exp, n_fsdp = mesh.shape["exp"], mesh.shape["fsdp"]
    n_pair = E // n_exp
    if n_pair not in (1, 2) or n_fsdp % n_pair:
        raise ValueError("unsupported mesh")
    fine = Mesh(mesh.devices.reshape(n_exp, n_fsdp // n_pair, n_pair), ALL)
    ring = Ring(fine)
    in_specs = (
        P(ALL, None),
        P(ALL, None),
        P(ALL),
        P(ALL, None),
        P(ALL, None),
        P(FSDP, "exp"),
        P(FSDP, "exp"),
        P(FSDP, "exp"),
        P(FSDP, "exp"),
        P(FSDP, "exp"),
        P(FSDP, "exp"),
        P("exp", None, FSDP),
        P("exp", FSDP, None),
    )
    out_specs = (
        P(ALL, None),
        P(ALL, None),
        P(ALL, None),
        P(FSDP, "exp"),
        P(FSDP, "exp"),
        P(FSDP, "exp"),
        P(FSDP, "exp"),
        P(FSDP, "exp"),
        P(FSDP, "exp"),
        P("exp", None, FSDP),
        P("exp", FSDP, None),
    )

    def step(*args):
        return local(ring, *args)

    return jax.shard_map(step, mesh=fine, in_specs=in_specs, out_specs=out_specs, check_vma=False)
```

```python
import jax
import jax.numpy as jnp
from jax import lax
from jax.experimental import pallas as pl
from jax.experimental.pallas import tpu as pltpu
from jax.sharding import Mesh
from jax.sharding import PartitionSpec as P

H = 12
HD = 64
E = 8
TOPK = 2
SHORT = 256
GROUP = 1024
CAP = 288

F32 = jnp.float32
BF16 = jnp.bfloat16

eps_norm = 1e-06
tanh_gain = 0.7978845608028654
ALL = ("exp", "zi", "yi")
FSDP = ("zi", "yi")

PIECES = 4
STRIPS = 8
LANES = 128
OUT_LANES = 2 * LANES


def layer_norm(values):
    centered = values - jnp.mean(values, axis=-1, keepdims=True)
    inverse = lax.rsqrt(jnp.mean(centered * centered, axis=-1, keepdims=True) + eps_norm)
    return (centered * inverse, inverse)


def norm_back(grad, normed, inverse):
    return inverse * (
        grad
        - jnp.mean(grad, axis=-1, keepdims=True)
        - normed * jnp.mean(grad * normed, axis=-1, keepdims=True)
    )


def silu_slope(values):
    sigma = jax.nn.sigmoid(values)
    return sigma * (1.0 + values * (1.0 - sigma))


def dot(left, right, dims):
    return lax.dot_general(left, right, (dims, ((), ())), preferred_element_type=F32)


def mm(left, right):
    return dot(left, right, ((1,), (0,)))


def mm_rt(left, right):
    return dot(left, right, ((1,), (1,)))


def mm_lt(left, right):
    return dot(left, right, ((0,), (0,)))


def slot_table(expert_ids):
    flat = expert_ids.reshape(-1)
    onehot = (flat[:, None] == jnp.arange(E, dtype=jnp.int32)[None, :]).astype(jnp.int32)
    before = jnp.cumsum(onehot, axis=0) - onehot
    return jnp.sum(before * onehot, axis=1).reshape(expert_ids.shape)


def cost(flops, moved):
    return pl.CostEstimate(flops=flops // 64, transcendentals=0, bytes_accessed=moved // 64)


def fixed(shape):
    return pl.BlockSpec(shape, lambda *_: (0,) * len(shape), pipeline_mode=pl.Buffered(1))


LOG2E = 1.4426950408889634
SCORE = HD ** (-0.5)


def attend_kernel(kind_ref, query_ref, key_ref, value_ref, mixed_ref, logsum_ref):
    left = lax.broadcasted_iota(jnp.int32, (GROUP, 2 * HD), 1) < HD
    keys = key_ref[...]
    zero = jnp.zeros_like(keys)
    split_keys = (jnp.where(left, keys, zero), jnp.where(left, zero, keys))

    def rows_of(part, first, count):
        rows = pl.ds(part * SHORT, SHORT)
        query = query_ref[rows, :]
        value = value_ref[pl.ds(first, count), :]
        halves = []
        for half in range(2):
            scores = mm_rt(query, split_keys[half][first : first + count])
            peak = jnp.max(scores, axis=1, keepdims=True)
            weights = jnp.exp2((scores - peak) * (SCORE * LOG2E))
            total = jnp.sum(weights, axis=1, keepdims=True)
            halves.append(mm(weights.astype(BF16), value) / total)
            logsum = peak * (SCORE * LOG2E) + jnp.log2(total)
            logsum_ref[0, 0, half, rows] = jnp.transpose(
                jnp.broadcast_to(logsum, (SHORT, 2 * HD))
            )[0]
        mixed_ref[rows, :] = jnp.where(left[:SHORT], halves[0], halves[1]).astype(BF16)

    is_long = kind_ref[pl.program_id(0)] == 1

    @pl.when(is_long)
    def _():
        for part in range(GROUP // SHORT):
            rows_of(part, 0, GROUP)

    @pl.when(jnp.logical_not(is_long))
    def _():
        for part in range(GROUP // SHORT):
            rows_of(part, part * SHORT, SHORT)


def attend(triple, image_kind, first, count):
    groups = triple.shape[0] // GROUP
    pairs = H // 2

    def part(offset):
        return pl.BlockSpec((GROUP, 2 * HD), lambda g, i, kind: (g, offset + i))

    return pl.pallas_call(
        attend_kernel,
        out_shape=(
            jax.ShapeDtypeStruct((triple.shape[0], count * 2 * HD), BF16),
            jax.ShapeDtypeStruct((groups, count, 8, GROUP), F32),
        ),
        grid_spec=pltpu.PrefetchScalarGridSpec(
            num_scalar_prefetch=1,
            grid=(groups, count),
            in_specs=[part(first), part(pairs + first), part(2 * pairs + first)],
            out_specs=(
                part(0),
                pl.BlockSpec((1, 1, 8, GROUP), lambda g, i, kind: (g, i, 0, 0)),
            ),
        ),
        compiler_params=pltpu.CompilerParams(vmem_limit_bytes=32 << 20),
        cost_estimate=cost(32 * triple.shape[0] * GROUP * count * HD, 2 * triple.size),
        name="attend",
    )(image_kind, triple, triple, triple)


def attend_back_kernel(
    kind_ref,
    query_ref,
    key_ref,
    value_ref,
    mixed_ref,
    grad_ref,
    logsum_ref,
    grads_ref,
    key_sum,
    value_sum,
):
    left = lax.broadcasted_iota(jnp.int32, (GROUP, 2 * HD), 1) < HD

    def split(values):
        zero = jnp.zeros_like(values)
        return (jnp.where(left, values, zero), jnp.where(left, zero, values))

    split_query = split(query_ref[...])
    split_keys = split(key_ref[...])
    split_values = split(value_ref[...])
    split_grad = split(grad_ref[...])
    outer = jnp.transpose(mixed_ref[...].astype(F32) * grad_ref[...].astype(F32))
    inner = (
        jnp.sum(outer[:HD], axis=0, keepdims=True),
        jnp.sum(outer[HD:], axis=0, keepdims=True),
    )

    def rows_of(part, first, count, fresh):
        low, high = part * SHORT, (part + 1) * SHORT
        keys_at = pl.ds(first, count)
        query = query_ref[pl.ds(low, SHORT), :]
        grad = grad_ref[pl.ds(low, SHORT), :]
        key_part = value_part = query_part = None
        for half in range(2):
            keys = split_keys[half][first : first + count]
            scores = mm_rt(keys, query)
            logsum = logsum_ref[0, 0, half : half + 1, low:high]
            attention = jnp.exp2(scores * (SCORE * LOG2E) - logsum)
            moved = mm_rt(split_values[half][first : first + count], grad)
            grad_scores = (attention * (moved - inner[half][:, low:high])).astype(BF16)
            value_add = mm(attention.astype(BF16), split_grad[half][low:high])
            key_add = mm(grad_scores, split_query[half][low:high])
            query_add = mm_lt(grad_scores, keys)
            if half == 0:
                key_part, value_part, query_part = key_add, value_add, query_add
            else:
                key_part, value_part = key_part + key_add, value_part + value_add
                query_part = query_part + query_add
        grads_ref[0, pl.ds(low, SHORT), :] = (query_part * SCORE).astype(BF16)
        if fresh:
            key_sum[keys_at, :] = key_part
            value_sum[keys_at, :] = value_part
        else:
            key_sum[keys_at, :] += key_part
            value_sum[keys_at, :] += value_part

    is_long = kind_ref[pl.program_id(0)] == 1

    @pl.when(is_long)
    def _():
        for part in range(GROUP // SHORT):
            rows_of(part, 0, GROUP, part == 0)

    @pl.when(jnp.logical_not(is_long))
    def _():
        for part in range(GROUP // SHORT):
            rows_of(part, part * SHORT, SHORT, True)

    grads_ref[1, :, :] = (key_sum[...] * SCORE).astype(BF16)
    grads_ref[2, :, :] = value_sum[...].astype(BF16)


def attend_back(triple, attended, logsum, grad_attended, image_kind, first):
    groups, count = logsum.shape[:2]
    pairs = H // 2

    def part(offset):
        return pl.BlockSpec((GROUP, 2 * HD), lambda g, i, kind: (g, offset + i))

    return pl.pallas_call(
        attend_back_kernel,
        out_shape=jax.ShapeDtypeStruct((3, triple.shape[0], count * 2 * HD), BF16),
        grid_spec=pltpu.PrefetchScalarGridSpec(
            num_scalar_prefetch=1,
            grid=(groups, count),
            in_specs=[
                part(first),
                part(pairs + first),
                part(2 * pairs + first),
                part(0),
                part(first),
                pl.BlockSpec((1, 1, 8, GROUP), lambda g, i, kind: (g, i, 0, 0)),
            ],
            out_specs=pl.BlockSpec((3, GROUP, 2 * HD), lambda g, i, kind: (0, g, i)),
            scratch_shapes=[pltpu.VMEM((GROUP, 2 * HD), F32)] * 2,
        ),
        compiler_params=pltpu.CompilerParams(vmem_limit_bytes=32 << 20),
        cost_estimate=cost(80 * triple.shape[0] * GROUP * count * HD, 4 * triple.size),
        name="attend_back",
    )(image_kind, triple, triple, triple, attended, grad_attended, logsum)


def gelu_both(values):
    square = values * values
    side = tanh_gain * 0.044715 * square
    half = 0.5 + 0.5 * jnp.tanh(values * (tanh_gain + side))
    slope = half + 2.0 * values * (tanh_gain + 3.0 * side) * (half * (1.0 - half))
    return values * half, slope


def way(me, piece, strip):
    sx, other = (piece >> 1) ^ me[1], (piece & 1) ^ me[0]
    sy, k = (strip & 1) ^ me[2], (me[3] - (strip >> 1)) & 3
    return other, sx, sy, k


def on_side(other, own_ref, other_ref, action):
    @pl.when(other == 0)
    def _():
        action(own_ref)

    @pl.when(other == 1)
    def _():
        action(other_ref)


def normalize(values):
    mean = jnp.mean(values, axis=1, keepdims=True)
    centered = values - mean
    return centered * lax.rsqrt(jnp.mean(centered * centered, axis=1, keepdims=True) + eps_norm)


def triple_kernel(me, x_ref, shift_ref, scale_ref, q1a, q1b, q2a, q2b, in_ref, out_ref, weight_ref):
    rows, cols = q1a.shape[3], q1a.shape[4] - OUT_LANES

    @pl.when(pl.program_id(0) == 0)
    def _():
        for piece in range(PIECES):
            for strip in range(STRIPS):
                other, sx, sy, k = way(me, piece, strip)
                low, at = strip * 2 * rows, slice(piece * cols, (piece + 1) * cols)

                def first(ref):
                    weight_ref[low : low + rows, at] = ref[sx, sy, k, :, OUT_LANES:]

                def second(ref):
                    weight_ref[low + rows : low + 2 * rows, at] = ref[sy, sx, k, :, OUT_LANES:]

                on_side(other, q1a, q1b, first)
                on_side(other, q2a, q2b, second)

    normed = normalize(x_ref[...].astype(F32))
    attend_in = (normed * (1.0 + scale_ref[0]) + shift_ref[0]).astype(BF16)
    in_ref[...] = attend_in
    out_ref[...] = mm(attend_in, weight_ref[...]).astype(BF16)


def make_triple(me, patches, shift, scale, weights):
    tok_count, width = patches.shape
    hidden = PIECES * (weights[0].shape[4] - OUT_LANES)
    rows = pl.BlockSpec((SHORT, width), lambda i, me: (i, 0))
    each = pl.BlockSpec((1, 1, width), lambda i, me: (i, 0, 0))
    return pl.pallas_call(
        triple_kernel,
        out_shape=(
            jax.ShapeDtypeStruct((tok_count, width), BF16),
            jax.ShapeDtypeStruct((tok_count, hidden), BF16),
            jax.ShapeDtypeStruct((width, hidden), BF16),
        ),
        grid_spec=pltpu.PrefetchScalarGridSpec(
            num_scalar_prefetch=1,
            grid=(tok_count // SHORT,),
            in_specs=[rows, each, each] + [fixed(w.shape) for w in weights],
            out_specs=(
                rows,
                pl.BlockSpec((SHORT, hidden), lambda i, me: (i, 0)),
                fixed((width, hidden)),
            ),
        ),
        compiler_params=pltpu.CompilerParams(vmem_limit_bytes=40 << 20),
        cost_estimate=cost(2 * tok_count * width * hidden, 8 * tok_count * width),
        name="triple",
    )(me, patches, shift, scale, *weights)


def project_kernel(
    me,
    left_ref,
    right_ref,
    x_ref,
    gate_ref,
    shift_ref,
    scale_ref,
    q1a,
    q1b,
    q2a,
    q2b,
    projected_ref,
    residual_ref,
    branch_ref,
    logits_ref,
    weight_ref,
    router_ref,
):
    width = x_ref.shape[1]
    rows, cols, experts = q1a.shape[3], width // PIECES, E // PIECES

    @pl.when(pl.program_id(0) == 0)
    def _():
        router_ref[...] = jnp.zeros_like(router_ref)
        for piece in range(PIECES):
            for strip in range(STRIPS):
                other, sx, sy, k = way(me, piece, strip)

                def place(block, low):
                    weight_ref[low : low + rows, piece * cols : (piece + 1) * cols] = block[
                        :, :cols
                    ]
                    router_ref[
                        low : low + rows, piece * experts : (piece + 1) * experts
                    ] = block[:, cols : cols + experts]

                def first(ref):
                    place(ref[sx, sy, k], strip * 2 * rows)

                def second(ref):
                    place(ref[sy, sx, k], strip * 2 * rows + rows)

                on_side(other, q1a, q1b, first)
                on_side(other, q2a, q2b, second)

    split = left_ref.shape[1]
    projected = mm(left_ref[...], weight_ref[:split, :]) + mm(right_ref[...], weight_ref[split:, :])
    projected_ref[...] = projected
    residual = x_ref[...].astype(F32) + gate_ref[0] * projected
    residual_ref[...] = residual
    branch = (normalize(residual) * (1.0 + scale_ref[0]) + shift_ref[0]).astype(BF16)
    branch_ref[...] = branch
    logits_ref[...] = mm(branch, router_ref[...])


def make_branch(me, left, right, patches, gate, shift, scale, weights):
    tok_count, width = patches.shape
    rows = pl.BlockSpec((SHORT, width), lambda i, me: (i, 0))
    each = pl.BlockSpec((1, 1, width), lambda i, me: (i, 0, 0))
    outs = fixed(weights[0].shape[:4] + (OUT_LANES,))
    part = pl.BlockSpec((SHORT, width // 2), lambda i, me: (i, 0))
    return pl.pallas_call(
        project_kernel,
        out_shape=(
            jax.ShapeDtypeStruct((tok_count, width), F32),
            jax.ShapeDtypeStruct((tok_count, width), F32),
            jax.ShapeDtypeStruct((tok_count, width), BF16),
            jax.ShapeDtypeStruct((tok_count, LANES), F32),
            jax.ShapeDtypeStruct((width, width), BF16),
            jax.ShapeDtypeStruct((width, LANES), BF16),
        ),
        grid_spec=pltpu.PrefetchScalarGridSpec(
            num_scalar_prefetch=1,
            grid=(tok_count // SHORT,),
            in_specs=[part, part, rows, each, each, each, outs, outs, outs, outs],
            out_specs=(
                rows,
                rows,
                rows,
                pl.BlockSpec((SHORT, LANES), lambda i, me: (i, 0)),
                fixed((width, width)),
                fixed((width, LANES)),
            ),
        ),
        compiler_params=pltpu.CompilerParams(vmem_limit_bytes=32 << 20),
        cost_estimate=cost(2 * tok_count * width * width, 16 * tok_count * width),
        name="project",
    )(me, left, right, patches, gate, shift, scale, *weights)


def shared_kernel(
    me,
    x_ref,
    grad_ref,
    in_own,
    in_other,
    out_own,
    out_other,
    res_ref,
    x_grad_ref,
    weight_grad_ref,
    weight_in,
    weight_out,
    x_turned,
    grad_turned,
):
    step = pl.program_id(0)
    width = x_ref.shape[1]
    rows, half = width // STRIPS, width // 2
    halves = [slice(0, half), slice(half, width)]

    @pl.when(step == 0)
    def _():
        x_turned[...] = jnp.transpose(x_ref[...])
        grad_turned[...] = jnp.transpose(grad_ref[...])

    def take_in(ref):
        for sy in range(2):
            for z in range(4):
                low = (2 * z + (sy ^ me[2])) * rows
                weight_in[pl.ds(pl.multiple_of(low, 32), rows), :] = ref[0, sy, z]

    on_side((step & 1) ^ me[0], in_own, in_other, take_in)
    for other, ref in enumerate((out_own, out_other)):
        for sx in range(2):
            low = (((sx ^ me[1]) << 1) | (other ^ me[0])) * 2 * rows
            for sy in range(2):
                at = pl.ds(pl.multiple_of((sy ^ me[2]) * half, LANES), half)
                for part in range(2):
                    start = pl.multiple_of(low + part * rows, 32)
                    weight_out[pl.ds(start, rows), at] = ref[sy, sx, 0, :, halves[part]]

    act, slope = gelu_both(mm(x_ref[...], weight_in[...]))
    act = act.astype(BF16)
    grad_pre = (mm(grad_ref[...], weight_out[...]) * slope).astype(BF16)
    res = mm_rt(act, weight_out[...])
    x_grad = mm_rt(grad_pre, weight_in[...])

    @pl.when(step == 0)
    def _():
        res_ref[...] = res
        x_grad_ref[...] = x_grad

    @pl.when(step != 0)
    def _():
        res_ref[...] += res
        x_grad_ref[...] += x_grad

    in_grad = mm(x_turned[...], grad_pre).astype(BF16)
    out_grad = mm(grad_turned[...], act).astype(BF16)
    weight_grad_ref[step, :, :rows, :] = in_grad.reshape(STRIPS, rows, width)
    for piece in range(PIECES):
        for strip in range(2):
            for part in range(2):
                low = (2 * piece + part) * rows
                weight_grad_ref[piece, 2 * step + strip, rows:, halves[part]] = out_grad[
                    low : low + rows, halves[strip]
                ]


def shared_expert(me, x, grad, in_own, in_other, out_own, out_other):
    tok_count, width = x.shape
    rows = width // STRIPS
    whole = fixed((tok_count, width))
    block_in = pl.BlockSpec((1, 2, 4, rows, width), lambda j, me: ((j >> 1) ^ me[1], 0, 0, 0, 0))
    block_out = pl.BlockSpec((2, 2, 1, rows, width), lambda j, me: (0, 0, j, 0, 0))
    grads = jax.ShapeDtypeStruct((PIECES, STRIPS, 2 * rows, width), BF16)
    return pl.pallas_call(
        shared_kernel,
        out_shape=(jax.ShapeDtypeStruct((tok_count, width), F32),) * 2 + (grads,),
        grid_spec=pltpu.PrefetchScalarGridSpec(
            num_scalar_prefetch=1,
            grid=(PIECES,),
            in_specs=[whole, whole, block_in, block_in, block_out, block_out],
            out_specs=(whole, whole, fixed(grads.shape)),
            scratch_shapes=[pltpu.VMEM((width, width), BF16)] * 2
            + [pltpu.VMEM((width, tok_count), BF16)] * 2,
        ),
        compiler_params=pltpu.CompilerParams(vmem_limit_bytes=56 << 20),
        cost_estimate=cost(12 * tok_count * width * 4 * width, 16 * tok_count * width),
        name="shared_expert",
    )(me, x, grad, in_own, in_other, out_own, out_other)


def project_back_kernel(
    left_ref,
    right_ref,
    grad_ref,
    branch_ref,
    logits_ref,
    weight_ref,
    back_ref,
    out_grad_ref,
    router_ref,
):
    split = left_ref.shape[1]
    back_ref[...] = mm_rt(grad_ref[...], weight_ref[...]).astype(BF16)
    out_grad_ref[:split, :] = mm_lt(left_ref[...], grad_ref[...]).astype(BF16)
    out_grad_ref[split:, :] = mm_lt(right_ref[...], grad_ref[...]).astype(BF16)
    router_ref[...] = mm_lt(branch_ref[...], logits_ref[...]).astype(BF16)


def project_back(left, right, grad, branch, grad_logits, weight):
    tok_count, width = grad.shape
    part = fixed((tok_count, width // 2))
    whole = fixed((tok_count, width))
    return pl.pallas_call(
        project_back_kernel,
        out_shape=(
            jax.ShapeDtypeStruct((tok_count, width), BF16),
            jax.ShapeDtypeStruct((width, width), BF16),
            jax.ShapeDtypeStruct((width, LANES), BF16),
        ),
        grid=(1,),
        in_specs=[part, part, whole, whole, fixed((tok_count, LANES)), fixed((width, width))],
        out_specs=(whole, fixed((width, width)), fixed((width, LANES))),
        compiler_params=pltpu.CompilerParams(vmem_limit_bytes=32 << 20),
        cost_estimate=cost(4 * tok_count * width * width, 8 * tok_count * width),
        name="project_back",
    )(left, right, grad, branch, grad_logits, weight)


def triple_back_kernel(
    me,
    left_ref,
    right_ref,
    in_ref,
    weight_ref,
    out_grad_ref,
    router_ref,
    back_ref,
    q1a,
    q1b,
    q2a,
    q2b,
    in_turned,
    weight_grad,
):
    step = pl.program_id(0)
    rows, cols = q1a.shape[3], q1a.shape[4] - OUT_LANES
    width = in_ref.shape[1]
    outs, experts = width // PIECES, E // PIECES

    @pl.when(step == 0)
    def _():
        in_turned[...] = jnp.transpose(in_ref[...])

    grad = jnp.concatenate((left_ref[0], right_ref[0]), axis=1)
    at = pl.ds(pl.multiple_of(step * width, LANES), width)
    weight_grad[:, at] = mm(in_turned[...], grad).astype(BF16)
    back = mm_rt(grad, weight_ref[...])

    @pl.when(step == 0)
    def _():
        back_ref[...] = back

    @pl.when(step != 0)
    def _():
        back_ref[...] += back

    @pl.when(step == 2)
    def _():
        for piece in range(PIECES):
            for strip in range(STRIPS):
                other, sx, sy, k = way(me, piece, strip)

                def place(ref, where, low):
                    at = slice(low, low + rows)
                    ref[where + (slice(None), slice(0, outs))] = out_grad_ref[
                        at, piece * outs : (piece + 1) * outs
                    ]
                    ref[where + (slice(None), slice(outs, outs + experts))] = router_ref[
                        at, piece * experts : (piece + 1) * experts
                    ]
                    ref[where + (slice(None), slice(outs + experts, OUT_LANES))] = jnp.zeros(
                        (rows, OUT_LANES - outs - experts), BF16
                    )
                    ref[where + (slice(None), slice(OUT_LANES, None))] = weight_grad[
                        at, piece * cols : (piece + 1) * cols
                    ]

                def first(ref):
                    place(ref, (sx, sy, k), strip * 2 * rows)

                def second(ref):
                    place(ref, (sy, sx, k), strip * 2 * rows + rows)

                on_side(other, q1a, q1b, first)
                on_side(other, q2a, q2b, second)


def triple_back(me, left, right, attend_in, weight, out_grad, router_grad):
    tok_count, width = attend_in.shape
    hidden = weight.shape[1]
    block = (2, 2, 4, width // STRIPS // 2, OUT_LANES + hidden // PIECES)
    block = jax.ShapeDtypeStruct(block, BF16)
    return pl.pallas_call(
        triple_back_kernel,
        out_shape=(jax.ShapeDtypeStruct((tok_count, width), F32),) + (block,) * 4,
        grid_spec=pltpu.PrefetchScalarGridSpec(
            num_scalar_prefetch=1,
            grid=(3,),
            in_specs=[
                pl.BlockSpec((1, tok_count, width // 2), lambda p, me: (p, 0, 0)),
                pl.BlockSpec((1, tok_count, width // 2), lambda p, me: (p, 0, 0)),
                fixed((tok_count, width)),
                pl.BlockSpec((width, width), lambda p, me: (0, p)),
                fixed((width, width)),
                fixed((width, LANES)),
            ],
            out_specs=(fixed((tok_count, width)),) + (fixed(block.shape),) * 4,
            scratch_shapes=[
                pltpu.VMEM((width, tok_count), BF16),
                pltpu.VMEM((width, hidden), BF16),
            ],
        ),
        compiler_params=pltpu.CompilerParams(vmem_limit_bytes=40 << 20),
        cost_estimate=cost(4 * tok_count * width * hidden, 12 * tok_count * width),
        name="triple_back",
    )(me, left, right, attend_in, weight, out_grad, router_grad)


ROW_TILE = 576


def expert_kernel(x_ref, weights_ref, res_ref, act_ref, slope_ref):
    x = x_ref[...]
    width = x_ref.shape[1]
    total = None
    for part in range(weights_ref.shape[0]):
        at = pl.ds(part * width, width)
        act, slope = gelu_both(mm(x, weights_ref[part, :width, :]))
        act = act.astype(BF16)
        act_ref[:, at] = act
        slope_ref[:, at] = slope.astype(BF16)
        res = mm(act, weights_ref[part, width:, :])
        total = res if total is None else total + res
    res_ref[...] = total.astype(BF16)


def expert_back_kernel(grad_ref, slope_ref, weights_ref, rows_ref, pre_ref):
    grad = grad_ref[...]
    width = grad_ref.shape[1]
    total = None
    for part in range(weights_ref.shape[0]):
        at = pl.ds(part * width, width)
        grad_pre = mm_rt(grad, weights_ref[part, width:, :]) * slope_ref[:, at].astype(F32)
        grad_pre = grad_pre.astype(BF16)
        pre_ref[:, at] = grad_pre
        rows = mm_rt(grad_pre, weights_ref[part, :width, :])
        total = rows if total is None else total + rows
    rows_ref[...] = total.astype(BF16)


def expert_call(kernel, name, rows_in, wide_in, weights, n_wide):
    rows, width = rows_in.shape
    hidden = weights.shape[0] * width
    narrow = pl.BlockSpec((ROW_TILE, width), lambda i: (i, 0))
    wide = pl.BlockSpec((ROW_TILE, hidden), lambda i: (i, 0))
    return pl.pallas_call(
        kernel,
        out_shape=(jax.ShapeDtypeStruct((rows, width), BF16),)
        + (jax.ShapeDtypeStruct((rows, hidden), BF16),) * n_wide,
        grid=(rows // ROW_TILE,),
        in_specs=[narrow] + [wide] * len(wide_in) + [fixed(weights.shape)],
        out_specs=(narrow,) + (wide,) * n_wide,
        compiler_params=pltpu.CompilerParams(vmem_limit_bytes=48 << 20),
        cost_estimate=cost(8 * rows * hidden * width, 2 * rows * hidden * (1 + n_wide)),
        name=name,
    )(rows_in, *wide_in, weights)


def expert_grads_kernel(part, x_ref, pre_ref, act_ref, grad_ref, out_ref, up_sum, down_sum):
    step, width = pl.program_id(0), x_ref.shape[1]
    up = mm_lt(x_ref[...], pre_ref[...])
    down = mm_lt(act_ref[...], grad_ref[...])

    @pl.when(step == 0)
    def _():
        up_sum[...] = up
        down_sum[...] = down

    @pl.when(step != 0)
    def _():
        up_sum[...] += up
        down_sum[...] += down

    @pl.when(step == pl.num_programs(0) - 1)
    def _():
        out_ref[:width, :] = up_sum[...].astype(BF16)
        out_ref[width:, :] = down_sum[...].astype(BF16)


def expert_grads(x, grad_pre, act, grad, part):
    rows, width = x.shape
    narrow = pl.BlockSpec((ROW_TILE, width), lambda i, part: (i, 0))
    wide = pl.BlockSpec((ROW_TILE, width), lambda i, part: (i, part[0]))
    return pl.pallas_call(
        expert_grads_kernel,
        out_shape=jax.ShapeDtypeStruct((2 * width, width), BF16),
        grid_spec=pltpu.PrefetchScalarGridSpec(
            num_scalar_prefetch=1,
            grid=(rows // ROW_TILE,),
            in_specs=[narrow, wide, wide, narrow],
            out_specs=fixed((2 * width, width)),
            scratch_shapes=[pltpu.VMEM((width, width), F32)] * 2,
        ),
        compiler_params=pltpu.CompilerParams(vmem_limit_bytes=40 << 20),
        cost_estimate=cost(4 * rows * width * width, 8 * rows * width),
        name="expert_grads",
    )(part, x, grad_pre, act, grad)


def by_way(blocks, y_outer, turns=True):
    rows, cols = blocks.shape[2:]
    blocks = blocks.reshape(2, 2, 4, 2, rows, cols)
    if turns:
        blocks = blocks[:, :, jnp.array([0, 3, 2, 1])]
    blocks = blocks.transpose((1, 3, 0, 2, 4, 5) if y_outer else (1, 0, 3, 2, 4, 5))
    return blocks[0], blocks[1]


def by_place(own, other, y_outer):
    blocks = jnp.stack((own, other))
    blocks = blocks.transpose((2, 0, 3, 1, 4, 5) if y_outer else (1, 0, 3, 2, 4, 5))
    rows, cols = blocks.shape[4:]
    return blocks[:, :, jnp.array([0, 3, 2, 1])].reshape(PIECES, STRIPS, rows, cols)


def to_blocks(whole):
    rows, cols = whole.shape
    return whole.reshape(STRIPS, rows // STRIPS, PIECES, cols // PIECES).transpose(2, 0, 1, 3)


def to_whole(blocks):
    rows, cols = blocks.shape[2:]
    return blocks.transpose(1, 2, 0, 3).reshape(STRIPS * rows, PIECES * cols)


def turn(block):
    block = block.T
    half = block.shape[0] // 2
    return jnp.concatenate((block[:half], block[half:]), axis=1)


def turn_back(block):
    half = block.shape[1] // 2
    return jnp.concatenate((block[:, :half], block[:, half:]), axis=0).T


def shared_bundle(up, down):
    down = to_blocks(down).swapaxes(2, 3)
    half = down.shape[2] // 2
    return jnp.concatenate(
        (to_blocks(up), jnp.concatenate((down[:, :, :half], down[:, :, half:]), axis=3)), axis=2
    )


def shared_unbundle(grads):
    rows, half = grads.shape[2] // 2, grads.shape[3] // 2
    down = grads[:, :, rows:]
    down = jnp.concatenate((down[..., :half], down[..., half:]), axis=2).swapaxes(2, 3)
    return to_whole(grads[:, :, :rows]), to_whole(down)


class Ring:
    def __init__(self, mesh):
        self.n_exp = mesh.shape["exp"]
        self.n_ring = mesh.shape["zi"]
        self.n_pair = mesh.shape["yi"]
        self.direct = (self.n_exp, self.n_ring, self.n_pair) == (PIECES, 4, 2)

    def step(self, value, by=1):
        n = self.n_ring
        return lax.ppermute(value, "zi", [(i, (i + by) % n) for i in range(n)])

    def over_y(self, value):
        return lax.ppermute(value, "yi", [(0, 1), (1, 0)])

    def over_x(self, value):
        return lax.ppermute(value, "exp", [(i, i ^ 2) for i in range(4)])

    def over_core(self, value):
        return lax.ppermute(value, "exp", [(i, i ^ 1) for i in range(4)])

    def near(self, block):
        return jnp.stack([block] + [self.step(block, k) for k in range(1, 4)])

    def second(self, held, y_outer):
        return jnp.stack((held, (self.over_x if y_outer else self.over_y)(held)))

    def third(self, held, y_outer):
        return jnp.stack((held, (self.over_y if y_outer else self.over_x)(held)))

    def outer(self, value, y_outer):
        return (self.over_y if y_outer else self.over_x)(value)

    def inner(self, value, y_outer):
        return (self.over_x if y_outer else self.over_y)(value)

    def line(self, held):
        return tuple(self.step(held[k], -k) for k in range(1, 4))


def add_both(keep, got):
    return add(keep[0], got[0]), add(keep[1], got[1])


def add_line(held, got):
    total = held.astype(F32)
    for part in got:
        total = total + part.astype(F32)
    return total


def add(left, right):
    return (left.astype(F32) + right.astype(F32)).astype(BF16)


def tie(*values):
    return lax.optimization_barrier(values)


def after(value, *others):
    return lax.optimization_barrier((value,) + others)[0]


def picked_experts(ring, y, expert_in, expert_out, first):
    own_in = jnp.where(y == 0, expert_in[0], expert_in[1])
    give_in = jnp.where(y == 0, expert_in[1], expert_in[0])
    own_out = jnp.where(y == 0, expert_out[0], expert_out[1])
    give_out = jnp.where(y == 0, expert_out[1], expert_out[0])
    got_in, got_out = after(ring.over_y(give_in), first), after(ring.over_y(give_out), first)
    ups = jnp.concatenate((own_in, got_in), axis=1)
    downs = jnp.concatenate((own_out, got_out), axis=0)
    return jnp.concatenate((ups, downs), axis=0)


def local(
    ring,
    patches,
    cond_embed,
    image_kind,
    expert_ids,
    out_grad,
    modulate_weight,
    attend_weight,
    output_weight,
    router_weight,
    shared_in,
    shared_out,
    expert_in,
    expert_out,
):
    tok_count, width = patches.shape
    blocks = tok_count // SHORT
    n_exp, n_ring, n_pair = ring.n_exp, ring.n_ring, ring.n_pair
    n_fsdp = n_ring * n_pair
    n_all = n_exp * n_fsdp
    e, z, y = (lax.axis_index(name) for name in ("exp", "zi", "yi"))
    mod_rows, mod_cols = modulate_weight.shape
    half = width // STRIPS // 2
    if ring.direct:
        me = jnp.stack((e & 1, e >> 1, y, z)).astype(jnp.int32)
    else:
        me = jnp.zeros((4,), jnp.int32)

    if ring.direct:
        spare = OUT_LANES - output_weight.shape[1] - router_weight.shape[1]
        block = jnp.concatenate(
            (
                output_weight,
                router_weight,
                jnp.zeros((router_weight.shape[0], spare), BF16),
                attend_weight,
            ),
            axis=1,
        )
        held = ring.near(block)

    cond_float = cond_embed.astype(F32)
    cond_act = jax.nn.silu(cond_float).astype(BF16)
    cond_send = cond_act.reshape(blocks, n_fsdp, mod_rows).transpose(1, 0, 2)
    cond_send = jnp.broadcast_to(cond_send[None], (n_exp, n_fsdp, blocks, mod_rows))
    cond_all = lax.all_to_all(
        cond_send.reshape(n_all, blocks, mod_rows), ALL, 0, 0, tiled=True
    ).reshape(n_all * blocks, mod_rows)
    if ring.direct:
        cond_all = after(cond_all, held)
    mod_part = mm(cond_all, modulate_weight).reshape(n_all, blocks, mod_cols)
    mod_part = lax.all_to_all(mod_part, ALL, 0, 0, tiled=True)
    modulation = jnp.sum(mod_part.reshape(n_exp, n_fsdp, blocks, mod_cols), axis=1)
    if ring.direct:
        held = after(held, modulation)
    modulation = modulation.transpose(1, 0, 2).reshape(blocks, 1, 6, width)

    if ring.direct:
        expert_block = picked_experts(ring, y, expert_in, expert_out, modulation)
        held = after(held, expert_block)
        held_1 = ring.second(held[:, :half], False)
        held_2 = ring.second(held[:, half:], True)
        bundle = jnp.concatenate((shared_in, turn(shared_out)), axis=0)
        shared_line = lax.all_gather(bundle, "zi", axis=0, tiled=False)
        expert_weights = lax.all_gather(after(expert_block, shared_line), "zi", axis=0)
        held_1 = ring.third(held_1, False)
        held_2 = ring.third(held_2, True)
        dense_weights = (held_1, ring.over_core(held_1), held_2, ring.over_core(held_2))
    else:
        wholes = [
            lax.all_gather(
                lax.all_gather(w, FSDP, axis=0, tiled=True), "exp", axis=1, tiled=True
            )
            for w in (attend_weight, output_weight, router_weight, shared_in, shared_out)
        ]
        attend_all, output_all, router_all = map(to_blocks, wholes[:3])
        up_all, down_all = wholes[3:]
        spare = jnp.zeros((PIECES, STRIPS, 2 * half, OUT_LANES - (width + E) // PIECES), BF16)
        dense_all = jnp.concatenate((output_all, router_all, spare, attend_all), axis=3)
        dense_weights = by_way(dense_all[:, :, :half], False)
        dense_weights += by_way(dense_all[:, :, half:], True)
        shared_all = shared_bundle(up_all, down_all)
        in_weights = by_way(shared_all[:, :, : 2 * half], False, False)
        out_weights = by_way(shared_all[:, :, 2 * half :], True, False)
        up_all = lax.all_gather(expert_in[0], FSDP, axis=1, tiled=True)
        down_all = lax.all_gather(expert_out[0], FSDP, axis=0, tiled=True)
        expert_weights = jnp.stack(
            [
                jnp.concatenate((up_all[:, at : at + width], down_all[at : at + width]), axis=0)
                for at in range(0, up_all.shape[1], width)
            ]
        )

    shift_first = modulation[:, :, 0]
    scale_first = modulation[:, :, 1]
    gate_first = modulation[:, :, 2]
    shift_second = modulation[:, :, 3]
    scale_second = modulation[:, :, 4]
    gate_second = modulation[:, :, 5]
    attend_in, triple, triple_weight = make_triple(
        me, patches, shift_first, scale_first, dense_weights
    )
    pairs = H // 4
    attended_1, logsum_1 = attend(triple, image_kind, 0, pairs)
    triple_2 = after(triple, attended_1)
    if ring.direct:
        shared_line = after(shared_line, triple)
        in_held = ring.second(shared_line[:, : 2 * half], False)
        out_held = ring.second(shared_line[:, 2 * half :], True)
        triple_2, in_held, out_held = tie(triple_2, in_held, out_held)
        in_held, out_held = ring.third(in_held, False), ring.third(out_held, True)
    attended_2, logsum_2 = attend(triple_2, image_kind, pairs, pairs)
    projected, residual, branch_in, logits, output_weight_all, router_all = make_branch(
        me,
        attended_1,
        attended_2,
        patches,
        gate_first,
        shift_second,
        scale_second,
        dense_weights,
    )
    choose = expert_ids[:, :, None] == jnp.arange(E, dtype=jnp.int32)[None, None, :]
    choose = choose.astype(F32)
    gates = jax.nn.softmax(jnp.sum(choose * logits[:, None, :E], axis=-1), axis=-1)

    grad_out = out_grad.astype(F32).reshape(blocks, SHORT, width)
    grad_branch = (gate_second * grad_out).astype(BF16).reshape(tok_count, width)
    grad_branch_wide = grad_branch.astype(F32)

    slots = slot_table(expert_ids)
    target = expert_ids * CAP + slots
    row_of = jnp.arange(E * CAP, dtype=jnp.int32)[:, None]
    pick0 = (row_of == target[None, :, 0]).astype(BF16)
    pick1 = (row_of == target[None, :, 1]).astype(BF16)
    send_rows = mm(pick0 + pick1, branch_in).astype(BF16).reshape(E, CAP, width)
    grad_picked = (gates[:, :, None] * grad_branch_wide[:, None, :]).astype(BF16)
    grad_picked = after(grad_picked, send_rows)
    if ring.direct:
        grad_picked, in_held, out_held = tie(grad_picked, in_held, out_held)
        in_weights = (in_held, ring.over_core(in_held))
        out_weights = (out_held, ring.over_core(out_held))
    grad_send = mm(pick0, grad_picked[:, 0]) + mm(pick1, grad_picked[:, 1])
    grad_send = grad_send.astype(BF16).reshape(E, CAP, width)
    shared_x = after(branch_in, send_rows, grad_send)

    def exchange(rows):
        return lax.all_to_all(rows, ("exp", "yi"), 0, 0, tiled=True)

    received = exchange(send_rows)

    shared_res, grad_branch_in, shared_grads = shared_expert(
        me, shared_x, grad_branch, *in_weights, *out_weights
    )

    received = after(received, shared_res)
    received = received.reshape(-1, width)
    grad_received = exchange(after(grad_send, received))
    expert_res, expert_act, expert_slope = expert_call(
        expert_kernel, "experts", received, (), expert_weights, 2
    )
    grad_received = grad_received.reshape(-1, width)
    expert_res = after(expert_res, grad_received)
    returned = exchange(expert_res.reshape(E, CAP, width))
    grad_rows, grad_pre = expert_call(
        expert_back_kernel, "experts_back", grad_received, (expert_slope,), expert_weights, 1
    )
    returned = returned.reshape(-1, width)
    grad_rows = after(grad_rows, returned)
    grad_returned = exchange(grad_rows.reshape(E, CAP, width)).reshape(-1, width)

    n_parts = expert_weights.shape[0]
    first = z - 1 if ring.direct else jnp.zeros((), jnp.int32)

    def grads_of(turn_at, act):
        part = ((first - turn_at) % n_parts if ring.direct else first + turn_at).reshape(1)
        return expert_grads(received, grad_pre, act, grad_received, part)

    grad_blocks = [grads_of(0, expert_act)]
    act = after(expert_act, returned)
    for part in range(1, n_parts):
        grad_blocks.append(grads_of(part, act))
        act = after(act, grad_blocks[-1])
    returned = after(returned, *grad_blocks)
    if ring.direct:
        moved = ring.step(grad_blocks[0])
        grad_returned, moved = tie(grad_returned, add(moved, grad_blocks[1]))
        moved = ring.step(moved)

    picked0 = mm_lt(pick0, returned)
    picked1 = mm_lt(pick1, returned)
    mixture = gates[:, 0:1] * picked0 + gates[:, 1:2] * picked1
    branch_out = (shared_res + mixture).reshape(blocks, SHORT, width)
    projected = projected.reshape(blocks, SHORT, width)
    residual = residual.reshape(blocks, SHORT, width)
    normed_second, inverse_second = layer_norm(residual)
    block_out = (residual + gate_second * branch_out).reshape(tok_count, width).astype(BF16)
    grad_gate_second = jnp.sum(grad_out * branch_out, axis=1)
    grad_gates = jnp.stack(
        (
            jnp.sum(grad_branch_wide * picked0, axis=-1),
            jnp.sum(grad_branch_wide * picked1, axis=-1),
        ),
        axis=1,
    )
    grad_chosen = gates * (grad_gates - jnp.sum(gates * grad_gates, axis=-1, keepdims=True))
    grad_logits = jnp.sum(choose * grad_chosen[:, :, None], axis=1).astype(BF16)
    grad_logits = jnp.concatenate((grad_logits, jnp.zeros((tok_count, LANES - E), BF16)), axis=1)
    grad_branch_in = (
        grad_branch_in
        + mm_lt(pick0 + pick1, grad_returned)
        + mm_rt(grad_logits, router_all)
    )
    grad_norm_in = grad_branch_in.reshape(blocks, SHORT, width)
    grad_shift_second = jnp.sum(grad_norm_in, axis=1)
    grad_scale_second = jnp.sum(grad_norm_in * normed_second, axis=1)
    grad_residual = grad_out + norm_back(
        grad_norm_in * (1.0 + scale_second), normed_second, inverse_second
    )
    grad_gate_first = jnp.sum(grad_residual * projected, axis=1)
    grad_projected = (gate_first * grad_residual).astype(BF16).reshape(tok_count, width)
    grad_attended, out_grad_all, router_grad_all = project_back(
        attended_1, attended_2, grad_projected, branch_in, grad_logits, output_weight_all
    )
    grad_triple_1 = attend_back(triple, attended_1, logsum_1, grad_attended, image_kind, 0)
    grad_attended_2 = after(grad_attended, grad_triple_1)
    if ring.direct:
        grad_attended_2, moved = tie(grad_attended_2, add(moved, grad_blocks[2]))
        moved = ring.step(moved)
    grad_triple_2 = attend_back(triple, attended_2, logsum_2, grad_attended_2, image_kind, pairs)
    grad_attend_in, *dense_grads = triple_back(
        me,
        grad_triple_1,
        grad_triple_2,
        attend_in,
        triple_weight,
        out_grad_all,
        router_grad_all,
    )
    if ring.direct:
        own_1, give_1, own_2, give_2 = dense_grads
        moved = moved.astype(F32) + grad_blocks[3].astype(F32)
        moved, give_1, give_2 = tie(moved, give_1, give_2)
        up_sum, down_sum = moved[:width], moved[width:]
        split = width // 2
        got_up = ring.over_y(up_sum[:, split:].astype(BF16)).astype(F32)
        got_down = ring.over_y(down_sum[split:].astype(BF16)).astype(F32)
        sum_1, give_1 = add_both(own_1, ring.over_core(give_1))
        sum_2, give_2 = add_both(own_2, ring.over_core(give_2))
        got_1, got_2 = ring.outer(give_1, False), ring.outer(give_2, True)
    inputs = patches.astype(F32).reshape(blocks, SHORT, width)
    normed_first, inverse_first = layer_norm(inputs)
    grad_attend_in = grad_attend_in.reshape(blocks, SHORT, width)
    grad_shift_first = jnp.sum(grad_attend_in, axis=1)
    grad_scale_first = jnp.sum(grad_attend_in * normed_first, axis=1)
    patches_grad = grad_residual + norm_back(
        grad_attend_in * (1.0 + scale_first), normed_first, inverse_first
    )
    patches_grad = patches_grad.reshape(tok_count, width)

    grad_modulation = jnp.stack(
        (
            grad_shift_first,
            grad_scale_first,
            grad_gate_first,
            grad_shift_second,
            grad_scale_second,
            grad_gate_second,
        ),
        axis=1,
    )
    grad_modulation = grad_modulation.reshape(blocks, n_exp, mod_cols).astype(BF16)
    mod_send = jnp.broadcast_to(
        grad_modulation.transpose(1, 0, 2)[:, None], (n_exp, n_fsdp, blocks, mod_cols)
    )
    if ring.direct:
        mod_send = after(mod_send, sum_1, sum_2)
    mod_all = lax.all_to_all(
        mod_send.reshape(n_all, blocks, mod_cols), ALL, 0, 0, tiled=True
    ).reshape(n_all * blocks, mod_cols)
    modulate_grad = mm_lt(cond_all, mod_all)
    cond_part = mm_rt(mod_all, modulate_weight).reshape(n_all, blocks, mod_rows)
    if ring.direct:
        sum_1, give_1 = add_both(sum_1, got_1)
        sum_2, give_2 = add_both(sum_2, got_2)
        sum_1 = add(sum_1, ring.inner(give_1, False))
        sum_2 = add(sum_2, ring.inner(give_2, True))
        cond_part = after(cond_part, sum_1, sum_2)
    cond_part = lax.all_to_all(cond_part, ALL, 0, 0, tiled=True)
    cond_grad = jnp.sum(cond_part.reshape(n_exp, n_fsdp, blocks, mod_rows), axis=0)
    cond_grad = cond_grad.transpose(1, 0, 2).reshape(blocks, width) * silu_slope(cond_float)

    if ring.direct:
        cols, experts = width // PIECES, E // PIECES
        summed = jnp.concatenate(
            (add_line(sum_1[0], ring.line(sum_1)), add_line(sum_2[0], ring.line(sum_2))), axis=0
        )
        output_grad, router_grad = summed[:, :cols], summed[:, cols : cols + experts]
        attend_grad = summed[:, OUT_LANES:]
        summed = lax.psum_scatter(
            shared_grads.reshape((n_all,) + bundle.shape), ALL, scatter_dimension=0
        ).astype(F32)
        shared_in_grad = summed[: 2 * half]
        shared_out_grad = turn_back(summed[2 * half :])
        own_up, own_down = up_sum[:, :split], down_sum[:split]
        expert_in_grad = jnp.stack(
            (jnp.where(y == 0, own_up, got_up), jnp.where(y == 0, got_up, own_up))
        )
        expert_out_grad = jnp.stack(
            (jnp.where(y == 0, own_down, got_down), jnp.where(y == 0, got_down, own_down))
        )
    else:

        def spread(grad):
            part = lax.psum_scatter(grad, "exp", scatter_dimension=1, tiled=True)
            return lax.psum_scatter(part, FSDP, scatter_dimension=0, tiled=True).astype(F32)

        dense_all = jnp.concatenate(
            (by_place(*dense_grads[:2], False), by_place(*dense_grads[2:], True)), axis=2
        )
        cols, experts = width // PIECES, E // PIECES
        attend_grad = spread(to_whole(dense_all[..., OUT_LANES:]))
        output_grad = spread(to_whole(dense_all[..., :cols]))
        router_grad = spread(to_whole(dense_all[..., cols : cols + experts]))
        shared_in_grad, shared_out_grad = map(spread, shared_unbundle(shared_grads))
        up_sum = jnp.concatenate([b[:width] for b in grad_blocks], axis=1)
        down_sum = jnp.concatenate([b[width:] for b in grad_blocks], axis=0)
        expert_in_grad = lax.psum_scatter(up_sum, FSDP, scatter_dimension=1, tiled=True)
        expert_out_grad = lax.psum_scatter(down_sum, FSDP, scatter_dimension=0, tiled=True)
        expert_in_grad = expert_in_grad.astype(F32)[None]
        expert_out_grad = expert_out_grad.astype(F32)[None]
    return (
        block_out,
        patches_grad,
        cond_grad,
        modulate_grad,
        attend_grad,
        output_grad,
        router_grad,
        shared_in_grad,
        shared_out_grad,
        expert_in_grad,
        expert_out_grad,
    )


def solution(mesh):
    n_exp, n_fsdp = mesh.shape["exp"], mesh.shape["fsdp"]
    n_pair = E // n_exp
    if n_pair not in (1, 2) or n_fsdp % n_pair:
        raise ValueError("unsupported mesh")
    fine = Mesh(mesh.devices.reshape(n_exp, n_fsdp // n_pair, n_pair), ALL)
    ring = Ring(fine)
    in_specs = (
        P(ALL, None),
        P(ALL, None),
        P(ALL),
        P(ALL, None),
        P(ALL, None),
        P(FSDP, "exp"),
        P(FSDP, "exp"),
        P(FSDP, "exp"),
        P(FSDP, "exp"),
        P(FSDP, "exp"),
        P(FSDP, "exp"),
        P("exp", None, FSDP),
        P("exp", FSDP, None),
    )
    out_specs = (
        P(ALL, None),
        P(ALL, None),
        P(ALL, None),
        P(FSDP, "exp"),
        P(FSDP, "exp"),
        P(FSDP, "exp"),
        P(FSDP, "exp"),
        P(FSDP, "exp"),
        P(FSDP, "exp"),
        P("exp", None, FSDP),
        P("exp", FSDP, None),
    )

    def step(*args):
        return local(ring, *args)

    return jax.shard_map(step, mesh=fine, in_specs=in_specs, out_specs=out_specs, check_vma=False)
```

```python
import jax
import jax.numpy as jnp
from jax import lax
from jax.experimental import pallas as pl
from jax.experimental.pallas import tpu as pltpu
from jax.sharding import Mesh
from jax.sharding import PartitionSpec as P

H = 12
HD = 64
E = 8
TOPK = 2
SHORT = 256
GROUP = 1024
CAP = 288

F32 = jnp.float32
BF16 = jnp.bfloat16

eps_norm = 1e-06
tanh_gain = 0.7978845608028654
ALL = ("exp", "zi", "yi")
FSDP = ("zi", "yi")

PIECES = 4
STRIPS = 8
LANES = 128
OUT_LANES = 2 * LANES


def layer_norm(values):
    centered = values - jnp.mean(values, axis=-1, keepdims=True)
    inverse = lax.rsqrt(jnp.mean(centered * centered, axis=-1, keepdims=True) + eps_norm)
    return (centered * inverse, inverse)


def norm_back(grad, normed, inverse):
    return inverse * (
        grad
        - jnp.mean(grad, axis=-1, keepdims=True)
        - normed * jnp.mean(grad * normed, axis=-1, keepdims=True)
    )


def silu_slope(values):
    sigma = jax.nn.sigmoid(values)
    return sigma * (1.0 + values * (1.0 - sigma))


def dot(left, right, dims):
    return lax.dot_general(left, right, (dims, ((), ())), preferred_element_type=F32)


def mm(left, right):
    return dot(left, right, ((1,), (0,)))


def mm_rt(left, right):
    return dot(left, right, ((1,), (1,)))


def mm_lt(left, right):
    return dot(left, right, ((0,), (0,)))


def slot_table(expert_ids):
    flat = expert_ids.reshape(-1)
    onehot = (flat[:, None] == jnp.arange(E, dtype=jnp.int32)[None, :]).astype(jnp.int32)
    before = jnp.cumsum(onehot, axis=0) - onehot
    return jnp.sum(before * onehot, axis=1).reshape(expert_ids.shape)


def cost(flops, moved, share=64):
    return pl.CostEstimate(flops=flops // share, transcendentals=0, bytes_accessed=moved // share)


def fixed(shape):
    return pl.BlockSpec(shape, lambda *_: (0,) * len(shape), pipeline_mode=pl.Buffered(1))


LOG2E = 1.4426950408889634
SCORE = HD ** (-0.5)


def attend_kernel(kind_ref, query_ref, key_ref, value_ref, mixed_ref, logsum_ref):
    left = lax.broadcasted_iota(jnp.int32, (GROUP, 2 * HD), 1) < HD
    keys = key_ref[...]
    zero = jnp.zeros_like(keys)
    split_keys = (jnp.where(left, keys, zero), jnp.where(left, zero, keys))

    def rows_of(part, first, count):
        rows = pl.ds(part * SHORT, SHORT)
        query = query_ref[rows, :]
        value = value_ref[pl.ds(first, count), :]
        halves = []
        for half in range(2):
            scores = mm_rt(query, split_keys[half][first : first + count])
            peak = jnp.max(scores, axis=1, keepdims=True)
            weights = jnp.exp2((scores - peak) * (SCORE * LOG2E))
            total = jnp.sum(weights, axis=1, keepdims=True)
            halves.append(mm(weights.astype(BF16), value) / total)
            logsum = peak * (SCORE * LOG2E) + jnp.log2(total)
            logsum_ref[0, 0, half, rows] = jnp.transpose(
                jnp.broadcast_to(logsum, (SHORT, 2 * HD))
            )[0]
        mixed_ref[rows, :] = jnp.where(left[:SHORT], halves[0], halves[1]).astype(BF16)

    is_long = kind_ref[pl.program_id(0)] == 1

    @pl.when(is_long)
    def _():
        for part in range(GROUP // SHORT):
            rows_of(part, 0, GROUP)

    @pl.when(jnp.logical_not(is_long))
    def _():
        for part in range(GROUP // SHORT):
            rows_of(part, part * SHORT, SHORT)


def attend(triple, image_kind, first, count):
    groups = triple.shape[0] // GROUP
    pairs = H // 2

    def part(offset):
        return pl.BlockSpec((GROUP, 2 * HD), lambda g, i, kind: (g, offset + i))

    return pl.pallas_call(
        attend_kernel,
        out_shape=(
            jax.ShapeDtypeStruct((triple.shape[0], count * 2 * HD), BF16),
            jax.ShapeDtypeStruct((groups, count, 8, GROUP), F32),
        ),
        grid_spec=pltpu.PrefetchScalarGridSpec(
            num_scalar_prefetch=1,
            grid=(groups, count),
            in_specs=[part(first), part(pairs + first), part(2 * pairs + first)],
            out_specs=(
                part(0),
                pl.BlockSpec((1, 1, 8, GROUP), lambda g, i, kind: (g, i, 0, 0)),
            ),
        ),
        compiler_params=pltpu.CompilerParams(vmem_limit_bytes=32 << 20),
        cost_estimate=cost(32 * triple.shape[0] * GROUP * count * HD, 2 * triple.size),
        name="attend",
    )(image_kind, triple, triple, triple)


def attend_back_kernel(
    kind_ref,
    query_ref,
    key_ref,
    value_ref,
    mixed_ref,
    grad_ref,
    logsum_ref,
    grads_ref,
    key_sum,
    value_sum,
):
    left = lax.broadcasted_iota(jnp.int32, (GROUP, 2 * HD), 1) < HD

    def split(values):
        zero = jnp.zeros_like(values)
        return (jnp.where(left, values, zero), jnp.where(left, zero, values))

    split_query = split(query_ref[...])
    split_keys = split(key_ref[...])
    split_values = split(value_ref[...])
    split_grad = split(grad_ref[...])
    outer = jnp.transpose(mixed_ref[...].astype(F32) * grad_ref[...].astype(F32))
    inner = (
        jnp.sum(outer[:HD], axis=0, keepdims=True),
        jnp.sum(outer[HD:], axis=0, keepdims=True),
    )

    def rows_of(part, first, count, fresh):
        low, high = part * SHORT, (part + 1) * SHORT
        keys_at = pl.ds(first, count)
        query = query_ref[pl.ds(low, SHORT), :]
        grad = grad_ref[pl.ds(low, SHORT), :]
        key_part = value_part = query_part = None
        for half in range(2):
            keys = split_keys[half][first : first + count]
            scores = mm_rt(keys, query)
            logsum = logsum_ref[0, 0, half : half + 1, low:high]
            attention = jnp.exp2(scores * (SCORE * LOG2E) - logsum)
            moved = mm_rt(split_values[half][first : first + count], grad)
            grad_scores = (attention * (moved - inner[half][:, low:high])).astype(BF16)
            value_add = mm(attention.astype(BF16), split_grad[half][low:high])
            key_add = mm(grad_scores, split_query[half][low:high])
            query_add = mm_lt(grad_scores, keys)
            if half == 0:
                key_part, value_part, query_part = key_add, value_add, query_add
            else:
                key_part, value_part = key_part + key_add, value_part + value_add
                query_part = query_part + query_add
        grads_ref[0, pl.ds(low, SHORT), :] = (query_part * SCORE).astype(BF16)
        if fresh:
            key_sum[keys_at, :] = key_part
            value_sum[keys_at, :] = value_part
        else:
            key_sum[keys_at, :] += key_part
            value_sum[keys_at, :] += value_part

    is_long = kind_ref[pl.program_id(0)] == 1

    @pl.when(is_long)
    def _():
        for part in range(GROUP // SHORT):
            rows_of(part, 0, GROUP, part == 0)

    @pl.when(jnp.logical_not(is_long))
    def _():
        for part in range(GROUP // SHORT):
            rows_of(part, part * SHORT, SHORT, True)

    grads_ref[1, :, :] = (key_sum[...] * SCORE).astype(BF16)
    grads_ref[2, :, :] = value_sum[...].astype(BF16)


def attend_back(triple, attended, logsum, grad_attended, image_kind, first):
    groups, count = logsum.shape[:2]
    pairs = H // 2

    def part(offset):
        return pl.BlockSpec((GROUP, 2 * HD), lambda g, i, kind: (g, offset + i))

    return pl.pallas_call(
        attend_back_kernel,
        out_shape=jax.ShapeDtypeStruct((3, triple.shape[0], count * 2 * HD), BF16),
        grid_spec=pltpu.PrefetchScalarGridSpec(
            num_scalar_prefetch=1,
            grid=(groups, count),
            in_specs=[
                part(first),
                part(pairs + first),
                part(2 * pairs + first),
                part(0),
                part(first),
                pl.BlockSpec((1, 1, 8, GROUP), lambda g, i, kind: (g, i, 0, 0)),
            ],
            out_specs=pl.BlockSpec((3, GROUP, 2 * HD), lambda g, i, kind: (0, g, i)),
            scratch_shapes=[pltpu.VMEM((GROUP, 2 * HD), F32)] * 2,
        ),
        compiler_params=pltpu.CompilerParams(vmem_limit_bytes=32 << 20),
        cost_estimate=cost(80 * triple.shape[0] * GROUP * count * HD, 4 * triple.size),
        name="attend_back",
    )(image_kind, triple, triple, triple, attended, grad_attended, logsum)


def gelu_both(values):
    square = values * values
    side = tanh_gain * 0.044715 * square
    half = 0.5 + 0.5 * jnp.tanh(values * (tanh_gain + side))
    slope = half + 2.0 * values * (tanh_gain + 3.0 * side) * (half * (1.0 - half))
    return values * half, slope


def way(me, piece, strip):
    sx, other = (piece >> 1) ^ me[1], (piece & 1) ^ me[0]
    sy, k = (strip & 1) ^ me[2], (me[3] - (strip >> 1)) & 3
    return other, sx, sy, k


def on_side(other, own_ref, other_ref, action):
    @pl.when(other == 0)
    def _():
        action(own_ref)

    @pl.when(other == 1)
    def _():
        action(other_ref)


def normalize(values):
    mean = jnp.mean(values, axis=1, keepdims=True)
    centered = values - mean
    return centered * lax.rsqrt(jnp.mean(centered * centered, axis=1, keepdims=True) + eps_norm)


def triple_kernel(me, x_ref, shift_ref, scale_ref, q1a, q1b, q2a, q2b, in_ref, out_ref, weight_ref):
    rows, cols = q1a.shape[3], q1a.shape[4] - OUT_LANES

    @pl.when(pl.program_id(0) == 0)
    def _():
        for piece in range(PIECES):
            for strip in range(STRIPS):
                other, sx, sy, k = way(me, piece, strip)
                low, at = strip * 2 * rows, slice(piece * cols, (piece + 1) * cols)

                def first(ref):
                    weight_ref[low : low + rows, at] = ref[sx, sy, k, :, OUT_LANES:]

                def second(ref):
                    weight_ref[low + rows : low + 2 * rows, at] = ref[sy, sx, k, :, OUT_LANES:]

                on_side(other, q1a, q1b, first)
                on_side(other, q2a, q2b, second)

    normed = normalize(x_ref[...].astype(F32))
    attend_in = (normed * (1.0 + scale_ref[0]) + shift_ref[0]).astype(BF16)
    in_ref[...] = attend_in
    out_ref[...] = mm(attend_in, weight_ref[...]).astype(BF16)


def make_triple(me, patches, shift, scale, weights):
    tok_count, width = patches.shape
    hidden = PIECES * (weights[0].shape[4] - OUT_LANES)
    rows = pl.BlockSpec((SHORT, width), lambda i, me: (i, 0))
    each = pl.BlockSpec((1, 1, width), lambda i, me: (i, 0, 0))
    return pl.pallas_call(
        triple_kernel,
        out_shape=(
            jax.ShapeDtypeStruct((tok_count, width), BF16),
            jax.ShapeDtypeStruct((tok_count, hidden), BF16),
            jax.ShapeDtypeStruct((width, hidden), BF16),
        ),
        grid_spec=pltpu.PrefetchScalarGridSpec(
            num_scalar_prefetch=1,
            grid=(tok_count // SHORT,),
            in_specs=[rows, each, each] + [fixed(w.shape) for w in weights],
            out_specs=(
                rows,
                pl.BlockSpec((SHORT, hidden), lambda i, me: (i, 0)),
                fixed((width, hidden)),
            ),
        ),
        compiler_params=pltpu.CompilerParams(vmem_limit_bytes=40 << 20),
        cost_estimate=cost(2 * tok_count * width * hidden, 8 * tok_count * width),
        name="triple",
    )(me, patches, shift, scale, *weights)


def project_kernel(
    me,
    left_ref,
    right_ref,
    x_ref,
    gate_ref,
    shift_ref,
    scale_ref,
    q1a,
    q1b,
    q2a,
    q2b,
    projected_ref,
    residual_ref,
    branch_ref,
    logits_ref,
    weight_ref,
    router_ref,
):
    width = x_ref.shape[1]
    rows, cols, experts = q1a.shape[3], width // PIECES, E // PIECES

    @pl.when(pl.program_id(0) == 0)
    def _():
        router_ref[...] = jnp.zeros_like(router_ref)
        for piece in range(PIECES):
            for strip in range(STRIPS):
                other, sx, sy, k = way(me, piece, strip)

                def place(block, low):
                    weight_ref[low : low + rows, piece * cols : (piece + 1) * cols] = block[
                        :, :cols
                    ]
                    router_ref[
                        low : low + rows, piece * experts : (piece + 1) * experts
                    ] = block[:, cols : cols + experts]

                def first(ref):
                    place(ref[sx, sy, k], strip * 2 * rows)

                def second(ref):
                    place(ref[sy, sx, k], strip * 2 * rows + rows)

                on_side(other, q1a, q1b, first)
                on_side(other, q2a, q2b, second)

    split = left_ref.shape[1]
    projected = mm(left_ref[...], weight_ref[:split, :]) + mm(right_ref[...], weight_ref[split:, :])
    projected_ref[...] = projected
    residual = x_ref[...].astype(F32) + gate_ref[0] * projected
    residual_ref[...] = residual
    branch = (normalize(residual) * (1.0 + scale_ref[0]) + shift_ref[0]).astype(BF16)
    branch_ref[...] = branch
    logits_ref[...] = mm(branch, router_ref[...])


def make_branch(me, left, right, patches, gate, shift, scale, weights):
    tok_count, width = patches.shape
    rows = pl.BlockSpec((SHORT, width), lambda i, me: (i, 0))
    each = pl.BlockSpec((1, 1, width), lambda i, me: (i, 0, 0))
    outs = fixed(weights[0].shape[:4] + (OUT_LANES,))
    part = pl.BlockSpec((SHORT, width // 2), lambda i, me: (i, 0))
    return pl.pallas_call(
        project_kernel,
        out_shape=(
            jax.ShapeDtypeStruct((tok_count, width), F32),
            jax.ShapeDtypeStruct((tok_count, width), F32),
            jax.ShapeDtypeStruct((tok_count, width), BF16),
            jax.ShapeDtypeStruct((tok_count, LANES), F32),
            jax.ShapeDtypeStruct((width, width), BF16),
            jax.ShapeDtypeStruct((width, LANES), BF16),
        ),
        grid_spec=pltpu.PrefetchScalarGridSpec(
            num_scalar_prefetch=1,
            grid=(tok_count // SHORT,),
            in_specs=[part, part, rows, each, each, each, outs, outs, outs, outs],
            out_specs=(
                rows,
                rows,
                rows,
                pl.BlockSpec((SHORT, LANES), lambda i, me: (i, 0)),
                fixed((width, width)),
                fixed((width, LANES)),
            ),
        ),
        compiler_params=pltpu.CompilerParams(vmem_limit_bytes=32 << 20),
        cost_estimate=cost(2 * tok_count * width * width, 16 * tok_count * width),
        name="project",
    )(me, left, right, patches, gate, shift, scale, *weights)


def shared_kernel(
    me,
    x_ref,
    grad_ref,
    in_own,
    in_other,
    out_own,
    out_other,
    res_ref,
    x_grad_ref,
    weight_grad_ref,
    weight_in,
    weight_out,
    x_turned,
    grad_turned,
):
    step = pl.program_id(0)
    width = x_ref.shape[1]
    rows, half = width // STRIPS, width // 2
    halves = [slice(0, half), slice(half, width)]

    @pl.when(step == 0)
    def _():
        x_turned[...] = jnp.transpose(x_ref[...])
        grad_turned[...] = jnp.transpose(grad_ref[...])

    def take_in(ref):
        for sy in range(2):
            for z in range(4):
                low = (2 * z + (sy ^ me[2])) * rows
                weight_in[pl.ds(pl.multiple_of(low, 32), rows), :] = ref[0, sy, z]

    on_side((step & 1) ^ me[0], in_own, in_other, take_in)
    for other, ref in enumerate((out_own, out_other)):
        for sx in range(2):
            low = (((sx ^ me[1]) << 1) | (other ^ me[0])) * 2 * rows
            for sy in range(2):
                at = pl.ds(pl.multiple_of((sy ^ me[2]) * half, LANES), half)
                for part in range(2):
                    start = pl.multiple_of(low + part * rows, 32)
                    weight_out[pl.ds(start, rows), at] = ref[sy, sx, 0, :, halves[part]]

    act, slope = gelu_both(mm(x_ref[...], weight_in[...]))
    act = act.astype(BF16)
    grad_pre = (mm(grad_ref[...], weight_out[...]) * slope).astype(BF16)
    res = mm_rt(act, weight_out[...])
    x_grad = mm_rt(grad_pre, weight_in[...])

    @pl.when(step == 0)
    def _():
        res_ref[...] = res
        x_grad_ref[...] = x_grad

    @pl.when(step != 0)
    def _():
        res_ref[...] += res
        x_grad_ref[...] += x_grad

    in_grad = mm(x_turned[...], grad_pre).astype(BF16)
    out_grad = mm(grad_turned[...], act).astype(BF16)
    weight_grad_ref[step, :, :rows, :] = in_grad.reshape(STRIPS, rows, width)
    for piece in range(PIECES):
        for strip in range(2):
            for part in range(2):
                low = (2 * piece + part) * rows
                weight_grad_ref[piece, 2 * step + strip, rows:, halves[part]] = out_grad[
                    low : low + rows, halves[strip]
                ]


def shared_expert(me, x, grad, in_own, in_other, out_own, out_other):
    tok_count, width = x.shape
    rows = width // STRIPS
    whole = fixed((tok_count, width))
    block_in = pl.BlockSpec((1, 2, 4, rows, width), lambda j, me: ((j >> 1) ^ me[1], 0, 0, 0, 0))
    block_out = pl.BlockSpec((2, 2, 1, rows, width), lambda j, me: (0, 0, j, 0, 0))
    grads = jax.ShapeDtypeStruct((PIECES, STRIPS, 2 * rows, width), BF16)
    return pl.pallas_call(
        shared_kernel,
        out_shape=(jax.ShapeDtypeStruct((tok_count, width), F32),) * 2 + (grads,),
        grid_spec=pltpu.PrefetchScalarGridSpec(
            num_scalar_prefetch=1,
            grid=(PIECES,),
            in_specs=[whole, whole, block_in, block_in, block_out, block_out],
            out_specs=(whole, whole, fixed(grads.shape)),
            scratch_shapes=[pltpu.VMEM((width, width), BF16)] * 2
            + [pltpu.VMEM((width, tok_count), BF16)] * 2,
        ),
        compiler_params=pltpu.CompilerParams(vmem_limit_bytes=56 << 20),
        cost_estimate=cost(12 * tok_count * width * 4 * width, 16 * tok_count * width, 1),
        name="shared_expert",
    )(me, x, grad, in_own, in_other, out_own, out_other)


def project_back_kernel(
    left_ref,
    right_ref,
    grad_ref,
    branch_ref,
    logits_ref,
    weight_ref,
    back_ref,
    out_grad_ref,
    router_ref,
):
    split = left_ref.shape[1]
    back_ref[...] = mm_rt(grad_ref[...], weight_ref[...]).astype(BF16)
    out_grad_ref[:split, :] = mm_lt(left_ref[...], grad_ref[...]).astype(BF16)
    out_grad_ref[split:, :] = mm_lt(right_ref[...], grad_ref[...]).astype(BF16)
    router_ref[...] = mm_lt(branch_ref[...], logits_ref[...]).astype(BF16)


def project_back(left, right, grad, branch, grad_logits, weight):
    tok_count, width = grad.shape
    part = fixed((tok_count, width // 2))
    whole = fixed((tok_count, width))
    return pl.pallas_call(
        project_back_kernel,
        out_shape=(
            jax.ShapeDtypeStruct((tok_count, width), BF16),
            jax.ShapeDtypeStruct((width, width), BF16),
            jax.ShapeDtypeStruct((width, LANES), BF16),
        ),
        grid=(1,),
        in_specs=[part, part, whole, whole, fixed((tok_count, LANES)), fixed((width, width))],
        out_specs=(whole, fixed((width, width)), fixed((width, LANES))),
        compiler_params=pltpu.CompilerParams(vmem_limit_bytes=32 << 20),
        cost_estimate=cost(4 * tok_count * width * width, 8 * tok_count * width),
        name="project_back",
    )(left, right, grad, branch, grad_logits, weight)


def triple_back_kernel(
    me,
    left_ref,
    right_ref,
    in_ref,
    weight_ref,
    out_grad_ref,
    router_ref,
    back_ref,
    q1a,
    q1b,
    q2a,
    q2b,
    in_turned,
    weight_grad,
):
    step = pl.program_id(0)
    rows, cols = q1a.shape[3], q1a.shape[4] - OUT_LANES
    width = in_ref.shape[1]
    outs, experts = width // PIECES, E // PIECES

    @pl.when(step == 0)
    def _():
        in_turned[...] = jnp.transpose(in_ref[...])

    grad = jnp.concatenate((left_ref[0], right_ref[0]), axis=1)
    at = pl.ds(pl.multiple_of(step * width, LANES), width)
    weight_grad[:, at] = mm(in_turned[...], grad).astype(BF16)
    back = mm_rt(grad, weight_ref[...])

    @pl.when(step == 0)
    def _():
        back_ref[...] = back

    @pl.when(step != 0)
    def _():
        back_ref[...] += back

    @pl.when(step == 2)
    def _():
        for piece in range(PIECES):
            for strip in range(STRIPS):
                other, sx, sy, k = way(me, piece, strip)

                def place(ref, where, low):
                    at = slice(low, low + rows)
                    ref[where + (slice(None), slice(0, outs))] = out_grad_ref[
                        at, piece * outs : (piece + 1) * outs
                    ]
                    ref[where + (slice(None), slice(outs, outs + experts))] = router_ref[
                        at, piece * experts : (piece + 1) * experts
                    ]
                    ref[where + (slice(None), slice(outs + experts, OUT_LANES))] = jnp.zeros(
                        (rows, OUT_LANES - outs - experts), BF16
                    )
                    ref[where + (slice(None), slice(OUT_LANES, None))] = weight_grad[
                        at, piece * cols : (piece + 1) * cols
                    ]

                def first(ref):
                    place(ref, (sx, sy, k), strip * 2 * rows)

                def second(ref):
                    place(ref, (sy, sx, k), strip * 2 * rows + rows)

                on_side(other, q1a, q1b, first)
                on_side(other, q2a, q2b, second)


def triple_back(me, left, right, attend_in, weight, out_grad, router_grad):
    tok_count, width = attend_in.shape
    hidden = weight.shape[1]
    block = (2, 2, 4, width // STRIPS // 2, OUT_LANES + hidden // PIECES)
    block = jax.ShapeDtypeStruct(block, BF16)
    return pl.pallas_call(
        triple_back_kernel,
        out_shape=(jax.ShapeDtypeStruct((tok_count, width), F32),) + (block,) * 4,
        grid_spec=pltpu.PrefetchScalarGridSpec(
            num_scalar_prefetch=1,
            grid=(3,),
            in_specs=[
                pl.BlockSpec((1, tok_count, width // 2), lambda p, me: (p, 0, 0)),
                pl.BlockSpec((1, tok_count, width // 2), lambda p, me: (p, 0, 0)),
                fixed((tok_count, width)),
                pl.BlockSpec((width, width), lambda p, me: (0, p)),
                fixed((width, width)),
                fixed((width, LANES)),
            ],
            out_specs=(fixed((tok_count, width)),) + (fixed(block.shape),) * 4,
            scratch_shapes=[
                pltpu.VMEM((width, tok_count), BF16),
                pltpu.VMEM((width, hidden), BF16),
            ],
        ),
        compiler_params=pltpu.CompilerParams(vmem_limit_bytes=40 << 20),
        cost_estimate=cost(4 * tok_count * width * hidden, 12 * tok_count * width),
        name="triple_back",
    )(me, left, right, attend_in, weight, out_grad, router_grad)


ROW_TILE = 576


def expert_kernel(x_ref, weights_ref, res_ref, act_ref, slope_ref):
    x = x_ref[...]
    width = x_ref.shape[1]
    total = None
    for part in range(weights_ref.shape[0]):
        at = pl.ds(part * width, width)
        act, slope = gelu_both(mm(x, weights_ref[part, :width, :]))
        act = act.astype(BF16)
        act_ref[:, at] = act
        slope_ref[:, at] = slope.astype(BF16)
        res = mm(act, weights_ref[part, width:, :])
        total = res if total is None else total + res
    res_ref[...] = total.astype(BF16)


def expert_back_kernel(grad_ref, slope_ref, weights_ref, rows_ref, pre_ref):
    grad = grad_ref[...]
    width = grad_ref.shape[1]
    total = None
    for part in range(weights_ref.shape[0]):
        at = pl.ds(part * width, width)
        grad_pre = mm_rt(grad, weights_ref[part, width:, :]) * slope_ref[:, at].astype(F32)
        grad_pre = grad_pre.astype(BF16)
        pre_ref[:, at] = grad_pre
        rows = mm_rt(grad_pre, weights_ref[part, :width, :])
        total = rows if total is None else total + rows
    rows_ref[...] = total.astype(BF16)


def expert_call(kernel, name, rows_in, wide_in, weights, n_wide):
    rows, width = rows_in.shape
    hidden = weights.shape[0] * width
    narrow = pl.BlockSpec((ROW_TILE, width), lambda i: (i, 0))
    wide = pl.BlockSpec((ROW_TILE, hidden), lambda i: (i, 0))
    return pl.pallas_call(
        kernel,
        out_shape=(jax.ShapeDtypeStruct((rows, width), BF16),)
        + (jax.ShapeDtypeStruct((rows, hidden), BF16),) * n_wide,
        grid=(rows // ROW_TILE,),
        in_specs=[narrow] + [wide] * len(wide_in) + [fixed(weights.shape)],
        out_specs=(narrow,) + (wide,) * n_wide,
        compiler_params=pltpu.CompilerParams(vmem_limit_bytes=48 << 20),
        cost_estimate=cost(8 * rows * hidden * width, 2 * rows * hidden * (1 + n_wide)),
        name=name,
    )(rows_in, *wide_in, weights)


def expert_grads_kernel(part, x_ref, pre_ref, act_ref, grad_ref, out_ref):
    step, cols = pl.program_id(0), x_ref.shape[1]
    up = mm_lt(x_ref[...], pre_ref[...]).astype(BF16)
    down = mm_lt(act_ref[...], grad_ref[...]).astype(BF16)
    out_ref[0, step] = up[:, :cols]
    out_ref[1, step] = up[:, cols:]
    out_ref[step, 2] = down[:, :cols]
    out_ref[step, 3] = down[:, cols:]


def expert_grads(x, grad_pre, act, grad, part):
    rows, width = x.shape
    cols = width // 2
    out = jax.ShapeDtypeStruct((2, 4, cols, cols), BF16)
    return pl.pallas_call(
        expert_grads_kernel,
        out_shape=out,
        grid_spec=pltpu.PrefetchScalarGridSpec(
            num_scalar_prefetch=1,
            grid=(2,),
            in_specs=[
                pl.BlockSpec((rows, cols), lambda i, part: (0, i)),
                pl.BlockSpec((rows, width), lambda i, part: (0, part[0])),
                pl.BlockSpec((rows, cols), lambda i, part: (0, part[0] * 2 + i)),
                fixed((rows, width)),
            ],
            out_specs=fixed(out.shape),
        ),
        compiler_params=pltpu.CompilerParams(vmem_limit_bytes=40 << 20),
        cost_estimate=cost(4 * rows * width * width, 8 * rows * width),
        name="expert_grads",
    )(part, x, grad_pre, act, grad)


def up_of(half):
    return jnp.concatenate((half[0], half[1]), axis=0)


def down_of(half):
    return jnp.concatenate((half[2], half[3]), axis=1)


def by_way(blocks, y_outer, turns=True):
    rows, cols = blocks.shape[2:]
    blocks = blocks.reshape(2, 2, 4, 2, rows, cols)
    if turns:
        blocks = blocks[:, :, jnp.array([0, 3, 2, 1])]
    blocks = blocks.transpose((1, 3, 0, 2, 4, 5) if y_outer else (1, 0, 3, 2, 4, 5))
    return blocks[0], blocks[1]


def by_place(own, other, y_outer):
    blocks = jnp.stack((own, other))
    blocks = blocks.transpose((2, 0, 3, 1, 4, 5) if y_outer else (1, 0, 3, 2, 4, 5))
    rows, cols = blocks.shape[4:]
    return blocks[:, :, jnp.array([0, 3, 2, 1])].reshape(PIECES, STRIPS, rows, cols)


def to_blocks(whole):
    rows, cols = whole.shape
    return whole.reshape(STRIPS, rows // STRIPS, PIECES, cols // PIECES).transpose(2, 0, 1, 3)


def to_whole(blocks):
    rows, cols = blocks.shape[2:]
    return blocks.transpose(1, 2, 0, 3).reshape(STRIPS * rows, PIECES * cols)


def turn(block):
    block = block.T
    half = block.shape[0] // 2
    return jnp.concatenate((block[:half], block[half:]), axis=1)


def turn_back(block):
    half = block.shape[1] // 2
    return jnp.concatenate((block[:, :half], block[:, half:]), axis=0).T


def shared_bundle(up, down):
    down = to_blocks(down).swapaxes(2, 3)
    half = down.shape[2] // 2
    return jnp.concatenate(
        (to_blocks(up), jnp.concatenate((down[:, :, :half], down[:, :, half:]), axis=3)), axis=2
    )


def shared_unbundle(grads):
    rows, half = grads.shape[2] // 2, grads.shape[3] // 2
    down = grads[:, :, rows:]
    down = jnp.concatenate((down[..., :half], down[..., half:]), axis=2).swapaxes(2, 3)
    return to_whole(grads[:, :, :rows]), to_whole(down)


class Ring:
    def __init__(self, mesh):
        self.n_exp = mesh.shape["exp"]
        self.n_ring = mesh.shape["zi"]
        self.n_pair = mesh.shape["yi"]
        self.direct = (self.n_exp, self.n_ring, self.n_pair) == (PIECES, 4, 2)

    def step(self, value, by=1):
        n = self.n_ring
        return lax.ppermute(value, "zi", [(i, (i + by) % n) for i in range(n)])

    def step_aside(self, value):
        n = 2 * self.n_ring
        return lax.ppermute(value, FSDP, [(i, (i + 2) % n ^ 1) for i in range(n)])

    def over_y(self, value):
        return lax.ppermute(value, "yi", [(0, 1), (1, 0)])

    def over_x(self, value):
        return lax.ppermute(value, "exp", [(i, i ^ 2) for i in range(4)])

    def over_core(self, value):
        return lax.ppermute(value, "exp", [(i, i ^ 1) for i in range(4)])

    def near(self, block):
        return jnp.stack([block] + [self.step(block, k) for k in range(1, 4)])

    def second(self, held, y_outer):
        return jnp.stack((held, (self.over_x if y_outer else self.over_y)(held)))

    def third(self, held, y_outer):
        return jnp.stack((held, (self.over_y if y_outer else self.over_x)(held)))

    def outer(self, value, y_outer):
        return (self.over_y if y_outer else self.over_x)(value)

    def inner(self, value, y_outer):
        return (self.over_x if y_outer else self.over_y)(value)

    def line(self, held):
        return tuple(self.step(held[k], -k) for k in range(1, 4))


def add_both(keep, got):
    return add(keep[0], got[0]), add(keep[1], got[1])


def add_line(held, got):
    total = held.astype(F32)
    for part in got:
        total = total + part.astype(F32)
    return total


def add(left, right):
    return (left.astype(F32) + right.astype(F32)).astype(BF16)


def tie(*values):
    return lax.optimization_barrier(values)


def after(value, *others):
    return lax.optimization_barrier((value,) + others)[0]


def local(
    ring,
    patches,
    cond_embed,
    image_kind,
    expert_ids,
    out_grad,
    modulate_weight,
    attend_weight,
    output_weight,
    router_weight,
    shared_in,
    shared_out,
    expert_in,
    expert_out,
):
    tok_count, width = patches.shape
    blocks = tok_count // SHORT
    n_exp, n_ring, n_pair = ring.n_exp, ring.n_ring, ring.n_pair
    n_fsdp = n_ring * n_pair
    n_all = n_exp * n_fsdp
    e, z, y = (lax.axis_index(name) for name in ("exp", "zi", "yi"))
    mod_rows, mod_cols = modulate_weight.shape
    half = width // STRIPS // 2
    if ring.direct:
        me = jnp.stack((e & 1, e >> 1, y, z)).astype(jnp.int32)
    else:
        me = jnp.zeros((4,), jnp.int32)

    if ring.direct:
        spare = OUT_LANES - output_weight.shape[1] - router_weight.shape[1]
        block = jnp.concatenate(
            (
                output_weight,
                router_weight,
                jnp.zeros((router_weight.shape[0], spare), BF16),
                attend_weight,
            ),
            axis=1,
        )
        held = ring.near(block)

    cond_float = cond_embed.astype(F32)
    cond_act = jax.nn.silu(cond_float).astype(BF16)
    cond_send = cond_act.reshape(blocks, n_fsdp, mod_rows).transpose(1, 0, 2)
    cond_send = jnp.broadcast_to(cond_send[None], (n_exp, n_fsdp, blocks, mod_rows))
    cond_all = lax.all_to_all(
        cond_send.reshape(n_all, blocks, mod_rows), ALL, 0, 0, tiled=True
    ).reshape(n_all * blocks, mod_rows)
    if ring.direct:
        own_in = jnp.where(y == 0, expert_in[0], expert_in[1])
        got_in = ring.over_y(jnp.where(y == 0, expert_in[1], expert_in[0]))
        cond_all = after(cond_all, held, got_in)
    mod_part = mm(cond_all, modulate_weight).astype(BF16).reshape(n_all, blocks, mod_cols)
    mod_part = lax.all_to_all(mod_part, ALL, 0, 0, tiled=True)
    mod_part = mod_part.reshape(n_exp, n_fsdp, blocks, mod_cols)
    modulation = jnp.sum(mod_part.astype(F32), axis=1)
    if ring.direct:
        held = after(held, modulation)
    modulation = modulation.transpose(1, 0, 2).reshape(blocks, 1, 6, width)

    if ring.direct:
        own_out = jnp.where(y == 0, expert_out[0], expert_out[1])
        got_out = ring.over_y(jnp.where(y == 0, expert_out[1], expert_out[0]))
        got_out = after(got_out, modulation)
        expert_block = jnp.concatenate(
            (
                jnp.concatenate((own_in, got_in), axis=1),
                jnp.concatenate((own_out, got_out), axis=0),
            ),
            axis=0,
        )
        held = after(held, expert_block)
        held_1 = ring.second(held[:, :half], False)
        held_2 = ring.second(held[:, half:], True)
        bundle = jnp.concatenate((shared_in, turn(shared_out)), axis=0)
        shared_line = lax.all_gather(bundle, "zi", axis=0, tiled=False)
        expert_weights = lax.all_gather(after(expert_block, shared_line), "zi", axis=0)
        held_1 = ring.third(held_1, False)
        held_2 = ring.third(held_2, True)
        dense_weights = (held_1, ring.over_core(held_1), held_2, ring.over_core(held_2))
    else:
        wholes = [
            lax.all_gather(
                lax.all_gather(w, FSDP, axis=0, tiled=True), "exp", axis=1, tiled=True
            )
            for w in (attend_weight, output_weight, router_weight, shared_in, shared_out)
        ]
        attend_all, output_all, router_all = map(to_blocks, wholes[:3])
        up_all, down_all = wholes[3:]
        spare = jnp.zeros((PIECES, STRIPS, 2 * half, OUT_LANES - (width + E) // PIECES), BF16)
        dense_all = jnp.concatenate((output_all, router_all, spare, attend_all), axis=3)
        dense_weights = by_way(dense_all[:, :, :half], False)
        dense_weights += by_way(dense_all[:, :, half:], True)
        shared_all = shared_bundle(up_all, down_all)
        in_weights = by_way(shared_all[:, :, : 2 * half], False, False)
        out_weights = by_way(shared_all[:, :, 2 * half :], True, False)
        up_all = lax.all_gather(expert_in[0], FSDP, axis=1, tiled=True)
        down_all = lax.all_gather(expert_out[0], FSDP, axis=0, tiled=True)
        expert_weights = jnp.stack(
            [
                jnp.concatenate((up_all[:, at : at + width], down_all[at : at + width]), axis=0)
                for at in range(0, up_all.shape[1], width)
            ]
        )

    shift_first = modulation[:, :, 0]
    scale_first = modulation[:, :, 1]
    gate_first = modulation[:, :, 2]
    shift_second = modulation[:, :, 3]
    scale_second = modulation[:, :, 4]
    gate_second = modulation[:, :, 5]
    attend_in, triple, triple_weight = make_triple(
        me, patches, shift_first, scale_first, dense_weights
    )
    pairs = H // 4
    attended_1, logsum_1 = attend(triple, image_kind, 0, pairs)
    triple_2 = after(triple, attended_1)
    if ring.direct:
        shared_line = after(shared_line, triple)
        in_held = ring.second(shared_line[:, : 2 * half], False)
        out_held = ring.second(shared_line[:, 2 * half :], True)
        triple_2, in_held, out_held = tie(triple_2, in_held, out_held)
        in_held, out_held = ring.third(in_held, False), ring.third(out_held, True)
    attended_2, logsum_2 = attend(triple_2, image_kind, pairs, pairs)
    projected, residual, branch_in, logits, output_weight_all, router_all = make_branch(
        me,
        attended_1,
        attended_2,
        patches,
        gate_first,
        shift_second,
        scale_second,
        dense_weights,
    )
    choose = expert_ids[:, :, None] == jnp.arange(E, dtype=jnp.int32)[None, None, :]
    choose = choose.astype(F32)
    gates = jax.nn.softmax(jnp.sum(choose * logits[:, None, :E], axis=-1), axis=-1)

    grad_out = out_grad.astype(F32).reshape(blocks, SHORT, width)
    grad_branch = (gate_second * grad_out).astype(BF16).reshape(tok_count, width)
    grad_branch_wide = grad_branch.astype(F32)

    slots = slot_table(expert_ids)
    target = expert_ids * CAP + slots
    row_of = jnp.arange(E * CAP, dtype=jnp.int32)[:, None]
    pick0 = (row_of == target[None, :, 0]).astype(BF16)
    pick1 = (row_of == target[None, :, 1]).astype(BF16)
    send_rows = mm(pick0 + pick1, branch_in).astype(BF16).reshape(E, CAP, width)
    gates_sent = after(gates, send_rows)
    grad_picked = (gates_sent[:, :, None] * grad_branch_wide[:, None, :]).astype(BF16)
    grad_picked = after(grad_picked, send_rows)
    if ring.direct:
        in_held, out_held = after(in_held, send_rows), after(out_held, send_rows)
        grad_picked, in_held, out_held = tie(grad_picked, in_held, out_held)
        in_weights = (in_held, ring.over_core(in_held))
        out_weights = (out_held, ring.over_core(out_held))
    grad_send = mm(pick0, grad_picked[:, 0]) + mm(pick1, grad_picked[:, 1])
    grad_send = grad_send.astype(BF16).reshape(E, CAP, width)
    shared_x = after(branch_in, send_rows, grad_send)

    def exchange(rows):
        return lax.all_to_all(rows, ("exp", "yi"), 0, 0, tiled=True)

    received = exchange(send_rows)

    shared_res, grad_branch_in, shared_grads = shared_expert(
        me, shared_x, grad_branch, *in_weights, *out_weights
    )

    received = after(received, shared_res)
    received = received.reshape(-1, width)
    grad_received = exchange(after(grad_send, received))
    expert_res, expert_act, expert_slope = expert_call(
        expert_kernel, "experts", received, (), expert_weights, 2
    )
    grad_received = grad_received.reshape(-1, width)
    expert_res = after(expert_res, grad_received)
    returned = exchange(expert_res.reshape(E, CAP, width))
    grad_rows, grad_pre = expert_call(
        expert_back_kernel, "experts_back", grad_received, (expert_slope,), expert_weights, 1
    )
    returned = returned.reshape(-1, width)
    grad_rows = after(grad_rows, returned)
    grad_returned = exchange(grad_rows.reshape(E, CAP, width)).reshape(-1, width)

    n_parts = expert_weights.shape[0]
    first = z - 1 if ring.direct else jnp.zeros((), jnp.int32)

    def grads_of(turn_at, act):
        part = ((first - turn_at) % n_parts if ring.direct else first + turn_at).reshape(1)
        return expert_grads(received, grad_pre, act, grad_received, part)

    grad_blocks = [grads_of(0, expert_act)]
    picked0 = mm_lt(pick0, returned)
    picked1 = mm_lt(pick1, returned)
    mixture = gates[:, 0:1] * picked0 + gates[:, 1:2] * picked1
    act = after(expert_act, mixture)
    for part in range(1, n_parts):
        grad_blocks.append(grads_of(part, act))
        act = after(act, grad_blocks[-1])
    if ring.direct:
        moved = ring.step(grad_blocks[0])

    if ring.direct:
        moved = add(after(moved, *grad_blocks), grad_blocks[1])
        grad_returned, moved = tie(grad_returned, moved)
        moved = ring.step(moved)
    branch_out = (shared_res + mixture).reshape(blocks, SHORT, width)
    projected = projected.reshape(blocks, SHORT, width)
    residual = residual.reshape(blocks, SHORT, width)
    normed_second, inverse_second = layer_norm(residual)
    block_out = (residual + gate_second * branch_out).reshape(tok_count, width).astype(BF16)
    grad_gate_second = jnp.sum(grad_out * branch_out, axis=1)
    grad_gates = jnp.stack(
        (
            jnp.sum(grad_branch_wide * picked0, axis=-1),
            jnp.sum(grad_branch_wide * picked1, axis=-1),
        ),
        axis=1,
    )
    grad_chosen = gates * (grad_gates - jnp.sum(gates * grad_gates, axis=-1, keepdims=True))
    grad_logits = jnp.sum(choose * grad_chosen[:, :, None], axis=1).astype(BF16)
    grad_logits = jnp.concatenate((grad_logits, jnp.zeros((tok_count, LANES - E), BF16)), axis=1)
    grad_branch_in = (
        grad_branch_in
        + mm_lt(pick0 + pick1, grad_returned)
        + mm_rt(grad_logits, router_all)
    )
    grad_norm_in = grad_branch_in.reshape(blocks, SHORT, width)
    grad_shift_second = jnp.sum(grad_norm_in, axis=1)
    grad_scale_second = jnp.sum(grad_norm_in * normed_second, axis=1)
    grad_residual = grad_out + norm_back(
        grad_norm_in * (1.0 + scale_second), normed_second, inverse_second
    )
    grad_gate_first = jnp.sum(grad_residual * projected, axis=1)
    grad_projected = (gate_first * grad_residual).astype(BF16).reshape(tok_count, width)
    grad_attended, out_grad_all, router_grad_all = project_back(
        attended_1, attended_2, grad_projected, branch_in, grad_logits, output_weight_all
    )
    if ring.direct:
        neighbour = ring.over_y(grad_blocks[3][1])
        grad_attended = after(grad_attended, neighbour)
    grad_triple_1 = attend_back(triple, attended_1, logsum_1, grad_attended, image_kind, 0)
    grad_attended_2 = after(grad_attended, grad_triple_1)
    if ring.direct:
        moved = add(moved, grad_blocks[2])
        grad_attended_2, own, aside = tie(grad_attended_2, moved[0], moved[1])
        own, aside = ring.step(own), ring.step_aside(aside)
    grad_triple_2 = attend_back(triple, attended_2, logsum_2, grad_attended_2, image_kind, pairs)
    grad_attend_in, *dense_grads = triple_back(
        me,
        grad_triple_1,
        grad_triple_2,
        attend_in,
        triple_weight,
        out_grad_all,
        router_grad_all,
    )
    if ring.direct:
        own_1, give_1, own_2, give_2 = dense_grads
        give_1, give_2 = after(give_1, own, aside), after(give_2, own, aside)
        grad_attend_in = after(grad_attend_in, own, aside)
        sum_1, give_1 = add_both(own_1, ring.over_core(give_1))
        sum_2, give_2 = add_both(own_2, ring.over_core(give_2))
        got_1, got_2 = ring.outer(give_1, False), ring.outer(give_2, True)
    inputs = patches.astype(F32).reshape(blocks, SHORT, width)
    normed_first, inverse_first = layer_norm(inputs)
    grad_attend_in = grad_attend_in.reshape(blocks, SHORT, width)
    grad_shift_first = jnp.sum(grad_attend_in, axis=1)
    grad_scale_first = jnp.sum(grad_attend_in * normed_first, axis=1)
    patches_grad = grad_residual + norm_back(
        grad_attend_in * (1.0 + scale_first), normed_first, inverse_first
    )
    patches_grad = patches_grad.reshape(tok_count, width)

    grad_modulation = jnp.stack(
        (
            grad_shift_first,
            grad_scale_first,
            grad_gate_first,
            grad_shift_second,
            grad_scale_second,
            grad_gate_second,
        ),
        axis=1,
    )
    grad_modulation = grad_modulation.reshape(blocks, n_exp, mod_cols).astype(BF16)
    mod_send = jnp.broadcast_to(
        grad_modulation.transpose(1, 0, 2)[:, None], (n_exp, n_fsdp, blocks, mod_cols)
    )
    if ring.direct:
        mod_send = after(mod_send, sum_1, sum_2)
    mod_all = lax.all_to_all(
        mod_send.reshape(n_all, blocks, mod_cols), ALL, 0, 0, tiled=True
    ).reshape(n_all * blocks, mod_cols)
    modulate_grad = mm_lt(cond_all, mod_all)
    cond_part = mm_rt(mod_all, modulate_weight).reshape(n_all, blocks, mod_rows)
    if ring.direct:
        sum_1, give_1 = add_both(sum_1, got_1)
        sum_2, give_2 = add_both(sum_2, got_2)
        got_1, got_2 = ring.inner(give_1, False), ring.inner(give_2, True)
        held = jnp.concatenate((add(sum_1, got_1), add(sum_2, got_2)), axis=1)
        cond_part = after(cond_part, held)
        got_line = ring.line(held)
    cond_part = lax.all_to_all(cond_part, ALL, 0, 0, tiled=True)
    cond_grad = jnp.sum(cond_part.reshape(n_exp, n_fsdp, blocks, mod_rows), axis=0)
    cond_grad = cond_grad.transpose(1, 0, 2).reshape(blocks, width) * silu_slope(cond_float)

    if ring.direct:
        cols, experts = width // PIECES, E // PIECES
        summed = add_line(held[0], got_line)
        output_grad, router_grad = summed[:, :cols], summed[:, cols : cols + experts]
        attend_grad = summed[:, OUT_LANES:]
        summed = lax.psum_scatter(
            shared_grads.reshape((n_all,) + bundle.shape), ALL, scatter_dimension=0
        ).astype(F32)
        shared_in_grad = summed[: 2 * half]
        shared_out_grad = turn_back(summed[2 * half :])
        own = own.astype(F32) + grad_blocks[3][0].astype(F32)
        aside = aside.astype(F32) + neighbour.astype(F32)
        first, second = jnp.where(y == 0, own, aside), jnp.where(y == 0, aside, own)
        expert_in_grad = jnp.stack((up_of(first), up_of(second)))
        expert_out_grad = jnp.stack((down_of(first), down_of(second)))
    else:

        def spread(grad):
            part = lax.psum_scatter(grad, "exp", scatter_dimension=1, tiled=True)
            return lax.psum_scatter(part, FSDP, scatter_dimension=0, tiled=True).astype(F32)

        dense_all = jnp.concatenate(
            (by_place(*dense_grads[:2], False), by_place(*dense_grads[2:], True)), axis=2
        )
        cols, experts = width // PIECES, E // PIECES
        attend_grad = spread(to_whole(dense_all[..., OUT_LANES:]))
        output_grad = spread(to_whole(dense_all[..., :cols]))
        router_grad = spread(to_whole(dense_all[..., cols : cols + experts]))
        shared_in_grad, shared_out_grad = map(spread, shared_unbundle(shared_grads))
        up_sum = jnp.concatenate([up_of(half) for block in grad_blocks for half in block], axis=1)
        down_sum = jnp.concatenate(
            [down_of(half) for block in grad_blocks for half in block], axis=0
        )
        expert_in_grad = lax.psum_scatter(up_sum, FSDP, scatter_dimension=1, tiled=True)
        expert_out_grad = lax.psum_scatter(down_sum, FSDP, scatter_dimension=0, tiled=True)
        expert_in_grad = expert_in_grad.astype(F32)[None]
        expert_out_grad = expert_out_grad.astype(F32)[None]
    return (
        block_out,
        patches_grad,
        cond_grad,
        modulate_grad,
        attend_grad,
        output_grad,
        router_grad,
        shared_in_grad,
        shared_out_grad,
        expert_in_grad,
        expert_out_grad,
    )


def solution(mesh):
    n_exp, n_fsdp = mesh.shape["exp"], mesh.shape["fsdp"]
    n_pair = E // n_exp
    if n_pair not in (1, 2) or n_fsdp % n_pair:
        raise ValueError("unsupported mesh")
    fine = Mesh(mesh.devices.reshape(n_exp, n_fsdp // n_pair, n_pair), ALL)
    ring = Ring(fine)
    in_specs = (
        P(ALL, None),
        P(ALL, None),
        P(ALL),
        P(ALL, None),
        P(ALL, None),
        P(FSDP, "exp"),
        P(FSDP, "exp"),
        P(FSDP, "exp"),
        P(FSDP, "exp"),
        P(FSDP, "exp"),
        P(FSDP, "exp"),
        P("exp", None, FSDP),
        P("exp", FSDP, None),
    )
    out_specs = (
        P(ALL, None),
        P(ALL, None),
        P(ALL, None),
        P(FSDP, "exp"),
        P(FSDP, "exp"),
        P(FSDP, "exp"),
        P(FSDP, "exp"),
        P(FSDP, "exp"),
        P(FSDP, "exp"),
        P("exp", None, FSDP),
        P("exp", FSDP, None),
    )

    def step(*args):
        return local(ring, *args)

    return jax.shard_map(step, mesh=fine, in_specs=in_specs, out_specs=out_specs, check_vma=False)
```

```python
import jax
import jax.numpy as jnp
from jax import lax
from jax.experimental import pallas as pl
from jax.experimental.pallas import tpu as pltpu
from jax.sharding import Mesh
from jax.sharding import PartitionSpec as P

H = 12
HD = 64
E = 8
TOPK = 2
SHORT = 256
GROUP = 1024
CAP = 288

F32 = jnp.float32
BF16 = jnp.bfloat16

eps_norm = 1e-06
tanh_gain = 0.7978845608028654
ALL = ("exp", "zi", "yi")
FSDP = ("zi", "yi")

PIECES = 4
STRIPS = 8
LANES = 128
OUT_LANES = 2 * LANES


def layer_norm(values):
    centered = values - jnp.mean(values, axis=-1, keepdims=True)
    inverse = lax.rsqrt(jnp.mean(centered * centered, axis=-1, keepdims=True) + eps_norm)
    return (centered * inverse, inverse)


def norm_back(grad, normed, inverse):
    return inverse * (
        grad
        - jnp.mean(grad, axis=-1, keepdims=True)
        - normed * jnp.mean(grad * normed, axis=-1, keepdims=True)
    )


def silu_slope(values):
    sigma = jax.nn.sigmoid(values)
    return sigma * (1.0 + values * (1.0 - sigma))


def dot(left, right, dims):
    return lax.dot_general(left, right, (dims, ((), ())), preferred_element_type=F32)


def mm(left, right):
    return dot(left, right, ((1,), (0,)))


def mm_rt(left, right):
    return dot(left, right, ((1,), (1,)))


def mm_lt(left, right):
    return dot(left, right, ((0,), (0,)))


def slot_table(expert_ids):
    flat = expert_ids.reshape(-1)
    onehot = (flat[:, None] == jnp.arange(E, dtype=jnp.int32)[None, :]).astype(jnp.int32)
    before = jnp.cumsum(onehot, axis=0) - onehot
    return jnp.sum(before * onehot, axis=1).reshape(expert_ids.shape)


def cost(flops, moved, share=64):
    return pl.CostEstimate(flops=flops // share, transcendentals=0, bytes_accessed=moved // share)


def fixed(shape):
    return pl.BlockSpec(shape, lambda *_: (0,) * len(shape), pipeline_mode=pl.Buffered(1))


LOG2E = 1.4426950408889634
SCORE = HD ** (-0.5)


def attend_kernel(kind_ref, query_ref, key_ref, value_ref, mixed_ref, logsum_ref):
    left = lax.broadcasted_iota(jnp.int32, (GROUP, 2 * HD), 1) < HD
    keys = key_ref[...]
    zero = jnp.zeros_like(keys)
    split_keys = (jnp.where(left, keys, zero), jnp.where(left, zero, keys))

    def rows_of(part, first, count):
        rows = pl.ds(part * SHORT, SHORT)
        query = query_ref[rows, :]
        value = value_ref[pl.ds(first, count), :]
        halves = []
        for half in range(2):
            scores = mm_rt(query, split_keys[half][first : first + count])
            peak = jnp.max(scores, axis=1, keepdims=True)
            weights = jnp.exp2((scores - peak) * (SCORE * LOG2E))
            total = jnp.sum(weights, axis=1, keepdims=True)
            halves.append(mm(weights.astype(BF16), value) / total)
            logsum = peak * (SCORE * LOG2E) + jnp.log2(total)
            logsum_ref[0, 0, half, rows] = jnp.transpose(
                jnp.broadcast_to(logsum, (SHORT, 2 * HD))
            )[0]
        mixed_ref[rows, :] = jnp.where(left[:SHORT], halves[0], halves[1]).astype(BF16)

    is_long = kind_ref[pl.program_id(0)] == 1

    @pl.when(is_long)
    def _():
        for part in range(GROUP // SHORT):
            rows_of(part, 0, GROUP)

    @pl.when(jnp.logical_not(is_long))
    def _():
        for part in range(GROUP // SHORT):
            rows_of(part, part * SHORT, SHORT)


def attend(triple, image_kind, first, count):
    groups = triple.shape[0] // GROUP
    pairs = H // 2

    def part(offset):
        return pl.BlockSpec((GROUP, 2 * HD), lambda g, i, kind: (g, offset + i))

    return pl.pallas_call(
        attend_kernel,
        out_shape=(
            jax.ShapeDtypeStruct((triple.shape[0], count * 2 * HD), BF16),
            jax.ShapeDtypeStruct((groups, count, 8, GROUP), F32),
        ),
        grid_spec=pltpu.PrefetchScalarGridSpec(
            num_scalar_prefetch=1,
            grid=(groups, count),
            in_specs=[part(first), part(pairs + first), part(2 * pairs + first)],
            out_specs=(
                part(0),
                pl.BlockSpec((1, 1, 8, GROUP), lambda g, i, kind: (g, i, 0, 0)),
            ),
        ),
        compiler_params=pltpu.CompilerParams(vmem_limit_bytes=32 << 20),
        cost_estimate=cost(32 * triple.shape[0] * GROUP * count * HD, 2 * triple.size),
        name="attend",
    )(image_kind, triple, triple, triple)


def attend_back_kernel(
    kind_ref,
    query_ref,
    key_ref,
    value_ref,
    mixed_ref,
    grad_ref,
    logsum_ref,
    grads_ref,
    key_sum,
    value_sum,
):
    left = lax.broadcasted_iota(jnp.int32, (GROUP, 2 * HD), 1) < HD

    def split(values):
        zero = jnp.zeros_like(values)
        return (jnp.where(left, values, zero), jnp.where(left, zero, values))

    split_query = split(query_ref[...])
    split_keys = split(key_ref[...])
    split_values = split(value_ref[...])
    split_grad = split(grad_ref[...])
    outer = jnp.transpose(mixed_ref[...].astype(F32) * grad_ref[...].astype(F32))
    inner = (
        jnp.sum(outer[:HD], axis=0, keepdims=True),
        jnp.sum(outer[HD:], axis=0, keepdims=True),
    )

    def rows_of(part, first, count, fresh):
        low, high = part * SHORT, (part + 1) * SHORT
        keys_at = pl.ds(first, count)
        query = query_ref[pl.ds(low, SHORT), :]
        grad = grad_ref[pl.ds(low, SHORT), :]
        key_part = value_part = query_part = None
        for half in range(2):
            keys = split_keys[half][first : first + count]
            scores = mm_rt(keys, query)
            logsum = logsum_ref[0, 0, half : half + 1, low:high]
            attention = jnp.exp2(scores * (SCORE * LOG2E) - logsum)
            moved = mm_rt(split_values[half][first : first + count], grad)
            grad_scores = (attention * (moved - inner[half][:, low:high])).astype(BF16)
            value_add = mm(attention.astype(BF16), split_grad[half][low:high])
            key_add = mm(grad_scores, split_query[half][low:high])
            query_add = mm_lt(grad_scores, keys)
            if half == 0:
                key_part, value_part, query_part = key_add, value_add, query_add
            else:
                key_part, value_part = key_part + key_add, value_part + value_add
                query_part = query_part + query_add
        grads_ref[0, pl.ds(low, SHORT), :] = (query_part * SCORE).astype(BF16)
        if fresh:
            key_sum[keys_at, :] = key_part
            value_sum[keys_at, :] = value_part
        else:
            key_sum[keys_at, :] += key_part
            value_sum[keys_at, :] += value_part

    is_long = kind_ref[pl.program_id(0)] == 1

    @pl.when(is_long)
    def _():
        for part in range(GROUP // SHORT):
            rows_of(part, 0, GROUP, part == 0)

    @pl.when(jnp.logical_not(is_long))
    def _():
        for part in range(GROUP // SHORT):
            rows_of(part, part * SHORT, SHORT, True)

    grads_ref[1, :, :] = (key_sum[...] * SCORE).astype(BF16)
    grads_ref[2, :, :] = value_sum[...].astype(BF16)


def attend_back(triple, attended, logsum, grad_attended, image_kind, first):
    groups, count = logsum.shape[:2]
    pairs = H // 2

    def part(offset):
        return pl.BlockSpec((GROUP, 2 * HD), lambda g, i, kind: (g, offset + i))

    return pl.pallas_call(
        attend_back_kernel,
        out_shape=jax.ShapeDtypeStruct((3, triple.shape[0], count * 2 * HD), BF16),
        grid_spec=pltpu.PrefetchScalarGridSpec(
            num_scalar_prefetch=1,
            grid=(groups, count),
            in_specs=[
                part(first),
                part(pairs + first),
                part(2 * pairs + first),
                part(0),
                part(first),
                pl.BlockSpec((1, 1, 8, GROUP), lambda g, i, kind: (g, i, 0, 0)),
            ],
            out_specs=pl.BlockSpec((3, GROUP, 2 * HD), lambda g, i, kind: (0, g, i)),
            scratch_shapes=[pltpu.VMEM((GROUP, 2 * HD), F32)] * 2,
        ),
        compiler_params=pltpu.CompilerParams(vmem_limit_bytes=32 << 20),
        cost_estimate=cost(80 * triple.shape[0] * GROUP * count * HD, 4 * triple.size),
        name="attend_back",
    )(image_kind, triple, triple, triple, attended, grad_attended, logsum)


def gelu_both(values):
    square = values * values
    side = tanh_gain * 0.044715 * square
    half = 0.5 + 0.5 * jnp.tanh(values * (tanh_gain + side))
    slope = half + 2.0 * values * (tanh_gain + 3.0 * side) * (half * (1.0 - half))
    return values * half, slope


def way(me, piece, strip):
    sx, other = (piece >> 1) ^ me[1], (piece & 1) ^ me[0]
    sy, k = (strip & 1) ^ me[2], (me[3] - (strip >> 1)) & 3
    return other, sx, sy, k


def on_side(other, own_ref, other_ref, action):
    @pl.when(other == 0)
    def _():
        action(own_ref)

    @pl.when(other == 1)
    def _():
        action(other_ref)


def normalize(values):
    mean = jnp.mean(values, axis=1, keepdims=True)
    centered = values - mean
    return centered * lax.rsqrt(jnp.mean(centered * centered, axis=1, keepdims=True) + eps_norm)


def triple_kernel(me, x_ref, shift_ref, scale_ref, q1a, q1b, q2a, q2b, in_ref, out_ref, weight_ref):
    rows, cols = q1a.shape[3], q1a.shape[4] - OUT_LANES

    @pl.when(pl.program_id(0) == 0)
    def _():
        for piece in range(PIECES):
            for strip in range(STRIPS):
                other, sx, sy, k = way(me, piece, strip)
                low, at = strip * 2 * rows, slice(piece * cols, (piece + 1) * cols)

                def first(ref):
                    weight_ref[low : low + rows, at] = ref[sx, sy, k, :, OUT_LANES:]

                def second(ref):
                    weight_ref[low + rows : low + 2 * rows, at] = ref[sy, sx, k, :, OUT_LANES:]

                on_side(other, q1a, q1b, first)
                on_side(other, q2a, q2b, second)

    normed = normalize(x_ref[...].astype(F32))
    attend_in = (normed * (1.0 + scale_ref[0]) + shift_ref[0]).astype(BF16)
    in_ref[...] = attend_in
    out_ref[...] = mm(attend_in, weight_ref[...]).astype(BF16)


def make_triple(me, patches, shift, scale, weights):
    tok_count, width = patches.shape
    hidden = PIECES * (weights[0].shape[4] - OUT_LANES)
    rows = pl.BlockSpec((SHORT, width), lambda i, me: (i, 0))
    each = pl.BlockSpec((1, 1, width), lambda i, me: (i, 0, 0))
    return pl.pallas_call(
        triple_kernel,
        out_shape=(
            jax.ShapeDtypeStruct((tok_count, width), BF16),
            jax.ShapeDtypeStruct((tok_count, hidden), BF16),
            jax.ShapeDtypeStruct((width, hidden), BF16),
        ),
        grid_spec=pltpu.PrefetchScalarGridSpec(
            num_scalar_prefetch=1,
            grid=(tok_count // SHORT,),
            in_specs=[rows, each, each] + [fixed(w.shape) for w in weights],
            out_specs=(
                rows,
                pl.BlockSpec((SHORT, hidden), lambda i, me: (i, 0)),
                fixed((width, hidden)),
            ),
        ),
        compiler_params=pltpu.CompilerParams(vmem_limit_bytes=40 << 20),
        cost_estimate=cost(2 * tok_count * width * hidden, 8 * tok_count * width),
        name="triple",
    )(me, patches, shift, scale, *weights)


def project_kernel(
    me,
    left_ref,
    right_ref,
    x_ref,
    gate_ref,
    shift_ref,
    scale_ref,
    q1a,
    q1b,
    q2a,
    q2b,
    projected_ref,
    residual_ref,
    branch_ref,
    logits_ref,
    weight_ref,
    router_ref,
):
    width = x_ref.shape[1]
    rows, cols, experts = q1a.shape[3], width // PIECES, E // PIECES

    @pl.when(pl.program_id(0) == 0)
    def _():
        router_ref[...] = jnp.zeros_like(router_ref)
        for piece in range(PIECES):
            for strip in range(STRIPS):
                other, sx, sy, k = way(me, piece, strip)

                def place(block, low):
                    weight_ref[low : low + rows, piece * cols : (piece + 1) * cols] = block[
                        :, :cols
                    ]
                    router_ref[
                        low : low + rows, piece * experts : (piece + 1) * experts
                    ] = block[:, cols : cols + experts]

                def first(ref):
                    place(ref[sx, sy, k], strip * 2 * rows)

                def second(ref):
                    place(ref[sy, sx, k], strip * 2 * rows + rows)

                on_side(other, q1a, q1b, first)
                on_side(other, q2a, q2b, second)

    split = left_ref.shape[1]
    projected = mm(left_ref[...], weight_ref[:split, :]) + mm(right_ref[...], weight_ref[split:, :])
    projected_ref[...] = projected
    residual = x_ref[...].astype(F32) + gate_ref[0] * projected
    residual_ref[...] = residual
    branch = (normalize(residual) * (1.0 + scale_ref[0]) + shift_ref[0]).astype(BF16)
    branch_ref[...] = branch
    logits_ref[...] = mm(branch, router_ref[...])


def make_branch(me, left, right, patches, gate, shift, scale, weights):
    tok_count, width = patches.shape
    rows = pl.BlockSpec((SHORT, width), lambda i, me: (i, 0))
    each = pl.BlockSpec((1, 1, width), lambda i, me: (i, 0, 0))
    outs = fixed(weights[0].shape[:4] + (OUT_LANES,))
    part = pl.BlockSpec((SHORT, width // 2), lambda i, me: (i, 0))
    return pl.pallas_call(
        project_kernel,
        out_shape=(
            jax.ShapeDtypeStruct((tok_count, width), F32),
            jax.ShapeDtypeStruct((tok_count, width), F32),
            jax.ShapeDtypeStruct((tok_count, width), BF16),
            jax.ShapeDtypeStruct((tok_count, LANES), F32),
            jax.ShapeDtypeStruct((width, width), BF16),
            jax.ShapeDtypeStruct((width, LANES), BF16),
        ),
        grid_spec=pltpu.PrefetchScalarGridSpec(
            num_scalar_prefetch=1,
            grid=(tok_count // SHORT,),
            in_specs=[part, part, rows, each, each, each, outs, outs, outs, outs],
            out_specs=(
                rows,
                rows,
                rows,
                pl.BlockSpec((SHORT, LANES), lambda i, me: (i, 0)),
                fixed((width, width)),
                fixed((width, LANES)),
            ),
        ),
        compiler_params=pltpu.CompilerParams(vmem_limit_bytes=32 << 20),
        cost_estimate=cost(2 * tok_count * width * width, 16 * tok_count * width),
        name="project",
    )(me, left, right, patches, gate, shift, scale, *weights)


def shared_kernel(
    me,
    x_ref,
    grad_ref,
    in_own,
    in_other,
    out_own,
    out_other,
    res_ref,
    x_grad_ref,
    weight_grad_ref,
    weight_in,
    weight_out,
    x_turned,
    grad_turned,
):
    step = pl.program_id(0)
    width = x_ref.shape[1]
    rows, half = width // STRIPS, width // 2
    halves = [slice(0, half), slice(half, width)]

    @pl.when(step == 0)
    def _():
        x_turned[...] = jnp.transpose(x_ref[...])
        grad_turned[...] = jnp.transpose(grad_ref[...])

    def take_in(ref):
        for sy in range(2):
            for z in range(4):
                low = (2 * z + (sy ^ me[2])) * rows
                weight_in[pl.ds(pl.multiple_of(low, 32), rows), :] = ref[0, sy, z]

    on_side((step & 1) ^ me[0], in_own, in_other, take_in)
    for other, ref in enumerate((out_own, out_other)):
        for sx in range(2):
            low = (((sx ^ me[1]) << 1) | (other ^ me[0])) * 2 * rows
            for sy in range(2):
                at = pl.ds(pl.multiple_of((sy ^ me[2]) * half, LANES), half)
                for part in range(2):
                    start = pl.multiple_of(low + part * rows, 32)
                    weight_out[pl.ds(start, rows), at] = ref[sy, sx, 0, :, halves[part]]

    act, slope = gelu_both(mm(x_ref[...], weight_in[...]))
    act = act.astype(BF16)
    grad_pre = (mm(grad_ref[...], weight_out[...]) * slope).astype(BF16)
    res = mm_rt(act, weight_out[...])
    x_grad = mm_rt(grad_pre, weight_in[...])

    @pl.when(step == 0)
    def _():
        res_ref[...] = res
        x_grad_ref[...] = x_grad

    @pl.when(step != 0)
    def _():
        res_ref[...] += res
        x_grad_ref[...] += x_grad

    in_grad = mm(x_turned[...], grad_pre).astype(BF16)
    out_grad = mm(grad_turned[...], act).astype(BF16)
    weight_grad_ref[step, :, :rows, :] = in_grad.reshape(STRIPS, rows, width)
    for piece in range(PIECES):
        for strip in range(2):
            for part in range(2):
                low = (2 * piece + part) * rows
                weight_grad_ref[piece, 2 * step + strip, rows:, halves[part]] = out_grad[
                    low : low + rows, halves[strip]
                ]


def shared_expert(me, x, grad, in_own, in_other, out_own, out_other):
    tok_count, width = x.shape
    rows = width // STRIPS
    whole = fixed((tok_count, width))
    block_in = pl.BlockSpec((1, 2, 4, rows, width), lambda j, me: ((j >> 1) ^ me[1], 0, 0, 0, 0))
    block_out = pl.BlockSpec((2, 2, 1, rows, width), lambda j, me: (0, 0, j, 0, 0))
    grads = jax.ShapeDtypeStruct((PIECES, STRIPS, 2 * rows, width), BF16)
    return pl.pallas_call(
        shared_kernel,
        out_shape=(jax.ShapeDtypeStruct((tok_count, width), F32),) * 2 + (grads,),
        grid_spec=pltpu.PrefetchScalarGridSpec(
            num_scalar_prefetch=1,
            grid=(PIECES,),
            in_specs=[whole, whole, block_in, block_in, block_out, block_out],
            out_specs=(whole, whole, fixed(grads.shape)),
            scratch_shapes=[pltpu.VMEM((width, width), BF16)] * 2
            + [pltpu.VMEM((width, tok_count), BF16)] * 2,
        ),
        compiler_params=pltpu.CompilerParams(vmem_limit_bytes=56 << 20),
        cost_estimate=cost(12 * tok_count * width * 4 * width, 16 * tok_count * width, 1),
        name="shared_expert",
    )(me, x, grad, in_own, in_other, out_own, out_other)


def project_back_kernel(
    left_ref,
    right_ref,
    grad_ref,
    branch_ref,
    logits_ref,
    weight_ref,
    back_ref,
    out_grad_ref,
):
    back_ref[...] = mm_rt(grad_ref[...], weight_ref[...]).astype(BF16)
    width = weight_ref.shape[0]
    outs, experts = width // PIECES, E // PIECES
    router = mm_lt(branch_ref[...], logits_ref[...]).astype(BF16)
    out_grad = jnp.concatenate(
        (mm_lt(left_ref[...], grad_ref[...]), mm_lt(right_ref[...], grad_ref[...])), axis=0
    ).astype(BF16)
    out_grad_ref[...] = jnp.zeros_like(out_grad_ref)
    for piece in range(PIECES):
        low = piece * OUT_LANES
        out_grad_ref[:, low : low + outs] = out_grad[:, piece * outs : (piece + 1) * outs]
        out_grad_ref[:, low + outs : low + outs + experts] = router[
            :, piece * experts : (piece + 1) * experts
        ]


def project_back(left, right, grad, branch, grad_logits, weight):
    tok_count, width = grad.shape
    part = fixed((tok_count, width // 2))
    whole = fixed((tok_count, width))
    return pl.pallas_call(
        project_back_kernel,
        out_shape=(
            jax.ShapeDtypeStruct((tok_count, width), BF16),
            jax.ShapeDtypeStruct((width, PIECES * OUT_LANES), BF16),
        ),
        grid=(1,),
        in_specs=[part, part, whole, whole, fixed((tok_count, LANES)), fixed((width, width))],
        out_specs=(whole, fixed((width, PIECES * OUT_LANES))),
        compiler_params=pltpu.CompilerParams(vmem_limit_bytes=32 << 20),
        cost_estimate=cost(4 * tok_count * width * width, 8 * tok_count * width),
        name="project_back",
    )(left, right, grad, branch, grad_logits, weight)


def triple_back_kernel(
    me,
    left_ref,
    right_ref,
    in_ref,
    weight_ref,
    out_grad_ref,
    back_ref,
    q1a,
    q1b,
    q2a,
    q2b,
    in_turned,
    weight_grad,
):
    step = pl.program_id(0)
    rows, cols = q1a.shape[3], q1a.shape[4] - OUT_LANES
    width = in_ref.shape[1]

    @pl.when(step == 0)
    def _():
        in_turned[...] = jnp.transpose(in_ref[...])

    grad = jnp.concatenate((left_ref[0], right_ref[0]), axis=1)
    at = pl.ds(pl.multiple_of(step * width, LANES), width)
    weight_grad[:, at] = mm(in_turned[...], grad).astype(BF16)
    back = mm_rt(grad, weight_ref[...])

    @pl.when(step == 0)
    def _():
        back_ref[...] = back

    @pl.when(step != 0)
    def _():
        back_ref[...] += back

    @pl.when(step == 2)
    def _():
        for piece in range(PIECES):
            for strip in range(STRIPS):
                other, sx, sy, k = way(me, piece, strip)

                def place(ref, where, low):
                    at = slice(low, low + rows)
                    ref[where + (slice(None), slice(0, OUT_LANES))] = out_grad_ref[
                        at, piece * OUT_LANES : (piece + 1) * OUT_LANES
                    ]
                    ref[where + (slice(None), slice(OUT_LANES, None))] = weight_grad[
                        at, piece * cols : (piece + 1) * cols
                    ]

                def first(ref):
                    place(ref, (sx, sy, k), strip * 2 * rows)

                def second(ref):
                    place(ref, (sy, sx, k), strip * 2 * rows + rows)

                on_side(other, q1a, q1b, first)
                on_side(other, q2a, q2b, second)


def triple_back(me, left, right, attend_in, weight, out_grad):
    tok_count, width = attend_in.shape
    hidden = weight.shape[1]
    block = (2, 2, 4, width // STRIPS // 2, OUT_LANES + hidden // PIECES)
    block = jax.ShapeDtypeStruct(block, BF16)
    return pl.pallas_call(
        triple_back_kernel,
        out_shape=(jax.ShapeDtypeStruct((tok_count, width), F32),) + (block,) * 4,
        grid_spec=pltpu.PrefetchScalarGridSpec(
            num_scalar_prefetch=1,
            grid=(3,),
            in_specs=[
                pl.BlockSpec((1, tok_count, width // 2), lambda p, me: (p, 0, 0)),
                pl.BlockSpec((1, tok_count, width // 2), lambda p, me: (p, 0, 0)),
                fixed((tok_count, width)),
                pl.BlockSpec((width, width), lambda p, me: (0, p)),
                fixed(out_grad.shape),
            ],
            out_specs=(fixed((tok_count, width)),) + (fixed(block.shape),) * 4,
            scratch_shapes=[
                pltpu.VMEM((width, tok_count), BF16),
                pltpu.VMEM((width, hidden), BF16),
            ],
        ),
        compiler_params=pltpu.CompilerParams(vmem_limit_bytes=40 << 20),
        cost_estimate=cost(4 * tok_count * width * hidden, 12 * tok_count * width),
        name="triple_back",
    )(me, left, right, attend_in, weight, out_grad)


ROW_TILE = 576


def expert_kernel(x_ref, weights_ref, res_ref, act_ref, slope_ref):
    x = x_ref[...]
    width = x_ref.shape[1]
    total = None
    for part in range(weights_ref.shape[0]):
        at = pl.ds(part * width, width)
        act, slope = gelu_both(mm(x, weights_ref[part, :width, :]))
        act = act.astype(BF16)
        act_ref[:, at] = act
        slope_ref[:, at] = slope.astype(BF16)
        res = mm(act, weights_ref[part, width:, :])
        total = res if total is None else total + res
    res_ref[...] = total.astype(BF16)


def expert_back_kernel(grad_ref, slope_ref, weights_ref, rows_ref, pre_ref):
    grad = grad_ref[...]
    width = grad_ref.shape[1]
    total = None
    for part in range(weights_ref.shape[0]):
        at = pl.ds(part * width, width)
        grad_pre = mm_rt(grad, weights_ref[part, width:, :]) * slope_ref[:, at].astype(F32)
        grad_pre = grad_pre.astype(BF16)
        pre_ref[:, at] = grad_pre
        rows = mm_rt(grad_pre, weights_ref[part, :width, :])
        total = rows if total is None else total + rows
    rows_ref[...] = total.astype(BF16)


def expert_call(kernel, name, rows_in, wide_in, weights, n_wide):
    rows, width = rows_in.shape
    hidden = weights.shape[0] * width
    narrow = pl.BlockSpec((ROW_TILE, width), lambda i: (i, 0))
    wide = pl.BlockSpec((ROW_TILE, hidden), lambda i: (i, 0))
    return pl.pallas_call(
        kernel,
        out_shape=(jax.ShapeDtypeStruct((rows, width), BF16),)
        + (jax.ShapeDtypeStruct((rows, hidden), BF16),) * n_wide,
        grid=(rows // ROW_TILE,),
        in_specs=[narrow] + [wide] * len(wide_in) + [fixed(weights.shape)],
        out_specs=(narrow,) + (wide,) * n_wide,
        compiler_params=pltpu.CompilerParams(vmem_limit_bytes=48 << 20),
        cost_estimate=cost(8 * rows * hidden * width, 2 * rows * hidden * (1 + n_wide)),
        name=name,
    )(rows_in, *wide_in, weights)


def expert_grads_kernel(part, x_ref, pre_ref, act_ref, grad_ref, out_ref):
    step, cols = pl.program_id(0), x_ref.shape[1]
    up = mm_lt(x_ref[...], pre_ref[...]).astype(BF16)
    down = mm_lt(act_ref[...], grad_ref[...]).astype(BF16)
    out_ref[0, step] = up[:, :cols]
    out_ref[1, step] = up[:, cols:]
    out_ref[step, 2] = down[:, :cols]
    out_ref[step, 3] = down[:, cols:]


def expert_grads(x, grad_pre, act, grad, part):
    rows, width = x.shape
    cols = width // 2
    out = jax.ShapeDtypeStruct((2, 4, cols, cols), BF16)
    return pl.pallas_call(
        expert_grads_kernel,
        out_shape=out,
        grid_spec=pltpu.PrefetchScalarGridSpec(
            num_scalar_prefetch=1,
            grid=(2,),
            in_specs=[
                pl.BlockSpec((rows, cols), lambda i, part: (0, i)),
                pl.BlockSpec((rows, width), lambda i, part: (0, part[0])),
                pl.BlockSpec((rows, cols), lambda i, part: (0, part[0] * 2 + i)),
                fixed((rows, width)),
            ],
            out_specs=fixed(out.shape),
        ),
        compiler_params=pltpu.CompilerParams(vmem_limit_bytes=40 << 20),
        cost_estimate=cost(4 * rows * width * width, 8 * rows * width),
        name="expert_grads",
    )(part, x, grad_pre, act, grad)


def up_of(half):
    return jnp.concatenate((half[0], half[1]), axis=0)


def down_of(half):
    return jnp.concatenate((half[2], half[3]), axis=1)


def by_way(blocks, y_outer, turns=True):
    rows, cols = blocks.shape[2:]
    blocks = blocks.reshape(2, 2, 4, 2, rows, cols)
    if turns:
        blocks = blocks[:, :, jnp.array([0, 3, 2, 1])]
    blocks = blocks.transpose((1, 3, 0, 2, 4, 5) if y_outer else (1, 0, 3, 2, 4, 5))
    return blocks[0], blocks[1]


def by_place(own, other, y_outer):
    blocks = jnp.stack((own, other))
    blocks = blocks.transpose((2, 0, 3, 1, 4, 5) if y_outer else (1, 0, 3, 2, 4, 5))
    rows, cols = blocks.shape[4:]
    return blocks[:, :, jnp.array([0, 3, 2, 1])].reshape(PIECES, STRIPS, rows, cols)


def to_blocks(whole):
    rows, cols = whole.shape
    return whole.reshape(STRIPS, rows // STRIPS, PIECES, cols // PIECES).transpose(2, 0, 1, 3)


def to_whole(blocks):
    rows, cols = blocks.shape[2:]
    return blocks.transpose(1, 2, 0, 3).reshape(STRIPS * rows, PIECES * cols)


def turn(block):
    block = block.T
    half = block.shape[0] // 2
    return jnp.concatenate((block[:half], block[half:]), axis=1)


def turn_back(block):
    half = block.shape[1] // 2
    return jnp.concatenate((block[:, :half], block[:, half:]), axis=0).T


def shared_bundle(up, down):
    down = to_blocks(down).swapaxes(2, 3)
    half = down.shape[2] // 2
    return jnp.concatenate(
        (to_blocks(up), jnp.concatenate((down[:, :, :half], down[:, :, half:]), axis=3)), axis=2
    )


def shared_unbundle(grads):
    rows, half = grads.shape[2] // 2, grads.shape[3] // 2
    down = grads[:, :, rows:]
    down = jnp.concatenate((down[..., :half], down[..., half:]), axis=2).swapaxes(2, 3)
    return to_whole(grads[:, :, :rows]), to_whole(down)


class Ring:
    def __init__(self, mesh):
        self.n_exp = mesh.shape["exp"]
        self.n_ring = mesh.shape["zi"]
        self.n_pair = mesh.shape["yi"]
        self.direct = (self.n_exp, self.n_ring, self.n_pair) == (PIECES, 4, 2)

    def step(self, value, by=1):
        n = self.n_ring
        return lax.ppermute(value, "zi", [(i, (i + by) % n) for i in range(n)])

    def step_aside(self, value):
        n = 2 * self.n_ring
        return lax.ppermute(value, FSDP, [(i, (i + 2) % n ^ 1) for i in range(n)])

    def over_y(self, value):
        return lax.ppermute(value, "yi", [(0, 1), (1, 0)])

    def over_x(self, value):
        return lax.ppermute(value, "exp", [(i, i ^ 2) for i in range(4)])

    def over_core(self, value):
        return lax.ppermute(value, "exp", [(i, i ^ 1) for i in range(4)])

    def near(self, block):
        return jnp.stack([block] + [self.step(block, k) for k in range(1, 4)])

    def second(self, held, y_outer):
        return jnp.stack((held, (self.over_x if y_outer else self.over_y)(held)))

    def third(self, held, y_outer):
        return jnp.stack((held, (self.over_y if y_outer else self.over_x)(held)))

    def outer(self, value, y_outer):
        return (self.over_y if y_outer else self.over_x)(value)

    def inner(self, value, y_outer):
        return (self.over_x if y_outer else self.over_y)(value)

    def line(self, held):
        return tuple(self.step(held[k], -k) for k in range(1, 4))


def add_both(keep, got):
    return add(keep[0], got[0]), add(keep[1], got[1])


def add_line(held, got):
    total = held.astype(F32)
    for part in got:
        total = total + part.astype(F32)
    return total


def add(left, right):
    return (left.astype(F32) + right.astype(F32)).astype(BF16)


def tie(*values):
    return lax.optimization_barrier(values)


def after(value, *others):
    return lax.optimization_barrier((value,) + others)[0]


def local(
    ring,
    patches,
    cond_embed,
    image_kind,
    expert_ids,
    out_grad,
    modulate_weight,
    attend_weight,
    output_weight,
    router_weight,
    shared_in,
    shared_out,
    expert_in,
    expert_out,
):
    tok_count, width = patches.shape
    blocks = tok_count // SHORT
    n_exp, n_ring, n_pair = ring.n_exp, ring.n_ring, ring.n_pair
    n_fsdp = n_ring * n_pair
    n_all = n_exp * n_fsdp
    e, z, y = (lax.axis_index(name) for name in ("exp", "zi", "yi"))
    mod_rows, mod_cols = modulate_weight.shape
    half = width // STRIPS // 2
    if ring.direct:
        me = jnp.stack((e & 1, e >> 1, y, z)).astype(jnp.int32)
    else:
        me = jnp.zeros((4,), jnp.int32)

    if ring.direct:
        spare = OUT_LANES - output_weight.shape[1] - router_weight.shape[1]
        block = jnp.concatenate(
            (
                output_weight,
                router_weight,
                jnp.zeros((router_weight.shape[0], spare), BF16),
                attend_weight,
            ),
            axis=1,
        )
        held = ring.near(block)

    cond_float = cond_embed.astype(F32)
    cond_act = jax.nn.silu(cond_float).astype(BF16)
    cond_send = cond_act.reshape(blocks, n_fsdp, mod_rows).transpose(1, 0, 2)
    cond_send = jnp.broadcast_to(cond_send[None], (n_exp, n_fsdp, blocks, mod_rows))
    cond_all = lax.all_to_all(
        cond_send.reshape(n_all, blocks, mod_rows), ALL, 0, 0, tiled=True
    ).reshape(n_all * blocks, mod_rows)
    if ring.direct:
        own_in = jnp.where(y == 0, expert_in[0], expert_in[1])
        got_in = ring.over_y(jnp.where(y == 0, expert_in[1], expert_in[0]))
        cond_all = after(cond_all, held, got_in)
    mod_part = mm(cond_all, modulate_weight).astype(BF16).reshape(n_all, blocks, mod_cols)
    mod_part = lax.all_to_all(mod_part, ALL, 0, 0, tiled=True)
    mod_part = mod_part.reshape(n_exp, n_fsdp, blocks, mod_cols)
    modulation = jnp.sum(mod_part.astype(F32), axis=1)
    if ring.direct:
        held = after(held, modulation)
    modulation = modulation.transpose(1, 0, 2).reshape(blocks, 1, 6, width)

    if ring.direct:
        own_out = jnp.where(y == 0, expert_out[0], expert_out[1])
        got_out = ring.over_y(jnp.where(y == 0, expert_out[1], expert_out[0]))
        got_out = after(got_out, modulation)
        expert_block = jnp.concatenate(
            (
                jnp.concatenate((own_in, got_in), axis=1),
                jnp.concatenate((own_out, got_out), axis=0),
            ),
            axis=0,
        )
        held = after(held, expert_block)
        held_1 = ring.second(held[:, :half], False)
        held_2 = ring.second(held[:, half:], True)
        bundle = jnp.concatenate((shared_in, turn(shared_out)), axis=0)
        shared_line = lax.all_gather(bundle, "zi", axis=0, tiled=False)
        expert_weights = lax.all_gather(after(expert_block, shared_line), "zi", axis=0)
        held_1 = ring.third(held_1, False)
        held_2 = ring.third(held_2, True)
        dense_weights = (held_1, ring.over_core(held_1), held_2, ring.over_core(held_2))
    else:
        wholes = [
            lax.all_gather(
                lax.all_gather(w, FSDP, axis=0, tiled=True), "exp", axis=1, tiled=True
            )
            for w in (attend_weight, output_weight, router_weight, shared_in, shared_out)
        ]
        attend_all, output_all, router_all = map(to_blocks, wholes[:3])
        up_all, down_all = wholes[3:]
        spare = jnp.zeros((PIECES, STRIPS, 2 * half, OUT_LANES - (width + E) // PIECES), BF16)
        dense_all = jnp.concatenate((output_all, router_all, spare, attend_all), axis=3)
        dense_weights = by_way(dense_all[:, :, :half], False)
        dense_weights += by_way(dense_all[:, :, half:], True)
        shared_all = shared_bundle(up_all, down_all)
        in_weights = by_way(shared_all[:, :, : 2 * half], False, False)
        out_weights = by_way(shared_all[:, :, 2 * half :], True, False)
        up_all = lax.all_gather(expert_in[0], FSDP, axis=1, tiled=True)
        down_all = lax.all_gather(expert_out[0], FSDP, axis=0, tiled=True)
        expert_weights = jnp.stack(
            [
                jnp.concatenate((up_all[:, at : at + width], down_all[at : at + width]), axis=0)
                for at in range(0, up_all.shape[1], width)
            ]
        )

    shift_first = modulation[:, :, 0]
    scale_first = modulation[:, :, 1]
    gate_first = modulation[:, :, 2]
    shift_second = modulation[:, :, 3]
    scale_second = modulation[:, :, 4]
    gate_second = modulation[:, :, 5]
    attend_in, triple, triple_weight = make_triple(
        me, patches, shift_first, scale_first, dense_weights
    )
    pairs = H // 4
    attended_1, logsum_1 = attend(triple, image_kind, 0, pairs)
    triple_2 = after(triple, attended_1)
    if ring.direct:
        shared_line = after(shared_line, triple)
        in_held = ring.second(shared_line[:, : 2 * half], False)
        out_held = ring.second(shared_line[:, 2 * half :], True)
        triple_2, in_held, out_held = tie(triple_2, in_held, out_held)
        in_held, out_held = ring.third(in_held, False), ring.third(out_held, True)
    attended_2, logsum_2 = attend(triple_2, image_kind, pairs, pairs)
    projected, residual, branch_in, logits, output_weight_all, router_all = make_branch(
        me,
        attended_1,
        attended_2,
        patches,
        gate_first,
        shift_second,
        scale_second,
        dense_weights,
    )
    choose = expert_ids[:, :, None] == jnp.arange(E, dtype=jnp.int32)[None, None, :]
    choose = choose.astype(F32)
    gates = jax.nn.softmax(jnp.sum(choose * logits[:, None, :E], axis=-1), axis=-1)

    grad_out = out_grad.astype(F32).reshape(blocks, SHORT, width)
    grad_branch = (gate_second * grad_out).astype(BF16).reshape(tok_count, width)
    grad_branch_wide = grad_branch.astype(F32)

    slots = slot_table(expert_ids)
    target = expert_ids * CAP + slots
    row_of = jnp.arange(E * CAP, dtype=jnp.int32)[:, None]
    pick0 = (row_of == target[None, :, 0]).astype(BF16)
    pick1 = (row_of == target[None, :, 1]).astype(BF16)
    send_rows = mm(pick0 + pick1, branch_in).astype(BF16).reshape(E, CAP, width)
    gates_sent = after(gates, send_rows)
    grad_picked = (gates_sent[:, :, None] * grad_branch_wide[:, None, :]).astype(BF16)
    grad_picked = after(grad_picked, send_rows)
    if ring.direct:
        in_held, out_held = after(in_held, send_rows), after(out_held, send_rows)
        grad_picked, in_held, out_held = tie(grad_picked, in_held, out_held)
        in_weights = (in_held, ring.over_core(in_held))
        out_weights = (out_held, ring.over_core(out_held))
    grad_send = mm(pick0, grad_picked[:, 0]) + mm(pick1, grad_picked[:, 1])
    grad_send = grad_send.astype(BF16).reshape(E, CAP, width)
    shared_x = after(branch_in, send_rows, grad_send)

    def exchange(rows):
        return lax.all_to_all(rows, ("exp", "yi"), 0, 0, tiled=True)

    received = exchange(send_rows)

    shared_res, grad_branch_in, shared_grads = shared_expert(
        me, shared_x, grad_branch, *in_weights, *out_weights
    )

    received = after(received, shared_res)
    received = received.reshape(-1, width)
    grad_received = exchange(after(grad_send, received))
    expert_res, expert_act, expert_slope = expert_call(
        expert_kernel, "experts", received, (), expert_weights, 2
    )
    grad_received = grad_received.reshape(-1, width)
    expert_res = after(expert_res, grad_received)
    returned = exchange(expert_res.reshape(E, CAP, width))
    grad_rows, grad_pre = expert_call(
        expert_back_kernel, "experts_back", grad_received, (expert_slope,), expert_weights, 1
    )
    returned = returned.reshape(-1, width)
    grad_rows = after(grad_rows, returned)
    grad_returned = exchange(grad_rows.reshape(E, CAP, width)).reshape(-1, width)

    n_parts = expert_weights.shape[0]
    first = z - 1 if ring.direct else jnp.zeros((), jnp.int32)

    def grads_of(turn_at, act):
        part = ((first - turn_at) % n_parts if ring.direct else first + turn_at).reshape(1)
        return expert_grads(received, grad_pre, act, grad_received, part)

    grad_blocks = [grads_of(0, expert_act)]
    picked0 = mm_lt(pick0, returned)
    picked1 = mm_lt(pick1, returned)
    mixture = gates[:, 0:1] * picked0 + gates[:, 1:2] * picked1
    act = after(expert_act, mixture)
    for part in range(1, n_parts):
        grad_blocks.append(grads_of(part, act))
        act = after(act, grad_blocks[-1])
    if ring.direct:
        moved = ring.step(grad_blocks[0])

    if ring.direct:
        moved = add(after(moved, *grad_blocks), grad_blocks[1])
        grad_returned, moved = tie(grad_returned, moved)
        moved = ring.step(moved)
    branch_out = (shared_res + mixture).reshape(blocks, SHORT, width)
    projected = projected.reshape(blocks, SHORT, width)
    residual = residual.reshape(blocks, SHORT, width)
    normed_second, inverse_second = layer_norm(residual)
    block_out = (residual + gate_second * branch_out).reshape(tok_count, width).astype(BF16)
    grad_gate_second = jnp.sum(grad_out * branch_out, axis=1)
    grad_gates = jnp.stack(
        (
            jnp.sum(grad_branch_wide * picked0, axis=-1),
            jnp.sum(grad_branch_wide * picked1, axis=-1),
        ),
        axis=1,
    )
    grad_chosen = gates * (grad_gates - jnp.sum(gates * grad_gates, axis=-1, keepdims=True))
    grad_logits = jnp.sum(choose * grad_chosen[:, :, None], axis=1).astype(BF16)
    grad_logits = jnp.concatenate((grad_logits, jnp.zeros((tok_count, LANES - E), BF16)), axis=1)
    grad_branch_in = (
        grad_branch_in
        + mm_lt(pick0 + pick1, grad_returned)
        + mm_rt(grad_logits, router_all)
    )
    grad_norm_in = grad_branch_in.reshape(blocks, SHORT, width)
    grad_shift_second = jnp.sum(grad_norm_in, axis=1)
    grad_scale_second = jnp.sum(grad_norm_in * normed_second, axis=1)
    grad_residual = grad_out + norm_back(
        grad_norm_in * (1.0 + scale_second), normed_second, inverse_second
    )
    grad_gate_first = jnp.sum(grad_residual * projected, axis=1)
    grad_projected = (gate_first * grad_residual).astype(BF16).reshape(tok_count, width)
    grad_attended, out_grad_all = project_back(
        attended_1, attended_2, grad_projected, branch_in, grad_logits, output_weight_all
    )
    if ring.direct:
        neighbour = ring.over_y(grad_blocks[3][1])
        grad_attended = after(grad_attended, neighbour)
    grad_triple_1 = attend_back(triple, attended_1, logsum_1, grad_attended, image_kind, 0)
    grad_attended_2 = after(grad_attended, grad_triple_1)
    if ring.direct:
        moved = add(moved, grad_blocks[2])
        grad_attended_2, own, aside = tie(grad_attended_2, moved[0], moved[1])
        own, aside = ring.step(own), ring.step_aside(aside)
    grad_triple_2 = attend_back(triple, attended_2, logsum_2, grad_attended_2, image_kind, pairs)
    grad_attend_in, *dense_grads = triple_back(
        me,
        grad_triple_1,
        grad_triple_2,
        attend_in,
        triple_weight,
        out_grad_all,
    )
    if ring.direct:
        own_1, give_1, own_2, give_2 = dense_grads
        give_1, give_2 = after(give_1, own, aside), after(give_2, own, aside)
        got_1, got_2 = ring.over_core(give_1), ring.over_core(give_2)
        grad_attend_in = after(grad_attend_in, got_1, got_2)
        sum_1, give_1 = add_both(own_1, got_1)
        sum_2, give_2 = add_both(own_2, got_2)
        got_1, got_2 = ring.outer(give_1, False), ring.outer(give_2, True)
    inputs = patches.astype(F32).reshape(blocks, SHORT, width)
    normed_first, inverse_first = layer_norm(inputs)
    grad_attend_in = grad_attend_in.reshape(blocks, SHORT, width)
    grad_shift_first = jnp.sum(grad_attend_in, axis=1)
    grad_scale_first = jnp.sum(grad_attend_in * normed_first, axis=1)
    patches_grad = grad_residual + norm_back(
        grad_attend_in * (1.0 + scale_first), normed_first, inverse_first
    )
    patches_grad = patches_grad.reshape(tok_count, width)

    grad_modulation = jnp.stack(
        (
            grad_shift_first,
            grad_scale_first,
            grad_gate_first,
            grad_shift_second,
            grad_scale_second,
            grad_gate_second,
        ),
        axis=1,
    )
    grad_modulation = grad_modulation.reshape(blocks, n_exp, mod_cols).astype(BF16)
    mod_send = jnp.broadcast_to(
        grad_modulation.transpose(1, 0, 2)[:, None], (n_exp, n_fsdp, blocks, mod_cols)
    )
    if ring.direct:
        mod_send = after(mod_send, sum_1, sum_2)
    mod_all = lax.all_to_all(
        mod_send.reshape(n_all, blocks, mod_cols), ALL, 0, 0, tiled=True
    ).reshape(n_all * blocks, mod_cols)
    modulate_grad = mm_lt(cond_all, mod_all)
    cond_part = mm_rt(mod_all, modulate_weight).reshape(n_all, blocks, mod_rows)
    if ring.direct:
        sum_1, give_1 = add_both(sum_1, got_1)
        sum_2, give_2 = add_both(sum_2, got_2)
        got_1, got_2 = ring.inner(give_1, False), ring.inner(give_2, True)
        held = jnp.concatenate((add(sum_1, got_1), add(sum_2, got_2)), axis=1)
        cond_part = after(cond_part, held)
        got_line = ring.line(held)
    cond_part = lax.all_to_all(cond_part, ALL, 0, 0, tiled=True)
    cond_grad = jnp.sum(cond_part.reshape(n_exp, n_fsdp, blocks, mod_rows), axis=0)
    cond_grad = cond_grad.transpose(1, 0, 2).reshape(blocks, width) * silu_slope(cond_float)

    if ring.direct:
        cols, experts = width // PIECES, E // PIECES
        summed = add_line(held[0], got_line)
        output_grad, router_grad = summed[:, :cols], summed[:, cols : cols + experts]
        attend_grad = summed[:, OUT_LANES:]
        summed = lax.psum_scatter(
            shared_grads.reshape((n_all,) + bundle.shape), ALL, scatter_dimension=0
        ).astype(F32)
        shared_in_grad = summed[: 2 * half]
        shared_out_grad = turn_back(summed[2 * half :])
        own = own.astype(F32) + grad_blocks[3][0].astype(F32)
        aside = aside.astype(F32) + neighbour.astype(F32)
        first, second = jnp.where(y == 0, own, aside), jnp.where(y == 0, aside, own)
        expert_in_grad = jnp.stack((up_of(first), up_of(second)))
        expert_out_grad = jnp.stack((down_of(first), down_of(second)))
    else:

        def spread(grad):
            part = lax.psum_scatter(grad, "exp", scatter_dimension=1, tiled=True)
            return lax.psum_scatter(part, FSDP, scatter_dimension=0, tiled=True).astype(F32)

        dense_all = jnp.concatenate(
            (by_place(*dense_grads[:2], False), by_place(*dense_grads[2:], True)), axis=2
        )
        cols, experts = width // PIECES, E // PIECES
        attend_grad = spread(to_whole(dense_all[..., OUT_LANES:]))
        output_grad = spread(to_whole(dense_all[..., :cols]))
        router_grad = spread(to_whole(dense_all[..., cols : cols + experts]))
        shared_in_grad, shared_out_grad = map(spread, shared_unbundle(shared_grads))
        up_sum = jnp.concatenate([up_of(half) for block in grad_blocks for half in block], axis=1)
        down_sum = jnp.concatenate(
            [down_of(half) for block in grad_blocks for half in block], axis=0
        )
        expert_in_grad = lax.psum_scatter(up_sum, FSDP, scatter_dimension=1, tiled=True)
        expert_out_grad = lax.psum_scatter(down_sum, FSDP, scatter_dimension=0, tiled=True)
        expert_in_grad = expert_in_grad.astype(F32)[None]
        expert_out_grad = expert_out_grad.astype(F32)[None]
    return (
        block_out,
        patches_grad,
        cond_grad,
        modulate_grad,
        attend_grad,
        output_grad,
        router_grad,
        shared_in_grad,
        shared_out_grad,
        expert_in_grad,
        expert_out_grad,
    )


def solution(mesh):
    n_exp, n_fsdp = mesh.shape["exp"], mesh.shape["fsdp"]
    n_pair = E // n_exp
    if n_pair not in (1, 2) or n_fsdp % n_pair:
        raise ValueError("unsupported mesh")
    fine = Mesh(mesh.devices.reshape(n_exp, n_fsdp // n_pair, n_pair), ALL)
    ring = Ring(fine)
    in_specs = (
        P(ALL, None),
        P(ALL, None),
        P(ALL),
        P(ALL, None),
        P(ALL, None),
        P(FSDP, "exp"),
        P(FSDP, "exp"),
        P(FSDP, "exp"),
        P(FSDP, "exp"),
        P(FSDP, "exp"),
        P(FSDP, "exp"),
        P("exp", None, FSDP),
        P("exp", FSDP, None),
    )
    out_specs = (
        P(ALL, None),
        P(ALL, None),
        P(ALL, None),
        P(FSDP, "exp"),
        P(FSDP, "exp"),
        P(FSDP, "exp"),
        P(FSDP, "exp"),
        P(FSDP, "exp"),
        P(FSDP, "exp"),
        P("exp", None, FSDP),
        P("exp", FSDP, None),
    )

    def step(*args):
        return local(ring, *args)

    return jax.shard_map(step, mesh=fine, in_specs=in_specs, out_specs=out_specs, check_vma=False)
```

```python
import jax
import jax.numpy as jnp
from jax import lax
from jax.experimental import pallas as pl
from jax.experimental.pallas import tpu as pltpu
from jax.sharding import Mesh
from jax.sharding import PartitionSpec as P

H = 12
HD = 64
E = 8
TOPK = 2
SHORT = 256
GROUP = 1024
CAP = 288

F32 = jnp.float32
BF16 = jnp.bfloat16

eps_norm = 1e-06
tanh_gain = 0.7978845608028654
ALL = ("exp", "zi", "yi")
FSDP = ("zi", "yi")

PIECES = 4
STRIPS = 8
LANES = 128
OUT_LANES = 2 * LANES


def layer_norm(values):
    centered = values - jnp.mean(values, axis=-1, keepdims=True)
    inverse = lax.rsqrt(jnp.mean(centered * centered, axis=-1, keepdims=True) + eps_norm)
    return (centered * inverse, inverse)


def norm_back(grad, normed, inverse):
    return inverse * (
        grad
        - jnp.mean(grad, axis=-1, keepdims=True)
        - normed * jnp.mean(grad * normed, axis=-1, keepdims=True)
    )


def silu_slope(values):
    sigma = jax.nn.sigmoid(values)
    return sigma * (1.0 + values * (1.0 - sigma))


def dot(left, right, dims):
    return lax.dot_general(left, right, (dims, ((), ())), preferred_element_type=F32)


def mm(left, right):
    return dot(left, right, ((1,), (0,)))


def mm_rt(left, right):
    return dot(left, right, ((1,), (1,)))


def mm_lt(left, right):
    return dot(left, right, ((0,), (0,)))


def slot_table(expert_ids):
    flat = expert_ids.reshape(-1)
    onehot = (flat[:, None] == jnp.arange(E, dtype=jnp.int32)[None, :]).astype(jnp.int32)
    before = jnp.cumsum(onehot, axis=0) - onehot
    return jnp.sum(before * onehot, axis=1).reshape(expert_ids.shape)


def cost(flops, moved, share=64):
    return pl.CostEstimate(flops=flops // share, transcendentals=0, bytes_accessed=moved // share)


def fixed(shape):
    return pl.BlockSpec(shape, lambda *_: (0,) * len(shape), pipeline_mode=pl.Buffered(1))


LOG2E = 1.4426950408889634
SCORE = HD ** (-0.5)


def attend_kernel(kind_ref, query_ref, key_ref, value_ref, mixed_ref, logsum_ref):
    left = lax.broadcasted_iota(jnp.int32, (GROUP, 2 * HD), 1) < HD
    keys = key_ref[...]
    zero = jnp.zeros_like(keys)
    split_keys = (jnp.where(left, keys, zero), jnp.where(left, zero, keys))

    def rows_of(part, first, count):
        rows = pl.ds(part * SHORT, SHORT)
        query = query_ref[rows, :]
        value = value_ref[pl.ds(first, count), :]
        halves = []
        for half in range(2):
            scores = mm_rt(query, split_keys[half][first : first + count])
            peak = jnp.max(scores, axis=1, keepdims=True)
            weights = jnp.exp2((scores - peak) * (SCORE * LOG2E))
            total = jnp.sum(weights, axis=1, keepdims=True)
            halves.append(mm(weights.astype(BF16), value) / total)
            logsum = peak * (SCORE * LOG2E) + jnp.log2(total)
            logsum_ref[0, 0, half, rows] = jnp.transpose(
                jnp.broadcast_to(logsum, (SHORT, 2 * HD))
            )[0]
        mixed_ref[rows, :] = jnp.where(left[:SHORT], halves[0], halves[1]).astype(BF16)

    is_long = kind_ref[pl.program_id(0)] == 1

    @pl.when(is_long)
    def _():
        for part in range(GROUP // SHORT):
            rows_of(part, 0, GROUP)

    @pl.when(jnp.logical_not(is_long))
    def _():
        for part in range(GROUP // SHORT):
            rows_of(part, part * SHORT, SHORT)


def attend(triple, image_kind, first, count):
    groups = triple.shape[0] // GROUP
    pairs = H // 2

    def part(offset):
        return pl.BlockSpec((GROUP, 2 * HD), lambda g, i, kind: (g, offset + i))

    return pl.pallas_call(
        attend_kernel,
        out_shape=(
            jax.ShapeDtypeStruct((triple.shape[0], count * 2 * HD), BF16),
            jax.ShapeDtypeStruct((groups, count, 8, GROUP), F32),
        ),
        grid_spec=pltpu.PrefetchScalarGridSpec(
            num_scalar_prefetch=1,
            grid=(groups, count),
            in_specs=[part(first), part(pairs + first), part(2 * pairs + first)],
            out_specs=(
                part(0),
                pl.BlockSpec((1, 1, 8, GROUP), lambda g, i, kind: (g, i, 0, 0)),
            ),
        ),
        compiler_params=pltpu.CompilerParams(vmem_limit_bytes=32 << 20),
        cost_estimate=cost(32 * triple.shape[0] * GROUP * count * HD, 2 * triple.size),
        name="attend",
    )(image_kind, triple, triple, triple)


def attend_back_kernel(
    kind_ref,
    query_ref,
    key_ref,
    value_ref,
    mixed_ref,
    grad_ref,
    logsum_ref,
    grads_ref,
    key_sum,
    value_sum,
):
    left = lax.broadcasted_iota(jnp.int32, (GROUP, 2 * HD), 1) < HD

    def split(values):
        zero = jnp.zeros_like(values)
        return (jnp.where(left, values, zero), jnp.where(left, zero, values))

    split_query = split(query_ref[...])
    split_keys = split(key_ref[...])
    split_values = split(value_ref[...])
    split_grad = split(grad_ref[...])
    outer = jnp.transpose(mixed_ref[...].astype(F32) * grad_ref[...].astype(F32))
    inner = (
        jnp.sum(outer[:HD], axis=0, keepdims=True),
        jnp.sum(outer[HD:], axis=0, keepdims=True),
    )

    def rows_of(part, first, count, fresh):
        low, high = part * SHORT, (part + 1) * SHORT
        keys_at = pl.ds(first, count)
        query = query_ref[pl.ds(low, SHORT), :]
        grad = grad_ref[pl.ds(low, SHORT), :]
        key_part = value_part = query_part = None
        for half in range(2):
            keys = split_keys[half][first : first + count]
            scores = mm_rt(keys, query)
            logsum = logsum_ref[0, 0, half : half + 1, low:high]
            attention = jnp.exp2(scores * (SCORE * LOG2E) - logsum)
            moved = mm_rt(split_values[half][first : first + count], grad)
            grad_scores = (attention * (moved - inner[half][:, low:high])).astype(BF16)
            value_add = mm(attention.astype(BF16), split_grad[half][low:high])
            key_add = mm(grad_scores, split_query[half][low:high])
            query_add = mm_lt(grad_scores, keys)
            if half == 0:
                key_part, value_part, query_part = key_add, value_add, query_add
            else:
                key_part, value_part = key_part + key_add, value_part + value_add
                query_part = query_part + query_add
        grads_ref[0, pl.ds(low, SHORT), :] = (query_part * SCORE).astype(BF16)
        if fresh:
            key_sum[keys_at, :] = key_part
            value_sum[keys_at, :] = value_part
        else:
            key_sum[keys_at, :] += key_part
            value_sum[keys_at, :] += value_part

    is_long = kind_ref[pl.program_id(0)] == 1

    @pl.when(is_long)
    def _():
        for part in range(GROUP // SHORT):
            rows_of(part, 0, GROUP, part == 0)

    @pl.when(jnp.logical_not(is_long))
    def _():
        for part in range(GROUP // SHORT):
            rows_of(part, part * SHORT, SHORT, True)

    grads_ref[1, :, :] = (key_sum[...] * SCORE).astype(BF16)
    grads_ref[2, :, :] = value_sum[...].astype(BF16)


def attend_back(triple, attended, logsum, grad_attended, image_kind, first):
    groups, count = logsum.shape[:2]
    pairs = H // 2

    def part(offset):
        return pl.BlockSpec((GROUP, 2 * HD), lambda g, i, kind: (g, offset + i))

    return pl.pallas_call(
        attend_back_kernel,
        out_shape=jax.ShapeDtypeStruct((3, triple.shape[0], count * 2 * HD), BF16),
        grid_spec=pltpu.PrefetchScalarGridSpec(
            num_scalar_prefetch=1,
            grid=(groups, count),
            in_specs=[
                part(first),
                part(pairs + first),
                part(2 * pairs + first),
                part(0),
                part(first),
                pl.BlockSpec((1, 1, 8, GROUP), lambda g, i, kind: (g, i, 0, 0)),
            ],
            out_specs=pl.BlockSpec((3, GROUP, 2 * HD), lambda g, i, kind: (0, g, i)),
            scratch_shapes=[pltpu.VMEM((GROUP, 2 * HD), F32)] * 2,
        ),
        compiler_params=pltpu.CompilerParams(vmem_limit_bytes=32 << 20),
        cost_estimate=cost(80 * triple.shape[0] * GROUP * count * HD, 4 * triple.size),
        name="attend_back",
    )(image_kind, triple, triple, triple, attended, grad_attended, logsum)


def gelu_both(values):
    square = values * values
    side = tanh_gain * 0.044715 * square
    half = 0.5 + 0.5 * jnp.tanh(values * (tanh_gain + side))
    slope = half + 2.0 * values * (tanh_gain + 3.0 * side) * (half * (1.0 - half))
    return values * half, slope


def way(me, piece, strip):
    sx, other = (piece >> 1) ^ me[1], (piece & 1) ^ me[0]
    sy, k = (strip & 1) ^ me[2], (me[3] - (strip >> 1)) & 3
    return other, sx, sy, k


def on_side(other, own_ref, other_ref, action):
    @pl.when(other == 0)
    def _():
        action(own_ref)

    @pl.when(other == 1)
    def _():
        action(other_ref)


def normalize(values):
    mean = jnp.mean(values, axis=1, keepdims=True)
    centered = values - mean
    return centered * lax.rsqrt(jnp.mean(centered * centered, axis=1, keepdims=True) + eps_norm)


def triple_kernel(me, x_ref, shift_ref, scale_ref, q1a, q1b, q2a, q2b, in_ref, out_ref, weight_ref):
    rows, cols = q1a.shape[3], q1a.shape[4] - OUT_LANES

    @pl.when(pl.program_id(0) == 0)
    def _():
        for piece in range(PIECES):
            for strip in range(STRIPS):
                other, sx, sy, k = way(me, piece, strip)
                low, at = strip * 2 * rows, slice(piece * cols, (piece + 1) * cols)

                def first(ref):
                    weight_ref[low : low + rows, at] = ref[sx, sy, k, :, OUT_LANES:]

                def second(ref):
                    weight_ref[low + rows : low + 2 * rows, at] = ref[sy, sx, k, :, OUT_LANES:]

                on_side(other, q1a, q1b, first)
                on_side(other, q2a, q2b, second)

    normed = normalize(x_ref[...].astype(F32))
    attend_in = (normed * (1.0 + scale_ref[0]) + shift_ref[0]).astype(BF16)
    in_ref[...] = attend_in
    out_ref[...] = mm(attend_in, weight_ref[...]).astype(BF16)


def make_triple(me, patches, shift, scale, weights):
    tok_count, width = patches.shape
    hidden = PIECES * (weights[0].shape[4] - OUT_LANES)
    rows = pl.BlockSpec((SHORT, width), lambda i, me: (i, 0))
    each = pl.BlockSpec((1, 1, width), lambda i, me: (i, 0, 0))
    return pl.pallas_call(
        triple_kernel,
        out_shape=(
            jax.ShapeDtypeStruct((tok_count, width), BF16),
            jax.ShapeDtypeStruct((tok_count, hidden), BF16),
            jax.ShapeDtypeStruct((width, hidden), BF16),
        ),
        grid_spec=pltpu.PrefetchScalarGridSpec(
            num_scalar_prefetch=1,
            grid=(tok_count // SHORT,),
            in_specs=[rows, each, each] + [fixed(w.shape) for w in weights],
            out_specs=(
                rows,
                pl.BlockSpec((SHORT, hidden), lambda i, me: (i, 0)),
                fixed((width, hidden)),
            ),
        ),
        compiler_params=pltpu.CompilerParams(vmem_limit_bytes=40 << 20),
        cost_estimate=cost(2 * tok_count * width * hidden, 8 * tok_count * width),
        name="triple",
    )(me, patches, shift, scale, *weights)


def project_kernel(
    me,
    left_ref,
    right_ref,
    x_ref,
    gate_ref,
    shift_ref,
    scale_ref,
    q1a,
    q1b,
    q2a,
    q2b,
    projected_ref,
    residual_ref,
    branch_ref,
    logits_ref,
    weight_ref,
    router_ref,
):
    width = x_ref.shape[1]
    rows, cols, experts = q1a.shape[3], width // PIECES, E // PIECES

    @pl.when(pl.program_id(0) == 0)
    def _():
        router_ref[...] = jnp.zeros_like(router_ref)
        for piece in range(PIECES):
            for strip in range(STRIPS):
                other, sx, sy, k = way(me, piece, strip)

                def place(block, low):
                    weight_ref[low : low + rows, piece * cols : (piece + 1) * cols] = block[
                        :, :cols
                    ]
                    router_ref[
                        low : low + rows, piece * experts : (piece + 1) * experts
                    ] = block[:, cols : cols + experts]

                def first(ref):
                    place(ref[sx, sy, k], strip * 2 * rows)

                def second(ref):
                    place(ref[sy, sx, k], strip * 2 * rows + rows)

                on_side(other, q1a, q1b, first)
                on_side(other, q2a, q2b, second)

    split = left_ref.shape[1]
    projected = mm(left_ref[...], weight_ref[:split, :]) + mm(right_ref[...], weight_ref[split:, :])
    projected_ref[...] = projected
    residual = x_ref[...].astype(F32) + gate_ref[0] * projected
    residual_ref[...] = residual
    branch = (normalize(residual) * (1.0 + scale_ref[0]) + shift_ref[0]).astype(BF16)
    branch_ref[...] = branch
    logits_ref[...] = mm(branch, router_ref[...])


def make_branch(me, left, right, patches, gate, shift, scale, weights):
    tok_count, width = patches.shape
    rows = pl.BlockSpec((SHORT, width), lambda i, me: (i, 0))
    each = pl.BlockSpec((1, 1, width), lambda i, me: (i, 0, 0))
    outs = fixed(weights[0].shape[:4] + (OUT_LANES,))
    part = pl.BlockSpec((SHORT, width // 2), lambda i, me: (i, 0))
    return pl.pallas_call(
        project_kernel,
        out_shape=(
            jax.ShapeDtypeStruct((tok_count, width), F32),
            jax.ShapeDtypeStruct((tok_count, width), F32),
            jax.ShapeDtypeStruct((tok_count, width), BF16),
            jax.ShapeDtypeStruct((tok_count, LANES), F32),
            jax.ShapeDtypeStruct((width, width), BF16),
            jax.ShapeDtypeStruct((width, LANES), BF16),
        ),
        grid_spec=pltpu.PrefetchScalarGridSpec(
            num_scalar_prefetch=1,
            grid=(tok_count // SHORT,),
            in_specs=[part, part, rows, each, each, each, outs, outs, outs, outs],
            out_specs=(
                rows,
                rows,
                rows,
                pl.BlockSpec((SHORT, LANES), lambda i, me: (i, 0)),
                fixed((width, width)),
                fixed((width, LANES)),
            ),
        ),
        compiler_params=pltpu.CompilerParams(vmem_limit_bytes=32 << 20),
        cost_estimate=cost(2 * tok_count * width * width, 16 * tok_count * width),
        name="project",
    )(me, left, right, patches, gate, shift, scale, *weights)


def shared_kernel(
    me,
    x_ref,
    grad_ref,
    in_own,
    in_other,
    out_own,
    out_other,
    res_ref,
    x_grad_ref,
    weight_grad_ref,
    weight_in,
    weight_out,
    x_turned,
    grad_turned,
):
    step = pl.program_id(0)
    width = x_ref.shape[1]
    rows, half = width // STRIPS, width // 2
    halves = [slice(0, half), slice(half, width)]

    @pl.when(step == 0)
    def _():
        x_turned[...] = jnp.transpose(x_ref[...])
        grad_turned[...] = jnp.transpose(grad_ref[...])

    def take_in(ref):
        for sy in range(2):
            for z in range(4):
                low = (2 * z + (sy ^ me[2])) * rows
                weight_in[pl.ds(pl.multiple_of(low, 32), rows), :] = ref[0, sy, z]

    on_side((step & 1) ^ me[0], in_own, in_other, take_in)
    for other, ref in enumerate((out_own, out_other)):
        for sx in range(2):
            low = (((sx ^ me[1]) << 1) | (other ^ me[0])) * 2 * rows
            for sy in range(2):
                at = pl.ds(pl.multiple_of((sy ^ me[2]) * half, LANES), half)
                for part in range(2):
                    start = pl.multiple_of(low + part * rows, 32)
                    weight_out[pl.ds(start, rows), at] = ref[sy, sx, 0, :, halves[part]]

    act, slope = gelu_both(mm(x_ref[...], weight_in[...]))
    act = act.astype(BF16)
    grad_pre = (mm(grad_ref[...], weight_out[...]) * slope).astype(BF16)
    res = mm_rt(act, weight_out[...])
    x_grad = mm_rt(grad_pre, weight_in[...])

    @pl.when(step == 0)
    def _():
        res_ref[...] = res
        x_grad_ref[...] = x_grad

    @pl.when(step != 0)
    def _():
        res_ref[...] += res
        x_grad_ref[...] += x_grad

    in_grad = mm(x_turned[...], grad_pre).astype(BF16)
    out_grad = mm(grad_turned[...], act).astype(BF16)
    weight_grad_ref[step, :, :rows, :] = in_grad.reshape(STRIPS, rows, width)
    for piece in range(PIECES):
        for strip in range(2):
            for part in range(2):
                low = (2 * piece + part) * rows
                weight_grad_ref[piece, 2 * step + strip, rows:, halves[part]] = out_grad[
                    low : low + rows, halves[strip]
                ]


def shared_expert(me, x, grad, in_own, in_other, out_own, out_other):
    tok_count, width = x.shape
    rows = width // STRIPS
    whole = fixed((tok_count, width))
    block_in = pl.BlockSpec((1, 2, 4, rows, width), lambda j, me: ((j >> 1) ^ me[1], 0, 0, 0, 0))
    block_out = pl.BlockSpec((2, 2, 1, rows, width), lambda j, me: (0, 0, j, 0, 0))
    grads = jax.ShapeDtypeStruct((PIECES, STRIPS, 2 * rows, width), BF16)
    return pl.pallas_call(
        shared_kernel,
        out_shape=(jax.ShapeDtypeStruct((tok_count, width), F32),) * 2 + (grads,),
        grid_spec=pltpu.PrefetchScalarGridSpec(
            num_scalar_prefetch=1,
            grid=(PIECES,),
            in_specs=[whole, whole, block_in, block_in, block_out, block_out],
            out_specs=(whole, whole, fixed(grads.shape)),
            scratch_shapes=[pltpu.VMEM((width, width), BF16)] * 2
            + [pltpu.VMEM((width, tok_count), BF16)] * 2,
        ),
        compiler_params=pltpu.CompilerParams(vmem_limit_bytes=56 << 20),
        cost_estimate=cost(12 * tok_count * width * 4 * width, 16 * tok_count * width, 1),
        name="shared_expert",
    )(me, x, grad, in_own, in_other, out_own, out_other)


def project_back_kernel(
    left_ref,
    right_ref,
    grad_ref,
    branch_ref,
    logits_ref,
    weight_ref,
    back_ref,
    out_grad_ref,
):
    back_ref[...] = mm_rt(grad_ref[...], weight_ref[...]).astype(BF16)
    width = weight_ref.shape[0]
    outs, experts = width // PIECES, E // PIECES
    router = mm_lt(branch_ref[...], logits_ref[...]).astype(BF16)
    out_grad = jnp.concatenate(
        (mm_lt(left_ref[...], grad_ref[...]), mm_lt(right_ref[...], grad_ref[...])), axis=0
    ).astype(BF16)
    out_grad_ref[...] = jnp.zeros_like(out_grad_ref)
    for piece in range(PIECES):
        low = piece * OUT_LANES
        out_grad_ref[:, low : low + outs] = out_grad[:, piece * outs : (piece + 1) * outs]
        out_grad_ref[:, low + outs : low + outs + experts] = router[
            :, piece * experts : (piece + 1) * experts
        ]


def project_back(left, right, grad, branch, grad_logits, weight):
    tok_count, width = grad.shape
    part = fixed((tok_count, width // 2))
    whole = fixed((tok_count, width))
    return pl.pallas_call(
        project_back_kernel,
        out_shape=(
            jax.ShapeDtypeStruct((tok_count, width), BF16),
            jax.ShapeDtypeStruct((width, PIECES * OUT_LANES), BF16),
        ),
        grid=(1,),
        in_specs=[part, part, whole, whole, fixed((tok_count, LANES)), fixed((width, width))],
        out_specs=(whole, fixed((width, PIECES * OUT_LANES))),
        compiler_params=pltpu.CompilerParams(vmem_limit_bytes=32 << 20),
        cost_estimate=cost(4 * tok_count * width * width, 8 * tok_count * width),
        name="project_back",
    )(left, right, grad, branch, grad_logits, weight)


def triple_back_kernel(
    me,
    left_ref,
    right_ref,
    in_ref,
    weight_ref,
    out_grad_ref,
    back_ref,
    q1a,
    q1b,
    q2a,
    q2b,
    in_turned,
    weight_grad,
):
    step = pl.program_id(0)
    rows, cols = q1a.shape[3], q1a.shape[4] - OUT_LANES
    width = in_ref.shape[1]

    @pl.when(step == 0)
    def _():
        in_turned[...] = jnp.transpose(in_ref[...])

    grad = jnp.concatenate((left_ref[0], right_ref[0]), axis=1)
    at = pl.ds(pl.multiple_of(step * width, LANES), width)
    weight_grad[:, at] = mm(in_turned[...], grad).astype(BF16)
    back = mm_rt(grad, weight_ref[...])

    @pl.when(step == 0)
    def _():
        back_ref[...] = back

    @pl.when(step != 0)
    def _():
        back_ref[...] += back

    @pl.when(step == 2)
    def _():
        for piece in range(PIECES):
            for strip in range(STRIPS):
                other, sx, sy, k = way(me, piece, strip)

                def place(ref, where, low):
                    at = slice(low, low + rows)
                    ref[where + (slice(None), slice(0, OUT_LANES))] = out_grad_ref[
                        at, piece * OUT_LANES : (piece + 1) * OUT_LANES
                    ]
                    ref[where + (slice(None), slice(OUT_LANES, None))] = weight_grad[
                        at, piece * cols : (piece + 1) * cols
                    ]

                def first(ref):
                    place(ref, (sx, sy, k), strip * 2 * rows)

                def second(ref):
                    place(ref, (sy, sx, k), strip * 2 * rows + rows)

                on_side(other, q1a, q1b, first)
                on_side(other, q2a, q2b, second)


def triple_back(me, left, right, attend_in, weight, out_grad):
    tok_count, width = attend_in.shape
    hidden = weight.shape[1]
    block = (2, 2, 4, width // STRIPS // 2, OUT_LANES + hidden // PIECES)
    block = jax.ShapeDtypeStruct(block, BF16)
    return pl.pallas_call(
        triple_back_kernel,
        out_shape=(jax.ShapeDtypeStruct((tok_count, width), F32),) + (block,) * 4,
        grid_spec=pltpu.PrefetchScalarGridSpec(
            num_scalar_prefetch=1,
            grid=(3,),
            in_specs=[
                pl.BlockSpec((1, tok_count, width // 2), lambda p, me: (p, 0, 0)),
                pl.BlockSpec((1, tok_count, width // 2), lambda p, me: (p, 0, 0)),
                fixed((tok_count, width)),
                pl.BlockSpec((width, width), lambda p, me: (0, p)),
                fixed(out_grad.shape),
            ],
            out_specs=(fixed((tok_count, width)),) + (fixed(block.shape),) * 4,
            scratch_shapes=[
                pltpu.VMEM((width, tok_count), BF16),
                pltpu.VMEM((width, hidden), BF16),
            ],
        ),
        compiler_params=pltpu.CompilerParams(vmem_limit_bytes=40 << 20),
        cost_estimate=cost(4 * tok_count * width * hidden, 12 * tok_count * width),
        name="triple_back",
    )(me, left, right, attend_in, weight, out_grad)


ROW_TILE = 576


def expert_kernel(x_ref, weights_ref, res_ref, act_ref, slope_ref):
    x = x_ref[...]
    width = x_ref.shape[1]
    total = None
    for part in range(weights_ref.shape[0]):
        at = pl.ds(part * width, width)
        act, slope = gelu_both(mm(x, weights_ref[part, :width, :]))
        act = act.astype(BF16)
        act_ref[:, at] = act
        slope_ref[:, at] = slope.astype(BF16)
        res = mm(act, weights_ref[part, width:, :])
        total = res if total is None else total + res
    res_ref[...] = total.astype(BF16)


def expert_back_kernel(grad_ref, slope_ref, weights_ref, rows_ref, pre_ref):
    grad = grad_ref[...]
    width = grad_ref.shape[1]
    total = None
    for part in range(weights_ref.shape[0]):
        at = pl.ds(part * width, width)
        grad_pre = mm_rt(grad, weights_ref[part, width:, :]) * slope_ref[:, at].astype(F32)
        grad_pre = grad_pre.astype(BF16)
        pre_ref[:, at] = grad_pre
        rows = mm_rt(grad_pre, weights_ref[part, :width, :])
        total = rows if total is None else total + rows
    rows_ref[...] = total.astype(BF16)


def expert_call(kernel, name, rows_in, wide_in, weights, n_wide):
    rows, width = rows_in.shape
    hidden = weights.shape[0] * width
    narrow = pl.BlockSpec((ROW_TILE, width), lambda i: (i, 0))
    wide = pl.BlockSpec((ROW_TILE, hidden), lambda i: (i, 0))
    return pl.pallas_call(
        kernel,
        out_shape=(jax.ShapeDtypeStruct((rows, width), BF16),)
        + (jax.ShapeDtypeStruct((rows, hidden), BF16),) * n_wide,
        grid=(rows // ROW_TILE,),
        in_specs=[narrow] + [wide] * len(wide_in) + [fixed(weights.shape)],
        out_specs=(narrow,) + (wide,) * n_wide,
        compiler_params=pltpu.CompilerParams(vmem_limit_bytes=48 << 20),
        cost_estimate=cost(8 * rows * hidden * width, 2 * rows * hidden * (1 + n_wide)),
        name=name,
    )(rows_in, *wide_in, weights)


def expert_grads_kernel(part, x_ref, pre_ref, act_ref, grad_ref, out_ref):
    step, cols = pl.program_id(0), x_ref.shape[1]
    up = mm_lt(x_ref[...], pre_ref[...]).astype(BF16)
    down = mm_lt(act_ref[...], grad_ref[...]).astype(BF16)
    out_ref[0, step] = up[:, :cols]
    out_ref[1, step] = up[:, cols:]
    out_ref[step, 2] = down[:, :cols]
    out_ref[step, 3] = down[:, cols:]


def expert_grads(x, grad_pre, act, grad, part):
    rows, width = x.shape
    cols = width // 2
    out = jax.ShapeDtypeStruct((2, 4, cols, cols), BF16)
    return pl.pallas_call(
        expert_grads_kernel,
        out_shape=out,
        grid_spec=pltpu.PrefetchScalarGridSpec(
            num_scalar_prefetch=1,
            grid=(2,),
            in_specs=[
                pl.BlockSpec((rows, cols), lambda i, part: (0, i)),
                pl.BlockSpec((rows, width), lambda i, part: (0, part[0])),
                pl.BlockSpec((rows, cols), lambda i, part: (0, part[0] * 2 + i)),
                fixed((rows, width)),
            ],
            out_specs=fixed(out.shape),
        ),
        compiler_params=pltpu.CompilerParams(vmem_limit_bytes=40 << 20),
        cost_estimate=cost(4 * rows * width * width, 8 * rows * width),
        name="expert_grads",
    )(part, x, grad_pre, act, grad)


def up_of(half):
    return jnp.concatenate((half[0], half[1]), axis=0)


def down_of(half):
    return jnp.concatenate((half[2], half[3]), axis=1)


def by_way(blocks, y_outer, turns=True):
    rows, cols = blocks.shape[2:]
    blocks = blocks.reshape(2, 2, 4, 2, rows, cols)
    if turns:
        blocks = blocks[:, :, jnp.array([0, 3, 2, 1])]
    blocks = blocks.transpose((1, 3, 0, 2, 4, 5) if y_outer else (1, 0, 3, 2, 4, 5))
    return blocks[0], blocks[1]


def by_place(own, other, y_outer):
    blocks = jnp.stack((own, other))
    blocks = blocks.transpose((2, 0, 3, 1, 4, 5) if y_outer else (1, 0, 3, 2, 4, 5))
    rows, cols = blocks.shape[4:]
    return blocks[:, :, jnp.array([0, 3, 2, 1])].reshape(PIECES, STRIPS, rows, cols)


def to_blocks(whole):
    rows, cols = whole.shape
    return whole.reshape(STRIPS, rows // STRIPS, PIECES, cols // PIECES).transpose(2, 0, 1, 3)


def to_whole(blocks):
    rows, cols = blocks.shape[2:]
    return blocks.transpose(1, 2, 0, 3).reshape(STRIPS * rows, PIECES * cols)


def turn(block):
    block = block.T
    half = block.shape[0] // 2
    return jnp.concatenate((block[:half], block[half:]), axis=1)


def turn_back(block):
    half = block.shape[1] // 2
    return jnp.concatenate((block[:, :half], block[:, half:]), axis=0).T


def shared_bundle(up, down):
    down = to_blocks(down).swapaxes(2, 3)
    half = down.shape[2] // 2
    return jnp.concatenate(
        (to_blocks(up), jnp.concatenate((down[:, :, :half], down[:, :, half:]), axis=3)), axis=2
    )


def shared_unbundle(grads):
    rows, half = grads.shape[2] // 2, grads.shape[3] // 2
    down = grads[:, :, rows:]
    down = jnp.concatenate((down[..., :half], down[..., half:]), axis=2).swapaxes(2, 3)
    return to_whole(grads[:, :, :rows]), to_whole(down)


class Ring:
    def __init__(self, mesh):
        self.n_exp = mesh.shape["exp"]
        self.n_ring = mesh.shape["zi"]
        self.n_pair = mesh.shape["yi"]
        self.direct = (self.n_exp, self.n_ring, self.n_pair) == (PIECES, 4, 2)

    def step(self, value, by=1):
        n = self.n_ring
        return lax.ppermute(value, "zi", [(i, (i + by) % n) for i in range(n)])

    def step_aside(self, value):
        n = 2 * self.n_ring
        return lax.ppermute(value, FSDP, [(i, (i + 2) % n ^ 1) for i in range(n)])

    def over_y(self, value):
        return lax.ppermute(value, "yi", [(0, 1), (1, 0)])

    def over_x(self, value):
        return lax.ppermute(value, "exp", [(i, i ^ 2) for i in range(4)])

    def over_core(self, value):
        return lax.ppermute(value, "exp", [(i, i ^ 1) for i in range(4)])

    def near(self, block):
        return jnp.stack([block] + [self.step(block, k) for k in range(1, 4)])

    def second(self, held, y_outer):
        return jnp.stack((held, (self.over_x if y_outer else self.over_y)(held)))

    def third(self, held, y_outer):
        return jnp.stack((held, (self.over_y if y_outer else self.over_x)(held)))

    def outer(self, value, y_outer):
        return (self.over_y if y_outer else self.over_x)(value)

    def inner(self, value, y_outer):
        return (self.over_x if y_outer else self.over_y)(value)

    def line(self, held):
        return tuple(self.step(held[k], -k) for k in range(1, 4))


def add_both(keep, got):
    return add(keep[0], got[0]), add(keep[1], got[1])


def add_line(held, got):
    total = held.astype(F32)
    for part in got:
        total = total + part.astype(F32)
    return total


def add(left, right):
    return (left.astype(F32) + right.astype(F32)).astype(BF16)


def tie(*values):
    return lax.optimization_barrier(values)


def after(value, *others):
    return lax.optimization_barrier((value,) + others)[0]


def local(
    ring,
    patches,
    cond_embed,
    image_kind,
    expert_ids,
    out_grad,
    modulate_weight,
    attend_weight,
    output_weight,
    router_weight,
    shared_in,
    shared_out,
    expert_in,
    expert_out,
):
    tok_count, width = patches.shape
    blocks = tok_count // SHORT
    n_exp, n_ring, n_pair = ring.n_exp, ring.n_ring, ring.n_pair
    n_fsdp = n_ring * n_pair
    n_all = n_exp * n_fsdp
    e, z, y = (lax.axis_index(name) for name in ("exp", "zi", "yi"))
    mod_rows, mod_cols = modulate_weight.shape
    half = width // STRIPS // 2
    if ring.direct:
        me = jnp.stack((e & 1, e >> 1, y, z)).astype(jnp.int32)
    else:
        me = jnp.zeros((4,), jnp.int32)

    if ring.direct:
        spare = OUT_LANES - output_weight.shape[1] - router_weight.shape[1]
        block = jnp.concatenate(
            (
                output_weight,
                router_weight,
                jnp.zeros((router_weight.shape[0], spare), BF16),
                attend_weight,
            ),
            axis=1,
        )
        held = ring.near(block)

    cond_float = cond_embed.astype(F32)
    cond_act = jax.nn.silu(cond_float).astype(BF16)
    cond_send = cond_act.reshape(blocks, n_fsdp, mod_rows).transpose(1, 0, 2)
    cond_send = jnp.broadcast_to(cond_send[None], (n_exp, n_fsdp, blocks, mod_rows))
    cond_all = lax.all_to_all(
        cond_send.reshape(n_all, blocks, mod_rows), ALL, 0, 0, tiled=True
    ).reshape(n_all * blocks, mod_rows)
    if ring.direct:
        own_in = jnp.where(y == 0, expert_in[0], expert_in[1])
        got_in = ring.over_y(jnp.where(y == 0, expert_in[1], expert_in[0]))
        cond_all = after(cond_all, held, got_in)
    mod_part = mm(cond_all, modulate_weight).astype(BF16).reshape(n_all, blocks, mod_cols)
    mod_part = lax.all_to_all(mod_part, ALL, 0, 0, tiled=True)
    mod_part = mod_part.reshape(n_exp, n_fsdp, blocks, mod_cols)
    modulation = jnp.sum(mod_part.astype(F32), axis=1)
    if ring.direct:
        held = after(held, modulation)
    modulation = modulation.transpose(1, 0, 2).reshape(blocks, 1, 6, width)

    if ring.direct:
        own_out = jnp.where(y == 0, expert_out[0], expert_out[1])
        got_out = ring.over_y(jnp.where(y == 0, expert_out[1], expert_out[0]))
        got_out = after(got_out, modulation)
        expert_block = jnp.concatenate(
            (
                jnp.concatenate((own_in, got_in), axis=1),
                jnp.concatenate((own_out, got_out), axis=0),
            ),
            axis=0,
        )
        held = after(held, expert_block)
        held_1 = ring.second(held[:, :half], False)
        held_2 = ring.second(held[:, half:], True)
        bundle = jnp.concatenate((shared_in, turn(shared_out)), axis=0)
        shared_line = lax.all_gather(bundle, "zi", axis=0, tiled=False)
        expert_weights = lax.all_gather(after(expert_block, shared_line), "zi", axis=0)
        held_1 = ring.third(held_1, False)
        held_2 = ring.third(held_2, True)
        dense_weights = (held_1, ring.over_core(held_1), held_2, ring.over_core(held_2))
    else:
        wholes = [
            lax.all_gather(
                lax.all_gather(w, FSDP, axis=0, tiled=True), "exp", axis=1, tiled=True
            )
            for w in (attend_weight, output_weight, router_weight, shared_in, shared_out)
        ]
        attend_all, output_all, router_all = map(to_blocks, wholes[:3])
        up_all, down_all = wholes[3:]
        spare = jnp.zeros((PIECES, STRIPS, 2 * half, OUT_LANES - (width + E) // PIECES), BF16)
        dense_all = jnp.concatenate((output_all, router_all, spare, attend_all), axis=3)
        dense_weights = by_way(dense_all[:, :, :half], False)
        dense_weights += by_way(dense_all[:, :, half:], True)
        shared_all = shared_bundle(up_all, down_all)
        in_weights = by_way(shared_all[:, :, : 2 * half], False, False)
        out_weights = by_way(shared_all[:, :, 2 * half :], True, False)
        up_all = lax.all_gather(expert_in[0], FSDP, axis=1, tiled=True)
        down_all = lax.all_gather(expert_out[0], FSDP, axis=0, tiled=True)
        expert_weights = jnp.stack(
            [
                jnp.concatenate((up_all[:, at : at + width], down_all[at : at + width]), axis=0)
                for at in range(0, up_all.shape[1], width)
            ]
        )

    shift_first = modulation[:, :, 0]
    scale_first = modulation[:, :, 1]
    gate_first = modulation[:, :, 2]
    shift_second = modulation[:, :, 3]
    scale_second = modulation[:, :, 4]
    gate_second = modulation[:, :, 5]
    attend_in, triple, triple_weight = make_triple(
        me, patches, shift_first, scale_first, dense_weights
    )
    pairs = H // 4
    attended_1, logsum_1 = attend(triple, image_kind, 0, pairs)
    triple_2 = after(triple, attended_1)
    if ring.direct:
        shared_line = after(shared_line, triple)
        in_held = ring.second(shared_line[:, : 2 * half], False)
        out_held = ring.second(shared_line[:, 2 * half :], True)
        triple_2, in_held, out_held = tie(triple_2, in_held, out_held)
        in_held, out_held = ring.third(in_held, False), ring.third(out_held, True)
    attended_2, logsum_2 = attend(triple_2, image_kind, pairs, pairs)
    projected, residual, branch_in, logits, output_weight_all, router_all = make_branch(
        me,
        attended_1,
        attended_2,
        patches,
        gate_first,
        shift_second,
        scale_second,
        dense_weights,
    )
    choose = expert_ids[:, :, None] == jnp.arange(E, dtype=jnp.int32)[None, None, :]
    choose = choose.astype(F32)
    gates = jax.nn.softmax(jnp.sum(choose * logits[:, None, :E], axis=-1), axis=-1)

    grad_out = out_grad.astype(F32).reshape(blocks, SHORT, width)
    grad_branch = (gate_second * grad_out).astype(BF16).reshape(tok_count, width)
    grad_branch_wide = grad_branch.astype(F32)

    slots = slot_table(expert_ids)
    target = expert_ids * CAP + slots
    row_of = jnp.arange(E * CAP, dtype=jnp.int32)[:, None]
    pick0 = (row_of == target[None, :, 0]).astype(BF16)
    pick1 = (row_of == target[None, :, 1]).astype(BF16)
    send_rows = mm(pick0 + pick1, branch_in).astype(BF16).reshape(E, CAP, width)
    gates_sent = after(gates, send_rows)
    grad_picked = (gates_sent[:, :, None] * grad_branch_wide[:, None, :]).astype(BF16)
    grad_picked = after(grad_picked, send_rows)
    if ring.direct:
        in_held, out_held = after(in_held, send_rows), after(out_held, send_rows)
        grad_picked, in_held, out_held = tie(grad_picked, in_held, out_held)
        in_weights = (in_held, ring.over_core(in_held))
        out_weights = (out_held, ring.over_core(out_held))
    grad_send = mm(pick0, grad_picked[:, 0]) + mm(pick1, grad_picked[:, 1])
    grad_send = grad_send.astype(BF16).reshape(E, CAP, width)
    shared_x = after(branch_in, send_rows, grad_send)

    def exchange(rows):
        return lax.all_to_all(rows, ("exp", "yi"), 0, 0, tiled=True)

    received = exchange(send_rows)

    shared_res, grad_branch_in, shared_grads = shared_expert(
        me, shared_x, grad_branch, *in_weights, *out_weights
    )

    received = after(received, shared_res)
    received = received.reshape(-1, width)
    grad_received = exchange(after(grad_send, received))
    expert_res, expert_act, expert_slope = expert_call(
        expert_kernel, "experts", received, (), expert_weights, 2
    )
    grad_received = grad_received.reshape(-1, width)
    expert_res = after(expert_res, grad_received)
    returned = exchange(expert_res.reshape(E, CAP, width))
    grad_rows, grad_pre = expert_call(
        expert_back_kernel, "experts_back", grad_received, (expert_slope,), expert_weights, 1
    )
    returned = returned.reshape(-1, width)
    grad_rows = after(grad_rows, returned)
    grad_returned = exchange(grad_rows.reshape(E, CAP, width)).reshape(-1, width)

    n_parts = expert_weights.shape[0]
    first = z - 1 if ring.direct else jnp.zeros((), jnp.int32)

    def grads_of(turn_at, act):
        part = ((first - turn_at) % n_parts if ring.direct else first + turn_at).reshape(1)
        return expert_grads(received, grad_pre, act, grad_received, part)

    grad_blocks = [grads_of(0, expert_act)]
    picked0 = mm_lt(pick0, returned)
    picked1 = mm_lt(pick1, returned)
    mixture = gates[:, 0:1] * picked0 + gates[:, 1:2] * picked1
    act = after(expert_act, mixture)
    for part in range(1, n_parts):
        grad_blocks.append(grads_of(part, act))
        act = after(act, grad_blocks[-1])
    if ring.direct:
        moved = ring.step(grad_blocks[0])

    if ring.direct:
        moved = add(after(moved, *grad_blocks), grad_blocks[1])
        grad_returned, moved = tie(grad_returned, moved)
        moved = ring.step(moved)
    branch_out = (shared_res + mixture).reshape(blocks, SHORT, width)
    projected = projected.reshape(blocks, SHORT, width)
    residual = residual.reshape(blocks, SHORT, width)
    normed_second, inverse_second = layer_norm(residual)
    block_out = (residual + gate_second * branch_out).reshape(tok_count, width).astype(BF16)
    grad_gate_second = jnp.sum(grad_out * branch_out, axis=1)
    grad_gates = jnp.stack(
        (
            jnp.sum(grad_branch_wide * picked0, axis=-1),
            jnp.sum(grad_branch_wide * picked1, axis=-1),
        ),
        axis=1,
    )
    grad_chosen = gates * (grad_gates - jnp.sum(gates * grad_gates, axis=-1, keepdims=True))
    grad_logits = jnp.sum(choose * grad_chosen[:, :, None], axis=1).astype(BF16)
    grad_logits = jnp.concatenate((grad_logits, jnp.zeros((tok_count, LANES - E), BF16)), axis=1)
    grad_branch_in = (
        grad_branch_in
        + mm_lt(pick0 + pick1, grad_returned)
        + mm_rt(grad_logits, router_all)
    )
    grad_norm_in = grad_branch_in.reshape(blocks, SHORT, width)
    grad_shift_second = jnp.sum(grad_norm_in, axis=1)
    grad_scale_second = jnp.sum(grad_norm_in * normed_second, axis=1)
    grad_residual = grad_out + norm_back(
        grad_norm_in * (1.0 + scale_second), normed_second, inverse_second
    )
    grad_gate_first = jnp.sum(grad_residual * projected, axis=1)
    grad_projected = (gate_first * grad_residual).astype(BF16).reshape(tok_count, width)
    grad_attended, out_grad_all = project_back(
        attended_1, attended_2, grad_projected, branch_in, grad_logits, output_weight_all
    )
    if ring.direct:
        neighbour = ring.over_y(grad_blocks[3][1])
        grad_attended = after(grad_attended, neighbour)
    grad_triple_1 = attend_back(triple, attended_1, logsum_1, grad_attended, image_kind, 0)
    grad_attended_2 = after(grad_attended, grad_triple_1)
    if ring.direct:
        moved = add(moved, grad_blocks[2])
        grad_attended_2, own, aside = tie(grad_attended_2, moved[0], moved[1])
        own, aside = ring.step(own), ring.step_aside(aside)
    grad_triple_2 = attend_back(triple, attended_2, logsum_2, grad_attended_2, image_kind, pairs)
    grad_attend_in, *dense_grads = triple_back(
        me,
        grad_triple_1,
        grad_triple_2,
        attend_in,
        triple_weight,
        out_grad_all,
    )
    if ring.direct:
        own_1, give_1, own_2, give_2 = dense_grads
        got_1, got_2 = ring.over_core(give_1), ring.over_core(give_2)
        grad_attend_in = after(grad_attend_in, own, aside)
        sum_1, give_1 = add_both(own_1, got_1)
        sum_2, give_2 = add_both(own_2, got_2)
        got_1, got_2 = ring.outer(give_1, False), ring.outer(give_2, True)
    inputs = patches.astype(F32).reshape(blocks, SHORT, width)
    normed_first, inverse_first = layer_norm(inputs)
    grad_attend_in = grad_attend_in.reshape(blocks, SHORT, width)
    grad_shift_first = jnp.sum(grad_attend_in, axis=1)
    grad_scale_first = jnp.sum(grad_attend_in * normed_first, axis=1)
    patches_grad = grad_residual + norm_back(
        grad_attend_in * (1.0 + scale_first), normed_first, inverse_first
    )
    patches_grad = patches_grad.reshape(tok_count, width)

    grad_modulation = jnp.stack(
        (
            grad_shift_first,
            grad_scale_first,
            grad_gate_first,
            grad_shift_second,
            grad_scale_second,
            grad_gate_second,
        ),
        axis=1,
    )
    grad_modulation = grad_modulation.reshape(blocks, n_exp, mod_cols).astype(BF16)
    mod_send = jnp.broadcast_to(
        grad_modulation.transpose(1, 0, 2)[:, None], (n_exp, n_fsdp, blocks, mod_cols)
    )
    if ring.direct:
        mod_send = after(mod_send, sum_1, sum_2)
    mod_all = lax.all_to_all(
        mod_send.reshape(n_all, blocks, mod_cols), ALL, 0, 0, tiled=True
    ).reshape(n_all * blocks, mod_cols)
    modulate_grad = mm_lt(cond_all, mod_all)
    cond_part = mm_rt(mod_all, modulate_weight).reshape(n_all, blocks, mod_rows)
    if ring.direct:
        sum_1, give_1 = add_both(sum_1, got_1)
        sum_2, give_2 = add_both(sum_2, got_2)
        got_1, got_2 = ring.inner(give_1, False), ring.inner(give_2, True)
        held = jnp.concatenate((add(sum_1, got_1), add(sum_2, got_2)), axis=1)
        cond_part = after(cond_part, held)
        got_line = ring.line(held)
    cond_part = lax.all_to_all(cond_part, ALL, 0, 0, tiled=True)
    cond_grad = jnp.sum(cond_part.reshape(n_exp, n_fsdp, blocks, mod_rows), axis=0)
    cond_grad = cond_grad.transpose(1, 0, 2).reshape(blocks, width) * silu_slope(cond_float)

    if ring.direct:
        cols, experts = width // PIECES, E // PIECES
        summed = add_line(held[0], got_line)
        output_grad, router_grad = summed[:, :cols], summed[:, cols : cols + experts]
        attend_grad = summed[:, OUT_LANES:]
        summed = lax.psum_scatter(
            shared_grads.reshape((n_all,) + bundle.shape), ALL, scatter_dimension=0
        ).astype(F32)
        shared_in_grad = summed[: 2 * half]
        shared_out_grad = turn_back(summed[2 * half :])
        own = own.astype(F32) + grad_blocks[3][0].astype(F32)
        aside = aside.astype(F32) + neighbour.astype(F32)
        first, second = jnp.where(y == 0, own, aside), jnp.where(y == 0, aside, own)
        expert_in_grad = jnp.stack((up_of(first), up_of(second)))
        expert_out_grad = jnp.stack((down_of(first), down_of(second)))
    else:

        def spread(grad):
            part = lax.psum_scatter(grad, "exp", scatter_dimension=1, tiled=True)
            return lax.psum_scatter(part, FSDP, scatter_dimension=0, tiled=True).astype(F32)

        dense_all = jnp.concatenate(
            (by_place(*dense_grads[:2], False), by_place(*dense_grads[2:], True)), axis=2
        )
        cols, experts = width // PIECES, E // PIECES
        attend_grad = spread(to_whole(dense_all[..., OUT_LANES:]))
        output_grad = spread(to_whole(dense_all[..., :cols]))
        router_grad = spread(to_whole(dense_all[..., cols : cols + experts]))
        shared_in_grad, shared_out_grad = map(spread, shared_unbundle(shared_grads))
        up_sum = jnp.concatenate([up_of(half) for block in grad_blocks for half in block], axis=1)
        down_sum = jnp.concatenate(
            [down_of(half) for block in grad_blocks for half in block], axis=0
        )
        expert_in_grad = lax.psum_scatter(up_sum, FSDP, scatter_dimension=1, tiled=True)
        expert_out_grad = lax.psum_scatter(down_sum, FSDP, scatter_dimension=0, tiled=True)
        expert_in_grad = expert_in_grad.astype(F32)[None]
        expert_out_grad = expert_out_grad.astype(F32)[None]
    return (
        block_out,
        patches_grad,
        cond_grad,
        modulate_grad,
        attend_grad,
        output_grad,
        router_grad,
        shared_in_grad,
        shared_out_grad,
        expert_in_grad,
        expert_out_grad,
    )


def solution(mesh):
    n_exp, n_fsdp = mesh.shape["exp"], mesh.shape["fsdp"]
    n_pair = E // n_exp
    if n_pair not in (1, 2) or n_fsdp % n_pair:
        raise ValueError("unsupported mesh")
    fine = Mesh(mesh.devices.reshape(n_exp, n_fsdp // n_pair, n_pair), ALL)
    ring = Ring(fine)
    in_specs = (
        P(ALL, None),
        P(ALL, None),
        P(ALL),
        P(ALL, None),
        P(ALL, None),
        P(FSDP, "exp"),
        P(FSDP, "exp"),
        P(FSDP, "exp"),
        P(FSDP, "exp"),
        P(FSDP, "exp"),
        P(FSDP, "exp"),
        P("exp", None, FSDP),
        P("exp", FSDP, None),
    )
    out_specs = (
        P(ALL, None),
        P(ALL, None),
        P(ALL, None),
        P(FSDP, "exp"),
        P(FSDP, "exp"),
        P(FSDP, "exp"),
        P(FSDP, "exp"),
        P(FSDP, "exp"),
        P(FSDP, "exp"),
        P("exp", None, FSDP),
        P("exp", FSDP, None),
    )

    def step(*args):
        return local(ring, *args)

    return jax.shard_map(step, mesh=fine, in_specs=in_specs, out_specs=out_specs, check_vma=False)
```

```python
import jax
import jax.numpy as jnp
from jax import lax
from jax.experimental import pallas as pl
from jax.experimental.pallas import tpu as pltpu
from jax.sharding import Mesh
from jax.sharding import PartitionSpec as P

H = 12
HD = 64
E = 8
TOPK = 2
SHORT = 256
GROUP = 1024
CAP = 288

F32 = jnp.float32
BF16 = jnp.bfloat16

eps_norm = 1e-06
tanh_gain = 0.7978845608028654
ALL = ("exp", "zi", "yi")
FSDP = ("zi", "yi")

PIECES = 4
STRIPS = 8
LANES = 128
OUT_LANES = 2 * LANES


def layer_norm(values):
    centered = values - jnp.mean(values, axis=-1, keepdims=True)
    inverse = lax.rsqrt(jnp.mean(centered * centered, axis=-1, keepdims=True) + eps_norm)
    return (centered * inverse, inverse)


def norm_back(grad, normed, inverse):
    return inverse * (
        grad
        - jnp.mean(grad, axis=-1, keepdims=True)
        - normed * jnp.mean(grad * normed, axis=-1, keepdims=True)
    )


def silu_slope(values):
    sigma = jax.nn.sigmoid(values)
    return sigma * (1.0 + values * (1.0 - sigma))


def dot(left, right, dims):
    return lax.dot_general(left, right, (dims, ((), ())), preferred_element_type=F32)


def mm(left, right):
    return dot(left, right, ((1,), (0,)))


def mm_rt(left, right):
    return dot(left, right, ((1,), (1,)))


def mm_lt(left, right):
    return dot(left, right, ((0,), (0,)))


def slot_table(expert_ids):
    flat = expert_ids.reshape(-1)
    onehot = (flat[:, None] == jnp.arange(E, dtype=jnp.int32)[None, :]).astype(jnp.int32)
    before = jnp.cumsum(onehot, axis=0) - onehot
    return jnp.sum(before * onehot, axis=1).reshape(expert_ids.shape)


def cost(flops, moved, share=64):
    return pl.CostEstimate(flops=flops // share, transcendentals=0, bytes_accessed=moved // share)


def fixed(shape):
    return pl.BlockSpec(shape, lambda *_: (0,) * len(shape), pipeline_mode=pl.Buffered(1))


LOG2E = 1.4426950408889634
SCORE = HD ** (-0.5)


def attend_kernel(kind_ref, query_ref, key_ref, value_ref, mixed_ref, logsum_ref):
    left = lax.broadcasted_iota(jnp.int32, (GROUP, 2 * HD), 1) < HD
    keys = key_ref[...]
    zero = jnp.zeros_like(keys)
    split_keys = (jnp.where(left, keys, zero), jnp.where(left, zero, keys))

    def rows_of(part, first, count):
        rows = pl.ds(part * SHORT, SHORT)
        query = query_ref[rows, :]
        value = value_ref[pl.ds(first, count), :]
        halves = []
        for half in range(2):
            scores = mm_rt(query, split_keys[half][first : first + count])
            peak = jnp.max(scores, axis=1, keepdims=True)
            weights = jnp.exp2((scores - peak) * (SCORE * LOG2E))
            total = jnp.sum(weights, axis=1, keepdims=True)
            halves.append(mm(weights.astype(BF16), value) / total)
            logsum = peak * (SCORE * LOG2E) + jnp.log2(total)
            logsum_ref[0, 0, half, rows] = jnp.transpose(
                jnp.broadcast_to(logsum, (SHORT, 2 * HD))
            )[0]
        mixed_ref[rows, :] = jnp.where(left[:SHORT], halves[0], halves[1]).astype(BF16)

    is_long = kind_ref[pl.program_id(0)] == 1

    @pl.when(is_long)
    def _():
        for part in range(GROUP // SHORT):
            rows_of(part, 0, GROUP)

    @pl.when(jnp.logical_not(is_long))
    def _():
        for part in range(GROUP // SHORT):
            rows_of(part, part * SHORT, SHORT)


def attend(triple, image_kind, first, count):
    groups = triple.shape[0] // GROUP
    pairs = H // 2

    def part(offset):
        return pl.BlockSpec((GROUP, 2 * HD), lambda g, i, kind: (g, offset + i))

    return pl.pallas_call(
        attend_kernel,
        out_shape=(
            jax.ShapeDtypeStruct((triple.shape[0], count * 2 * HD), BF16),
            jax.ShapeDtypeStruct((groups, count, 8, GROUP), F32),
        ),
        grid_spec=pltpu.PrefetchScalarGridSpec(
            num_scalar_prefetch=1,
            grid=(groups, count),
            in_specs=[part(first), part(pairs + first), part(2 * pairs + first)],
            out_specs=(
                part(0),
                pl.BlockSpec((1, 1, 8, GROUP), lambda g, i, kind: (g, i, 0, 0)),
            ),
        ),
        compiler_params=pltpu.CompilerParams(vmem_limit_bytes=32 << 20),
        cost_estimate=cost(32 * triple.shape[0] * GROUP * count * HD, 2 * triple.size),
        name="attend",
    )(image_kind, triple, triple, triple)


def attend_back_kernel(
    kind_ref,
    query_ref,
    key_ref,
    value_ref,
    mixed_ref,
    grad_ref,
    logsum_ref,
    grads_ref,
    key_sum,
    value_sum,
):
    left = lax.broadcasted_iota(jnp.int32, (GROUP, 2 * HD), 1) < HD

    def split(values):
        zero = jnp.zeros_like(values)
        return (jnp.where(left, values, zero), jnp.where(left, zero, values))

    split_query = split(query_ref[...])
    split_keys = split(key_ref[...])
    split_values = split(value_ref[...])
    split_grad = split(grad_ref[...])
    outer = jnp.transpose(mixed_ref[...].astype(F32) * grad_ref[...].astype(F32))
    inner = (
        jnp.sum(outer[:HD], axis=0, keepdims=True),
        jnp.sum(outer[HD:], axis=0, keepdims=True),
    )

    def rows_of(part, first, count, fresh):
        low, high = part * SHORT, (part + 1) * SHORT
        keys_at = pl.ds(first, count)
        query = query_ref[pl.ds(low, SHORT), :]
        grad = grad_ref[pl.ds(low, SHORT), :]
        key_part = value_part = query_part = None
        for half in range(2):
            keys = split_keys[half][first : first + count]
            scores = mm_rt(keys, query)
            logsum = logsum_ref[0, 0, half : half + 1, low:high]
            attention = jnp.exp2(scores * (SCORE * LOG2E) - logsum)
            moved = mm_rt(split_values[half][first : first + count], grad)
            grad_scores = (attention * (moved - inner[half][:, low:high])).astype(BF16)
            value_add = mm(attention.astype(BF16), split_grad[half][low:high])
            key_add = mm(grad_scores, split_query[half][low:high])
            query_add = mm_lt(grad_scores, keys)
            if half == 0:
                key_part, value_part, query_part = key_add, value_add, query_add
            else:
                key_part, value_part = key_part + key_add, value_part + value_add
                query_part = query_part + query_add
        grads_ref[0, pl.ds(low, SHORT), :] = (query_part * SCORE).astype(BF16)
        if fresh:
            key_sum[keys_at, :] = key_part
            value_sum[keys_at, :] = value_part
        else:
            key_sum[keys_at, :] += key_part
            value_sum[keys_at, :] += value_part

    is_long = kind_ref[pl.program_id(0)] == 1

    @pl.when(is_long)
    def _():
        for part in range(GROUP // SHORT):
            rows_of(part, 0, GROUP, part == 0)

    @pl.when(jnp.logical_not(is_long))
    def _():
        for part in range(GROUP // SHORT):
            rows_of(part, part * SHORT, SHORT, True)

    grads_ref[1, :, :] = (key_sum[...] * SCORE).astype(BF16)
    grads_ref[2, :, :] = value_sum[...].astype(BF16)


def attend_back(triple, attended, logsum, grad_attended, image_kind, first):
    groups, count = logsum.shape[:2]
    pairs = H // 2

    def part(offset):
        return pl.BlockSpec((GROUP, 2 * HD), lambda g, i, kind: (g, offset + i))

    return pl.pallas_call(
        attend_back_kernel,
        out_shape=jax.ShapeDtypeStruct((3, triple.shape[0], count * 2 * HD), BF16),
        grid_spec=pltpu.PrefetchScalarGridSpec(
            num_scalar_prefetch=1,
            grid=(groups, count),
            in_specs=[
                part(first),
                part(pairs + first),
                part(2 * pairs + first),
                part(0),
                part(first),
                pl.BlockSpec((1, 1, 8, GROUP), lambda g, i, kind: (g, i, 0, 0)),
            ],
            out_specs=pl.BlockSpec((3, GROUP, 2 * HD), lambda g, i, kind: (0, g, i)),
            scratch_shapes=[pltpu.VMEM((GROUP, 2 * HD), F32)] * 2,
        ),
        compiler_params=pltpu.CompilerParams(vmem_limit_bytes=32 << 20),
        cost_estimate=cost(80 * triple.shape[0] * GROUP * count * HD, 4 * triple.size),
        name="attend_back",
    )(image_kind, triple, triple, triple, attended, grad_attended, logsum)


def gelu_both(values):
    square = values * values
    side = tanh_gain * 0.044715 * square
    half = 0.5 + 0.5 * jnp.tanh(values * (tanh_gain + side))
    slope = half + 2.0 * values * (tanh_gain + 3.0 * side) * (half * (1.0 - half))
    return values * half, slope


def way(me, piece, strip):
    sx, other = (piece >> 1) ^ me[1], (piece & 1) ^ me[0]
    sy, k = (strip & 1) ^ me[2], (me[3] - (strip >> 1)) & 3
    return other, sx, sy, k


def on_side(other, own_ref, other_ref, action):
    @pl.when(other == 0)
    def _():
        action(own_ref)

    @pl.when(other == 1)
    def _():
        action(other_ref)


def normalize(values):
    mean = jnp.mean(values, axis=1, keepdims=True)
    centered = values - mean
    return centered * lax.rsqrt(jnp.mean(centered * centered, axis=1, keepdims=True) + eps_norm)


def triple_kernel(me, x_ref, shift_ref, scale_ref, q1a, q1b, q2a, q2b, in_ref, out_ref, weight_ref):
    rows, cols = q1a.shape[3], q1a.shape[4] - OUT_LANES

    @pl.when(pl.program_id(0) == 0)
    def _():
        for piece in range(PIECES):
            for strip in range(STRIPS):
                other, sx, sy, k = way(me, piece, strip)
                low, at = strip * 2 * rows, slice(piece * cols, (piece + 1) * cols)

                def first(ref):
                    weight_ref[low : low + rows, at] = ref[sx, sy, k, :, OUT_LANES:]

                def second(ref):
                    weight_ref[low + rows : low + 2 * rows, at] = ref[sy, sx, k, :, OUT_LANES:]

                on_side(other, q1a, q1b, first)
                on_side(other, q2a, q2b, second)

    normed = normalize(x_ref[...].astype(F32))
    attend_in = (normed * (1.0 + scale_ref[0]) + shift_ref[0]).astype(BF16)
    in_ref[...] = attend_in
    out_ref[...] = mm(attend_in, weight_ref[...]).astype(BF16)


def make_triple(me, patches, shift, scale, weights):
    tok_count, width = patches.shape
    hidden = PIECES * (weights[0].shape[4] - OUT_LANES)
    rows = pl.BlockSpec((SHORT, width), lambda i, me: (i, 0))
    each = pl.BlockSpec((1, 1, width), lambda i, me: (i, 0, 0))
    return pl.pallas_call(
        triple_kernel,
        out_shape=(
            jax.ShapeDtypeStruct((tok_count, width), BF16),
            jax.ShapeDtypeStruct((tok_count, hidden), BF16),
            jax.ShapeDtypeStruct((width, hidden), BF16),
        ),
        grid_spec=pltpu.PrefetchScalarGridSpec(
            num_scalar_prefetch=1,
            grid=(tok_count // SHORT,),
            in_specs=[rows, each, each] + [fixed(w.shape) for w in weights],
            out_specs=(
                rows,
                pl.BlockSpec((SHORT, hidden), lambda i, me: (i, 0)),
                fixed((width, hidden)),
            ),
        ),
        compiler_params=pltpu.CompilerParams(vmem_limit_bytes=40 << 20),
        cost_estimate=cost(2 * tok_count * width * hidden, 8 * tok_count * width),
        name="triple",
    )(me, patches, shift, scale, *weights)


def project_kernel(
    me,
    left_ref,
    right_ref,
    x_ref,
    gate_ref,
    shift_ref,
    scale_ref,
    q1a,
    q1b,
    q2a,
    q2b,
    projected_ref,
    residual_ref,
    branch_ref,
    logits_ref,
    weight_ref,
    router_ref,
):
    width = x_ref.shape[1]
    rows, cols, experts = q1a.shape[3], width // PIECES, E // PIECES

    @pl.when(pl.program_id(0) == 0)
    def _():
        router_ref[...] = jnp.zeros_like(router_ref)
        for piece in range(PIECES):
            for strip in range(STRIPS):
                other, sx, sy, k = way(me, piece, strip)

                def place(block, low):
                    weight_ref[low : low + rows, piece * cols : (piece + 1) * cols] = block[
                        :, :cols
                    ]
                    router_ref[
                        low : low + rows, piece * experts : (piece + 1) * experts
                    ] = block[:, cols : cols + experts]

                def first(ref):
                    place(ref[sx, sy, k], strip * 2 * rows)

                def second(ref):
                    place(ref[sy, sx, k], strip * 2 * rows + rows)

                on_side(other, q1a, q1b, first)
                on_side(other, q2a, q2b, second)

    split = left_ref.shape[1]
    projected = mm(left_ref[...], weight_ref[:split, :]) + mm(right_ref[...], weight_ref[split:, :])
    projected_ref[...] = projected
    residual = x_ref[...].astype(F32) + gate_ref[0] * projected
    residual_ref[...] = residual
    branch = (normalize(residual) * (1.0 + scale_ref[0]) + shift_ref[0]).astype(BF16)
    branch_ref[...] = branch
    logits_ref[...] = mm(branch, router_ref[...])


def make_branch(me, left, right, patches, gate, shift, scale, weights):
    tok_count, width = patches.shape
    rows = pl.BlockSpec((SHORT, width), lambda i, me: (i, 0))
    each = pl.BlockSpec((1, 1, width), lambda i, me: (i, 0, 0))
    outs = fixed(weights[0].shape[:4] + (OUT_LANES,))
    part = pl.BlockSpec((SHORT, width // 2), lambda i, me: (i, 0))
    return pl.pallas_call(
        project_kernel,
        out_shape=(
            jax.ShapeDtypeStruct((tok_count, width), F32),
            jax.ShapeDtypeStruct((tok_count, width), F32),
            jax.ShapeDtypeStruct((tok_count, width), BF16),
            jax.ShapeDtypeStruct((tok_count, LANES), F32),
            jax.ShapeDtypeStruct((width, width), BF16),
            jax.ShapeDtypeStruct((width, LANES), BF16),
        ),
        grid_spec=pltpu.PrefetchScalarGridSpec(
            num_scalar_prefetch=1,
            grid=(tok_count // SHORT,),
            in_specs=[part, part, rows, each, each, each, outs, outs, outs, outs],
            out_specs=(
                rows,
                rows,
                rows,
                pl.BlockSpec((SHORT, LANES), lambda i, me: (i, 0)),
                fixed((width, width)),
                fixed((width, LANES)),
            ),
        ),
        compiler_params=pltpu.CompilerParams(vmem_limit_bytes=32 << 20),
        cost_estimate=cost(2 * tok_count * width * width, 16 * tok_count * width),
        name="project",
    )(me, left, right, patches, gate, shift, scale, *weights)


def shared_kernel(
    me,
    x_ref,
    grad_ref,
    in_own,
    in_other,
    out_own,
    out_other,
    res_ref,
    x_grad_ref,
    weight_grad_ref,
    weight_in,
    weight_out,
    x_turned,
    grad_turned,
):
    step = pl.program_id(0)
    width = x_ref.shape[1]
    rows, half = width // STRIPS, width // 2
    halves = [slice(0, half), slice(half, width)]

    @pl.when(step == 0)
    def _():
        x_turned[...] = jnp.transpose(x_ref[...])
        grad_turned[...] = jnp.transpose(grad_ref[...])

    def take_in(ref):
        for sy in range(2):
            for z in range(4):
                low = (2 * z + (sy ^ me[2])) * rows
                weight_in[pl.ds(pl.multiple_of(low, 32), rows), :] = ref[0, sy, z]

    on_side((step & 1) ^ me[0], in_own, in_other, take_in)
    for other, ref in enumerate((out_own, out_other)):
        for sx in range(2):
            low = (((sx ^ me[1]) << 1) | (other ^ me[0])) * 2 * rows
            for sy in range(2):
                at = pl.ds(pl.multiple_of((sy ^ me[2]) * half, LANES), half)
                for part in range(2):
                    start = pl.multiple_of(low + part * rows, 32)
                    weight_out[pl.ds(start, rows), at] = ref[sy, sx, 0, :, halves[part]]

    act, slope = gelu_both(mm(x_ref[...], weight_in[...]))
    act = act.astype(BF16)
    grad_pre = (mm(grad_ref[...], weight_out[...]) * slope).astype(BF16)
    res = mm_rt(act, weight_out[...])
    x_grad = mm_rt(grad_pre, weight_in[...])

    @pl.when(step == 0)
    def _():
        res_ref[...] = res
        x_grad_ref[...] = x_grad

    @pl.when(step != 0)
    def _():
        res_ref[...] += res
        x_grad_ref[...] += x_grad

    in_grad = mm(x_turned[...], grad_pre).astype(BF16)
    out_grad = mm(grad_turned[...], act).astype(BF16)
    weight_grad_ref[step, :, :rows, :] = in_grad.reshape(STRIPS, rows, width)
    for piece in range(PIECES):
        for strip in range(2):
            for part in range(2):
                low = (2 * piece + part) * rows
                weight_grad_ref[piece, 2 * step + strip, rows:, halves[part]] = out_grad[
                    low : low + rows, halves[strip]
                ]


def shared_expert(me, x, grad, in_own, in_other, out_own, out_other):
    tok_count, width = x.shape
    rows = width // STRIPS
    whole = fixed((tok_count, width))
    block_in = pl.BlockSpec((1, 2, 4, rows, width), lambda j, me: ((j >> 1) ^ me[1], 0, 0, 0, 0))
    block_out = pl.BlockSpec((2, 2, 1, rows, width), lambda j, me: (0, 0, j, 0, 0))
    grads = jax.ShapeDtypeStruct((PIECES, STRIPS, 2 * rows, width), BF16)
    return pl.pallas_call(
        shared_kernel,
        out_shape=(jax.ShapeDtypeStruct((tok_count, width), F32),) * 2 + (grads,),
        grid_spec=pltpu.PrefetchScalarGridSpec(
            num_scalar_prefetch=1,
            grid=(PIECES,),
            in_specs=[whole, whole, block_in, block_in, block_out, block_out],
            out_specs=(whole, whole, fixed(grads.shape)),
            scratch_shapes=[pltpu.VMEM((width, width), BF16)] * 2
            + [pltpu.VMEM((width, tok_count), BF16)] * 2,
        ),
        compiler_params=pltpu.CompilerParams(vmem_limit_bytes=56 << 20),
        cost_estimate=cost(12 * tok_count * width * 4 * width, 16 * tok_count * width, 1),
        name="shared_expert",
    )(me, x, grad, in_own, in_other, out_own, out_other)


def project_back_kernel(
    left_ref,
    right_ref,
    grad_ref,
    branch_ref,
    logits_ref,
    weight_ref,
    back_ref,
    out_grad_ref,
):
    back_ref[...] = mm_rt(grad_ref[...], weight_ref[...]).astype(BF16)
    width = weight_ref.shape[0]
    outs, experts = width // PIECES, E // PIECES
    router = mm_lt(branch_ref[...], logits_ref[...]).astype(BF16)
    out_grad = jnp.concatenate(
        (mm_lt(left_ref[...], grad_ref[...]), mm_lt(right_ref[...], grad_ref[...])), axis=0
    ).astype(BF16)
    out_grad_ref[...] = jnp.zeros_like(out_grad_ref)
    for piece in range(PIECES):
        low = piece * OUT_LANES
        out_grad_ref[:, low : low + outs] = out_grad[:, piece * outs : (piece + 1) * outs]
        out_grad_ref[:, low + outs : low + outs + experts] = router[
            :, piece * experts : (piece + 1) * experts
        ]


def project_back(left, right, grad, branch, grad_logits, weight):
    tok_count, width = grad.shape
    part = fixed((tok_count, width // 2))
    whole = fixed((tok_count, width))
    return pl.pallas_call(
        project_back_kernel,
        out_shape=(
            jax.ShapeDtypeStruct((tok_count, width), BF16),
            jax.ShapeDtypeStruct((width, PIECES * OUT_LANES), BF16),
        ),
        grid=(1,),
        in_specs=[part, part, whole, whole, fixed((tok_count, LANES)), fixed((width, width))],
        out_specs=(whole, fixed((width, PIECES * OUT_LANES))),
        compiler_params=pltpu.CompilerParams(vmem_limit_bytes=32 << 20),
        cost_estimate=cost(4 * tok_count * width * width, 8 * tok_count * width),
        name="project_back",
    )(left, right, grad, branch, grad_logits, weight)


def triple_back_kernel(
    me,
    left_ref,
    right_ref,
    in_ref,
    weight_ref,
    out_grad_ref,
    back_ref,
    q1a,
    q1b,
    q2a,
    q2b,
    in_turned,
    weight_grad,
):
    step = pl.program_id(0)
    rows, cols = q1a.shape[3], q1a.shape[4] - OUT_LANES
    width = in_ref.shape[1]

    @pl.when(step == 0)
    def _():
        in_turned[...] = jnp.transpose(in_ref[...])

    grad = jnp.concatenate((left_ref[0], right_ref[0]), axis=1)
    at = pl.ds(pl.multiple_of(step * width, LANES), width)
    weight_grad[:, at] = mm(in_turned[...], grad).astype(BF16)
    back = mm_rt(grad, weight_ref[...])

    @pl.when(step == 0)
    def _():
        back_ref[...] = back

    @pl.when(step != 0)
    def _():
        back_ref[...] += back

    @pl.when(step == 2)
    def _():
        for piece in range(PIECES):
            for strip in range(STRIPS):
                other, sx, sy, k = way(me, piece, strip)

                def place(ref, where, low):
                    at = slice(low, low + rows)
                    ref[where + (slice(None), slice(0, OUT_LANES))] = out_grad_ref[
                        at, piece * OUT_LANES : (piece + 1) * OUT_LANES
                    ]
                    ref[where + (slice(None), slice(OUT_LANES, None))] = weight_grad[
                        at, piece * cols : (piece + 1) * cols
                    ]

                def first(ref):
                    place(ref, (sx, sy, k), strip * 2 * rows)

                def second(ref):
                    place(ref, (sy, sx, k), strip * 2 * rows + rows)

                on_side(other, q1a, q1b, first)
                on_side(other, q2a, q2b, second)


def triple_back(me, left, right, attend_in, weight, out_grad):
    tok_count, width = attend_in.shape
    hidden = weight.shape[1]
    block = (2, 2, 4, width // STRIPS // 2, OUT_LANES + hidden // PIECES)
    block = jax.ShapeDtypeStruct(block, BF16)
    return pl.pallas_call(
        triple_back_kernel,
        out_shape=(jax.ShapeDtypeStruct((tok_count, width), F32),) + (block,) * 4,
        grid_spec=pltpu.PrefetchScalarGridSpec(
            num_scalar_prefetch=1,
            grid=(3,),
            in_specs=[
                pl.BlockSpec((1, tok_count, width // 2), lambda p, me: (p, 0, 0)),
                pl.BlockSpec((1, tok_count, width // 2), lambda p, me: (p, 0, 0)),
                fixed((tok_count, width)),
                pl.BlockSpec((width, width), lambda p, me: (0, p)),
                fixed(out_grad.shape),
            ],
            out_specs=(fixed((tok_count, width)),) + (fixed(block.shape),) * 4,
            scratch_shapes=[
                pltpu.VMEM((width, tok_count), BF16),
                pltpu.VMEM((width, hidden), BF16),
            ],
        ),
        compiler_params=pltpu.CompilerParams(vmem_limit_bytes=40 << 20),
        cost_estimate=cost(4 * tok_count * width * hidden, 12 * tok_count * width),
        name="triple_back",
    )(me, left, right, attend_in, weight, out_grad)


ROW_TILE = 576


def expert_kernel(x_ref, weights_ref, res_ref, act_ref, slope_ref):
    x = x_ref[...]
    width = x_ref.shape[1]
    total = None
    for part in range(weights_ref.shape[0]):
        at = pl.ds(part * width, width)
        act, slope = gelu_both(mm(x, weights_ref[part, :width, :]))
        act = act.astype(BF16)
        act_ref[:, at] = act
        slope_ref[:, at] = slope.astype(BF16)
        res = mm(act, weights_ref[part, width:, :])
        total = res if total is None else total + res
    res_ref[...] = total.astype(BF16)


def expert_back_kernel(grad_ref, slope_ref, weights_ref, rows_ref, pre_ref):
    grad = grad_ref[...]
    width = grad_ref.shape[1]
    total = None
    for part in range(weights_ref.shape[0]):
        at = pl.ds(part * width, width)
        grad_pre = mm_rt(grad, weights_ref[part, width:, :]) * slope_ref[:, at].astype(F32)
        grad_pre = grad_pre.astype(BF16)
        pre_ref[:, at] = grad_pre
        rows = mm_rt(grad_pre, weights_ref[part, :width, :])
        total = rows if total is None else total + rows
    rows_ref[...] = total.astype(BF16)


def expert_call(kernel, name, rows_in, wide_in, weights, n_wide):
    rows, width = rows_in.shape
    hidden = weights.shape[0] * width
    narrow = pl.BlockSpec((ROW_TILE, width), lambda i: (i, 0))
    wide = pl.BlockSpec((ROW_TILE, hidden), lambda i: (i, 0))
    return pl.pallas_call(
        kernel,
        out_shape=(jax.ShapeDtypeStruct((rows, width), BF16),)
        + (jax.ShapeDtypeStruct((rows, hidden), BF16),) * n_wide,
        grid=(rows // ROW_TILE,),
        in_specs=[narrow] + [wide] * len(wide_in) + [fixed(weights.shape)],
        out_specs=(narrow,) + (wide,) * n_wide,
        compiler_params=pltpu.CompilerParams(vmem_limit_bytes=48 << 20),
        cost_estimate=cost(8 * rows * hidden * width, 2 * rows * hidden * (1 + n_wide)),
        name=name,
    )(rows_in, *wide_in, weights)


def expert_grads_kernel(part, x_ref, pre_ref, act_ref, grad_ref, out_ref):
    step, cols = pl.program_id(0), x_ref.shape[1]
    up = mm_lt(x_ref[...], pre_ref[...]).astype(BF16)
    down = mm_lt(act_ref[...], grad_ref[...]).astype(BF16)
    out_ref[0, step] = up[:, :cols]
    out_ref[1, step] = up[:, cols:]
    out_ref[step, 2] = down[:, :cols]
    out_ref[step, 3] = down[:, cols:]


def expert_grads(x, grad_pre, act, grad, part):
    rows, width = x.shape
    cols = width // 2
    out = jax.ShapeDtypeStruct((2, 4, cols, cols), BF16)
    return pl.pallas_call(
        expert_grads_kernel,
        out_shape=out,
        grid_spec=pltpu.PrefetchScalarGridSpec(
            num_scalar_prefetch=1,
            grid=(2,),
            in_specs=[
                pl.BlockSpec((rows, cols), lambda i, part: (0, i)),
                pl.BlockSpec((rows, width), lambda i, part: (0, part[0])),
                pl.BlockSpec((rows, cols), lambda i, part: (0, part[0] * 2 + i)),
                fixed((rows, width)),
            ],
            out_specs=fixed(out.shape),
        ),
        compiler_params=pltpu.CompilerParams(vmem_limit_bytes=40 << 20),
        cost_estimate=cost(4 * rows * width * width, 8 * rows * width),
        name="expert_grads",
    )(part, x, grad_pre, act, grad)


def up_of(half):
    return jnp.concatenate((half[0], half[1]), axis=0)


def down_of(half):
    return jnp.concatenate((half[2], half[3]), axis=1)


def by_way(blocks, y_outer, turns=True):
    rows, cols = blocks.shape[2:]
    blocks = blocks.reshape(2, 2, 4, 2, rows, cols)
    if turns:
        blocks = blocks[:, :, jnp.array([0, 3, 2, 1])]
    blocks = blocks.transpose((1, 3, 0, 2, 4, 5) if y_outer else (1, 0, 3, 2, 4, 5))
    return blocks[0], blocks[1]


def by_place(own, other, y_outer):
    blocks = jnp.stack((own, other))
    blocks = blocks.transpose((2, 0, 3, 1, 4, 5) if y_outer else (1, 0, 3, 2, 4, 5))
    rows, cols = blocks.shape[4:]
    return blocks[:, :, jnp.array([0, 3, 2, 1])].reshape(PIECES, STRIPS, rows, cols)


def to_blocks(whole):
    rows, cols = whole.shape
    return whole.reshape(STRIPS, rows // STRIPS, PIECES, cols // PIECES).transpose(2, 0, 1, 3)


def to_whole(blocks):
    rows, cols = blocks.shape[2:]
    return blocks.transpose(1, 2, 0, 3).reshape(STRIPS * rows, PIECES * cols)


def turn(block):
    block = block.T
    half = block.shape[0] // 2
    return jnp.concatenate((block[:half], block[half:]), axis=1)


def turn_back(block):
    half = block.shape[1] // 2
    return jnp.concatenate((block[:, :half], block[:, half:]), axis=0).T


def shared_bundle(up, down):
    down = to_blocks(down).swapaxes(2, 3)
    half = down.shape[2] // 2
    return jnp.concatenate(
        (to_blocks(up), jnp.concatenate((down[:, :, :half], down[:, :, half:]), axis=3)), axis=2
    )


def shared_unbundle(grads):
    rows, half = grads.shape[2] // 2, grads.shape[3] // 2
    down = grads[:, :, rows:]
    down = jnp.concatenate((down[..., :half], down[..., half:]), axis=2).swapaxes(2, 3)
    return to_whole(grads[:, :, :rows]), to_whole(down)


class Ring:
    def __init__(self, mesh):
        self.n_exp = mesh.shape["exp"]
        self.n_ring = mesh.shape["zi"]
        self.n_pair = mesh.shape["yi"]
        self.direct = (self.n_exp, self.n_ring, self.n_pair) == (PIECES, 4, 2)

    def step(self, value, by=1):
        n = self.n_ring
        return lax.ppermute(value, "zi", [(i, (i + by) % n) for i in range(n)])

    def step_aside(self, value):
        n = 2 * self.n_ring
        return lax.ppermute(value, FSDP, [(i, (i + 2) % n ^ 1) for i in range(n)])

    def over_y(self, value):
        return lax.ppermute(value, "yi", [(0, 1), (1, 0)])

    def over_x(self, value):
        return lax.ppermute(value, "exp", [(i, i ^ 2) for i in range(4)])

    def over_core(self, value):
        return lax.ppermute(value, "exp", [(i, i ^ 1) for i in range(4)])

    def near(self, block):
        return jnp.stack([block] + [self.step(block, k) for k in range(1, 4)])

    def second(self, held, y_outer):
        return jnp.stack((held, (self.over_x if y_outer else self.over_y)(held)))

    def third(self, held, y_outer):
        return jnp.stack((held, (self.over_y if y_outer else self.over_x)(held)))

    def outer(self, value, y_outer):
        return (self.over_y if y_outer else self.over_x)(value)

    def inner(self, value, y_outer):
        return (self.over_x if y_outer else self.over_y)(value)

    def line(self, held):
        return tuple(self.step(held[k], -k) for k in range(1, 4))


def add_both(keep, got):
    return add(keep[0], got[0]), add(keep[1], got[1])


def add_line(held, got):
    total = held.astype(F32)
    for part in got:
        total = total + part.astype(F32)
    return total


def add(left, right):
    return (left.astype(F32) + right.astype(F32)).astype(BF16)


def tie(*values):
    return lax.optimization_barrier(values)


def after(value, *others):
    return lax.optimization_barrier((value,) + others)[0]


def local(
    ring,
    patches,
    cond_embed,
    image_kind,
    expert_ids,
    out_grad,
    modulate_weight,
    attend_weight,
    output_weight,
    router_weight,
    shared_in,
    shared_out,
    expert_in,
    expert_out,
):
    tok_count, width = patches.shape
    blocks = tok_count // SHORT
    n_exp, n_ring, n_pair = ring.n_exp, ring.n_ring, ring.n_pair
    n_fsdp = n_ring * n_pair
    n_all = n_exp * n_fsdp
    e, z, y = (lax.axis_index(name) for name in ("exp", "zi", "yi"))
    mod_rows, mod_cols = modulate_weight.shape
    half = width // STRIPS // 2
    if ring.direct:
        me = jnp.stack((e & 1, e >> 1, y, z)).astype(jnp.int32)
    else:
        me = jnp.zeros((4,), jnp.int32)

    if ring.direct:
        spare = OUT_LANES - output_weight.shape[1] - router_weight.shape[1]
        block = jnp.concatenate(
            (
                output_weight,
                router_weight,
                jnp.zeros((router_weight.shape[0], spare), BF16),
                attend_weight,
            ),
            axis=1,
        )
        held = ring.near(block)

    cond_float = cond_embed.astype(F32)
    cond_act = jax.nn.silu(cond_float).astype(BF16)
    cond_send = cond_act.reshape(blocks, n_fsdp, mod_rows).transpose(1, 0, 2)
    cond_send = jnp.broadcast_to(cond_send[None], (n_exp, n_fsdp, blocks, mod_rows))
    cond_all = lax.all_to_all(
        cond_send.reshape(n_all, blocks, mod_rows), ALL, 0, 0, tiled=True
    ).reshape(n_all * blocks, mod_rows)
    if ring.direct:
        own_in = jnp.where(y == 0, expert_in[0], expert_in[1])
        got_in = ring.over_y(jnp.where(y == 0, expert_in[1], expert_in[0]))
        cond_all = after(cond_all, held, got_in)
    mod_part = mm(cond_all, modulate_weight).astype(BF16).reshape(n_all, blocks, mod_cols)
    mod_part = lax.all_to_all(mod_part, ALL, 0, 0, tiled=True)
    mod_part = mod_part.reshape(n_exp, n_fsdp, blocks, mod_cols)
    modulation = jnp.sum(mod_part.astype(F32), axis=1)
    if ring.direct:
        held = after(held, modulation)
    modulation = modulation.transpose(1, 0, 2).reshape(blocks, 1, 6, width)

    if ring.direct:
        own_out = jnp.where(y == 0, expert_out[0], expert_out[1])
        got_out = ring.over_y(jnp.where(y == 0, expert_out[1], expert_out[0]))
        got_out = after(got_out, modulation)
        expert_block = jnp.concatenate(
            (
                jnp.concatenate((own_in, got_in), axis=1),
                jnp.concatenate((own_out, got_out), axis=0),
            ),
            axis=0,
        )
        held = after(held, expert_block)
        held_1 = ring.second(held[:, :half], False)
        held_2 = ring.second(held[:, half:], True)
        bundle = jnp.concatenate((shared_in, turn(shared_out)), axis=0)
        shared_line = lax.all_gather(bundle, "zi", axis=0, tiled=False)
        expert_weights = lax.all_gather(after(expert_block, shared_line), "zi", axis=0)
        held_1 = ring.third(held_1, False)
        held_2 = ring.third(held_2, True)
        dense_weights = (held_1, ring.over_core(held_1), held_2, ring.over_core(held_2))
    else:
        wholes = [
            lax.all_gather(
                lax.all_gather(w, FSDP, axis=0, tiled=True), "exp", axis=1, tiled=True
            )
            for w in (attend_weight, output_weight, router_weight, shared_in, shared_out)
        ]
        attend_all, output_all, router_all = map(to_blocks, wholes[:3])
        up_all, down_all = wholes[3:]
        spare = jnp.zeros((PIECES, STRIPS, 2 * half, OUT_LANES - (width + E) // PIECES), BF16)
        dense_all = jnp.concatenate((output_all, router_all, spare, attend_all), axis=3)
        dense_weights = by_way(dense_all[:, :, :half], False)
        dense_weights += by_way(dense_all[:, :, half:], True)
        shared_all = shared_bundle(up_all, down_all)
        in_weights = by_way(shared_all[:, :, : 2 * half], False, False)
        out_weights = by_way(shared_all[:, :, 2 * half :], True, False)
        up_all = lax.all_gather(expert_in[0], FSDP, axis=1, tiled=True)
        down_all = lax.all_gather(expert_out[0], FSDP, axis=0, tiled=True)
        expert_weights = jnp.stack(
            [
                jnp.concatenate((up_all[:, at : at + width], down_all[at : at + width]), axis=0)
                for at in range(0, up_all.shape[1], width)
            ]
        )

    shift_first = modulation[:, :, 0]
    scale_first = modulation[:, :, 1]
    gate_first = modulation[:, :, 2]
    shift_second = modulation[:, :, 3]
    scale_second = modulation[:, :, 4]
    gate_second = modulation[:, :, 5]
    attend_in, triple, triple_weight = make_triple(
        me, patches, shift_first, scale_first, dense_weights
    )
    pairs = H // 4
    attended_1, logsum_1 = attend(triple, image_kind, 0, pairs)
    triple_2 = after(triple, attended_1)
    if ring.direct:
        shared_line = after(shared_line, triple)
        in_held = ring.second(shared_line[:, : 2 * half], False)
        out_held = ring.second(shared_line[:, 2 * half :], True)
        triple_2, in_held, out_held = tie(triple_2, in_held, out_held)
        in_held, out_held = ring.third(in_held, False), ring.third(out_held, True)
    attended_2, logsum_2 = attend(triple_2, image_kind, pairs, pairs)
    projected, residual, branch_in, logits, output_weight_all, router_all = make_branch(
        me,
        attended_1,
        attended_2,
        patches,
        gate_first,
        shift_second,
        scale_second,
        dense_weights,
    )
    choose = expert_ids[:, :, None] == jnp.arange(E, dtype=jnp.int32)[None, None, :]
    choose = choose.astype(F32)
    gates = jax.nn.softmax(jnp.sum(choose * logits[:, None, :E], axis=-1), axis=-1)

    grad_out = out_grad.astype(F32).reshape(blocks, SHORT, width)
    grad_branch = (gate_second * grad_out).astype(BF16).reshape(tok_count, width)
    grad_branch_wide = grad_branch.astype(F32)

    slots = slot_table(expert_ids)
    target = expert_ids * CAP + slots
    row_of = jnp.arange(E * CAP, dtype=jnp.int32)[:, None]
    pick0 = (row_of == target[None, :, 0]).astype(BF16)
    pick1 = (row_of == target[None, :, 1]).astype(BF16)
    send_rows = mm(pick0 + pick1, branch_in).astype(BF16).reshape(E, CAP, width)
    gates_sent = after(gates, send_rows)
    grad_picked = (gates_sent[:, :, None] * grad_branch_wide[:, None, :]).astype(BF16)
    grad_picked = after(grad_picked, send_rows)
    if ring.direct:
        in_held, out_held = after(in_held, send_rows), after(out_held, send_rows)
        grad_picked, in_held, out_held = tie(grad_picked, in_held, out_held)
        in_weights = (in_held, ring.over_core(in_held))
        out_weights = (out_held, ring.over_core(out_held))
    grad_send = mm(pick0, grad_picked[:, 0]) + mm(pick1, grad_picked[:, 1])
    grad_send = grad_send.astype(BF16).reshape(E, CAP, width)
    shared_x = after(branch_in, send_rows, grad_send)

    def exchange(rows):
        return lax.all_to_all(rows, ("exp", "yi"), 0, 0, tiled=True)

    received = exchange(send_rows)

    shared_res, grad_branch_in, shared_grads = shared_expert(
        me, shared_x, grad_branch, *in_weights, *out_weights
    )

    received = after(received, shared_res)
    received = received.reshape(-1, width)
    grad_received = exchange(after(grad_send, received))
    expert_res, expert_act, expert_slope = expert_call(
        expert_kernel, "experts", received, (), expert_weights, 2
    )
    grad_received = grad_received.reshape(-1, width)
    expert_res = after(expert_res, grad_received)
    returned = exchange(expert_res.reshape(E, CAP, width))
    grad_rows, grad_pre = expert_call(
        expert_back_kernel, "experts_back", grad_received, (expert_slope,), expert_weights, 1
    )
    returned = returned.reshape(-1, width)
    grad_rows = after(grad_rows, returned)
    grad_returned = exchange(grad_rows.reshape(E, CAP, width)).reshape(-1, width)

    n_parts = expert_weights.shape[0]
    first = z - 1 if ring.direct else jnp.zeros((), jnp.int32)

    def grads_of(turn_at, act):
        part = ((first - turn_at) % n_parts if ring.direct else first + turn_at).reshape(1)
        return expert_grads(received, grad_pre, act, grad_received, part)

    grad_blocks = [grads_of(0, expert_act)]
    picked0 = mm_lt(pick0, returned)
    picked1 = mm_lt(pick1, returned)
    mixture = gates[:, 0:1] * picked0 + gates[:, 1:2] * picked1
    act = after(expert_act, mixture)
    for part in range(1, n_parts):
        grad_blocks.append(grads_of(part, act))
        act = after(act, grad_blocks[-1])
    if ring.direct:
        moved = ring.step(grad_blocks[0])

    if ring.direct:
        moved = add(after(moved, *grad_blocks), grad_blocks[1])
        grad_returned, moved = tie(grad_returned, moved)
        moved = ring.step(moved)
    branch_out = (shared_res + mixture).reshape(blocks, SHORT, width)
    projected = projected.reshape(blocks, SHORT, width)
    residual = residual.reshape(blocks, SHORT, width)
    normed_second, inverse_second = layer_norm(residual)
    block_out = (residual + gate_second * branch_out).reshape(tok_count, width).astype(BF16)
    grad_gate_second = jnp.sum(grad_out * branch_out, axis=1)
    grad_gates = jnp.stack(
        (
            jnp.sum(grad_branch_wide * picked0, axis=-1),
            jnp.sum(grad_branch_wide * picked1, axis=-1),
        ),
        axis=1,
    )
    grad_chosen = gates * (grad_gates - jnp.sum(gates * grad_gates, axis=-1, keepdims=True))
    grad_logits = jnp.sum(choose * grad_chosen[:, :, None], axis=1).astype(BF16)
    grad_logits = jnp.concatenate((grad_logits, jnp.zeros((tok_count, LANES - E), BF16)), axis=1)
    grad_branch_in = (
        grad_branch_in
        + mm_lt(pick0 + pick1, grad_returned)
        + mm_rt(grad_logits, router_all)
    )
    grad_norm_in = grad_branch_in.reshape(blocks, SHORT, width)
    grad_shift_second = jnp.sum(grad_norm_in, axis=1)
    grad_scale_second = jnp.sum(grad_norm_in * normed_second, axis=1)
    grad_residual = grad_out + norm_back(
        grad_norm_in * (1.0 + scale_second), normed_second, inverse_second
    )
    grad_gate_first = jnp.sum(grad_residual * projected, axis=1)
    grad_projected = (gate_first * grad_residual).astype(BF16).reshape(tok_count, width)
    grad_attended, out_grad_all = project_back(
        attended_1, attended_2, grad_projected, branch_in, grad_logits, output_weight_all
    )
    if ring.direct:
        neighbour = ring.over_y(grad_blocks[3][1])
        grad_attended = after(grad_attended, neighbour)
    grad_triple_1 = attend_back(triple, attended_1, logsum_1, grad_attended, image_kind, 0)
    grad_attended_2 = after(grad_attended, grad_triple_1)
    if ring.direct:
        moved = add(moved, grad_blocks[2])
        grad_attended_2, own, aside = tie(grad_attended_2, moved[0], moved[1])
        own, aside = ring.step(own), ring.step_aside(aside)
    grad_triple_2 = attend_back(triple, attended_2, logsum_2, grad_attended_2, image_kind, pairs)
    grad_attend_in, *dense_grads = triple_back(
        me,
        grad_triple_1,
        grad_triple_2,
        attend_in,
        triple_weight,
        out_grad_all,
    )
    if ring.direct:
        own_1, give_1, own_2, give_2 = dense_grads
        got_1, got_2 = ring.over_core(give_1), ring.over_core(give_2)
        grad_attend_in = after(grad_attend_in, own, aside, got_1, got_2)
        sum_1, give_1 = add_both(own_1, got_1)
        sum_2, give_2 = add_both(own_2, got_2)
        got_1, got_2 = ring.outer(give_1, False), ring.outer(give_2, True)
    inputs = patches.astype(F32).reshape(blocks, SHORT, width)
    normed_first, inverse_first = layer_norm(inputs)
    grad_attend_in = grad_attend_in.reshape(blocks, SHORT, width)
    grad_shift_first = jnp.sum(grad_attend_in, axis=1)
    grad_scale_first = jnp.sum(grad_attend_in * normed_first, axis=1)
    patches_grad = grad_residual + norm_back(
        grad_attend_in * (1.0 + scale_first), normed_first, inverse_first
    )
    patches_grad = patches_grad.reshape(tok_count, width)

    grad_modulation = jnp.stack(
        (
            grad_shift_first,
            grad_scale_first,
            grad_gate_first,
            grad_shift_second,
            grad_scale_second,
            grad_gate_second,
        ),
        axis=1,
    )
    grad_modulation = grad_modulation.reshape(blocks, n_exp, mod_cols).astype(BF16)
    mod_send = jnp.broadcast_to(
        grad_modulation.transpose(1, 0, 2)[:, None], (n_exp, n_fsdp, blocks, mod_cols)
    )
    if ring.direct:
        mod_send = after(mod_send, sum_1, sum_2)
    mod_all = lax.all_to_all(
        mod_send.reshape(n_all, blocks, mod_cols), ALL, 0, 0, tiled=True
    ).reshape(n_all * blocks, mod_cols)
    modulate_grad = mm_lt(cond_all, mod_all)
    cond_part = mm_rt(mod_all, modulate_weight).reshape(n_all, blocks, mod_rows)
    if ring.direct:
        sum_1, give_1 = add_both(sum_1, got_1)
        sum_2, give_2 = add_both(sum_2, got_2)
        got_1, got_2 = ring.inner(give_1, False), ring.inner(give_2, True)
        held = jnp.concatenate((add(sum_1, got_1), add(sum_2, got_2)), axis=1)
        cond_part = after(cond_part, held)
        got_line = ring.line(held)
    cond_part = lax.all_to_all(cond_part, ALL, 0, 0, tiled=True)
    cond_grad = jnp.sum(cond_part.reshape(n_exp, n_fsdp, blocks, mod_rows), axis=0)
    cond_grad = cond_grad.transpose(1, 0, 2).reshape(blocks, width) * silu_slope(cond_float)

    if ring.direct:
        cols, experts = width // PIECES, E // PIECES
        summed = add_line(held[0], got_line)
        output_grad, router_grad = summed[:, :cols], summed[:, cols : cols + experts]
        attend_grad = summed[:, OUT_LANES:]
        summed = lax.psum_scatter(
            shared_grads.reshape((n_all,) + bundle.shape), ALL, scatter_dimension=0
        ).astype(F32)
        shared_in_grad = summed[: 2 * half]
        shared_out_grad = turn_back(summed[2 * half :])
        own = own.astype(F32) + grad_blocks[3][0].astype(F32)
        aside = aside.astype(F32) + neighbour.astype(F32)
        first, second = jnp.where(y == 0, own, aside), jnp.where(y == 0, aside, own)
        expert_in_grad = jnp.stack((up_of(first), up_of(second)))
        expert_out_grad = jnp.stack((down_of(first), down_of(second)))
    else:

        def spread(grad):
            part = lax.psum_scatter(grad, "exp", scatter_dimension=1, tiled=True)
            return lax.psum_scatter(part, FSDP, scatter_dimension=0, tiled=True).astype(F32)

        dense_all = jnp.concatenate(
            (by_place(*dense_grads[:2], False), by_place(*dense_grads[2:], True)), axis=2
        )
        cols, experts = width // PIECES, E // PIECES
        attend_grad = spread(to_whole(dense_all[..., OUT_LANES:]))
        output_grad = spread(to_whole(dense_all[..., :cols]))
        router_grad = spread(to_whole(dense_all[..., cols : cols + experts]))
        shared_in_grad, shared_out_grad = map(spread, shared_unbundle(shared_grads))
        up_sum = jnp.concatenate([up_of(half) for block in grad_blocks for half in block], axis=1)
        down_sum = jnp.concatenate(
            [down_of(half) for block in grad_blocks for half in block], axis=0
        )
        expert_in_grad = lax.psum_scatter(up_sum, FSDP, scatter_dimension=1, tiled=True)
        expert_out_grad = lax.psum_scatter(down_sum, FSDP, scatter_dimension=0, tiled=True)
        expert_in_grad = expert_in_grad.astype(F32)[None]
        expert_out_grad = expert_out_grad.astype(F32)[None]
    return (
        block_out,
        patches_grad,
        cond_grad,
        modulate_grad,
        attend_grad,
        output_grad,
        router_grad,
        shared_in_grad,
        shared_out_grad,
        expert_in_grad,
        expert_out_grad,
    )


def solution(mesh):
    n_exp, n_fsdp = mesh.shape["exp"], mesh.shape["fsdp"]
    n_pair = E // n_exp
    if n_pair not in (1, 2) or n_fsdp % n_pair:
        raise ValueError("unsupported mesh")
    fine = Mesh(mesh.devices.reshape(n_exp, n_fsdp // n_pair, n_pair), ALL)
    ring = Ring(fine)
    in_specs = (
        P(ALL, None),
        P(ALL, None),
        P(ALL),
        P(ALL, None),
        P(ALL, None),
        P(FSDP, "exp"),
        P(FSDP, "exp"),
        P(FSDP, "exp"),
        P(FSDP, "exp"),
        P(FSDP, "exp"),
        P(FSDP, "exp"),
        P("exp", None, FSDP),
        P("exp", FSDP, None),
    )
    out_specs = (
        P(ALL, None),
        P(ALL, None),
        P(ALL, None),
        P(FSDP, "exp"),
        P(FSDP, "exp"),
        P(FSDP, "exp"),
        P(FSDP, "exp"),
        P(FSDP, "exp"),
        P(FSDP, "exp"),
        P("exp", None, FSDP),
        P("exp", FSDP, None),
    )

    def step(*args):
        return local(ring, *args)

    return jax.shard_map(step, mesh=fine, in_specs=in_specs, out_specs=out_specs, check_vma=False)
```
